32 devices in a mesh: seq: 8 (over z, x), head: 4 (over y, core).
Axes of the slice: x: 2, y: 2, z: 4, core: 2. Of those that a mesh axis runs over, the one named last changes fastest.
Arguments:
- tokens_in: bfloat16 [256, 32, 6144], P('seq', None, 'head'), may hold values from -6 to 6
- gate_rows: bfloat16 [256, 32, 6144], P('seq', None, 'head'), may hold values from -28 to 28
- gate_cols: bfloat16 [256, 32, 6144], P(None, 'seq', 'head'), may hold values from -28 to 28
- write_rows: bfloat16 [64, 8192], P(None, 'seq'), may hold values from -6 to 6
- read_rows: bfloat16 [64, 8192], P(None, 'seq'), may hold values from -0.75 to 0.75
- step_rows: float32 [48, 8192], P('head', 'seq'), may hold values from 0 to 2, as said below
- decay_rows: float32 [48, 8192], P('head', 'seq'), may hold values from -1 to 0, as said below
- skip_rows: float32 [48], P('head'), may hold values from 0.5 to 2
- norm_rows: float32 [6144], P('head'), may hold values from 0.5 to 1.5
- write_cols: bfloat16 [64, 8192], P(None, 'seq'), may hold values from -6 to 6
- read_cols: bfloat16 [64, 8192], P(None, 'seq'), may hold values from -0.75 to 0.75
- step_cols: float32 [48, 8192], P('head', 'seq'), may hold values from 0 to 2, as said below
- decay_cols: float32 [48, 8192], P('head', 'seq'), may hold values from -1 to 0, as said below
- skip_cols: float32 [48], P('head'), may hold values from 0.5 to 2
- norm_cols: float32 [6144], P('head'), may hold values from 0.5 to 1.5
Outputs:
- mixed_cols: bfloat16 [256, 32, 6144], P(None, 'seq', 'head')
The draws below stay inside these ranges and needn't reach their ends.
Inputs may be any that keep to these rules, and one draw needn't show every extreme that they name: `step_rows`: positive. `step_cols`: positive. `decay_rows`: never positive. `decay_cols`: never positive.
All inputs are finite; a program needn't handle non-finite values.
Results may differ from the reference program's by a relative error of at most 0.0063.
Values may be sent and summed in bfloat16 or wider, within the bound.
A program may use at most 128 MiB of HBM per device.

```python
import math
import jax
import jax.numpy as jnp
from jax import lax

HEADS = 48
HEADDIM = 128
NSTATE = 64
BLOCK = 256
GRID_W = 32
ROWS = 256
LENGTH = 8192
INNER = 6144


def head_laws(key, salt):
    folded = jax.random.fold_in(key, salt)
    keys = jax.random.split(folded, 7)
    share = 0.5
    slow_heads = jax.random.uniform(keys[0], (HEADS,)) < share
    slow_rate = jax.random.uniform(keys[1], (HEADS,), minval=0.05, maxval=0.5) / LENGTH
    fast_rate = jax.random.uniform(keys[2], (HEADS,), minval=1.0 / 50.0, maxval=1.0 / 30.0)
    each_head_values = jnp.where(slow_heads, slow_rate, fast_rate)
    coarse_estimate = jax.random.uniform(keys[3], (HEADS, LENGTH), minval=0.5, maxval=1.5)
    spread = jax.random.uniform(keys[6], (HEADS, LENGTH), minval=0.5, maxval=1.5)
    grid_points = jax.random.randint(keys[4], (2,), 0, LENGTH)
    retained_values = jax.random.uniform(keys[5], (2,), minval=0.5, maxval=0.8)
    token_locations = jnp.arange(LENGTH, dtype=jnp.int32)
    sudden_jump = jnp.sum(jnp.where(token_locations[None, :] == grid_points[:, None], jnp.log(retained_values)[:, None], 0.0), axis=0)
    decay_factors = -each_head_values[:, None] * coarse_estimate + sudden_jump[None, :]
    scales = jnp.where(slow_heads, jnp.sqrt(40.0 / LENGTH), 1.0)
    steps = scales[:, None] * spread
    return (steps.astype(jnp.float32), decay_factors.astype(jnp.float32))


def gate_draw(key, salt):
    folded = jax.random.fold_in(key, salt)
    head_index = jnp.arange(INNER, dtype=jnp.int32) // HEADDIM
    fraction = head_index.astype(jnp.float32) / (HEADS - 1)
    scales = 4.0 ** fraction
    values = jnp.clip(jax.random.normal(folded, (ROWS, GRID_W, INNER)), -3.0, 3.0)
    return (values * scales).astype(jnp.bfloat16)


def draw_gate_rows(key, part):
    return gate_draw(key, 31)


def draw_gate_cols(key, part):
    return gate_draw(key, 37)


def draw_step_rows(key, part):
    return head_laws(key, 11)[0]


def draw_decay_rows(key, part):
    return head_laws(key, 11)[1]


def draw_step_cols(key, part):
    return head_laws(key, 23)[0]


def draw_decay_cols(key, part):
    return head_laws(key, 23)[1]


def steps_of(own_key, dims, cuts, smallest, high):
    gain = 1.0
    for axis_at, blocks in cuts:
        draws = jax.random.uniform(jax.random.fold_in(jax.random.fold_in(own_key, 6), axis_at), (blocks,), jnp.float32, smallest / len(cuts), high / len(cuts))
        gain = gain * jnp.repeat(jnp.exp(draws), dims[axis_at] // blocks).reshape((-1,) + (1,) * (len(dims) - 1 - axis_at))
    return gain


def centred(rng, extent, scale, limit, cuts=(), kind=jnp.bfloat16):
    array = jax.random.normal(rng, extent, jnp.float32) * scale
    if len(cuts) > 0:
        array = steps_of(rng, extent, cuts, -0.22, 0.18) * array
    return jnp.clip(array, min=-limit, max=limit).astype(kind)


def setup_inputs(seed: int = 0) -> dict:
    arg_keys = jax.random.split(jax.random.key(seed), 16)
    tokens_in = centred(arg_keys[0], (ROWS, GRID_W, INNER), 1.0, 6.0, ((0, 8), (2, 4)))
    gate_rows = draw_gate_rows(jax.random.fold_in(arg_keys[15], 71), 0)
    gate_cols = draw_gate_cols(jax.random.fold_in(arg_keys[15], 71), 0)
    write_rows = centred(arg_keys[3], (NSTATE, LENGTH), 1.0, 6.0, ((1, 8),))
    read_rows = centred(arg_keys[4], (NSTATE, LENGTH), NSTATE ** -0.5, 0.75, ((1, 8),))
    step_rows = draw_step_rows(jax.random.fold_in(arg_keys[15], 71), 0)
    decay_rows = draw_decay_rows(jax.random.fold_in(arg_keys[15], 71), 0)
    skip_rows = jnp.clip(jnp.exp(math.log(2.0) - 1.3862944 * jax.random.uniform(arg_keys[7], (HEADS,), jnp.float32) ** steps_of(arg_keys[7], (HEADS,), ((0, 4),), -0.2, 0.2)), 0.5, 2.0)
    norm_rows = jnp.clip(1.0 + 0.1 * jax.random.normal(arg_keys[8], (INNER,), jnp.float32), 0.5, 1.5)
    write_cols = centred(arg_keys[9], (NSTATE, LENGTH), 1.0, 6.0, ((1, 8),))
    read_cols = centred(arg_keys[10], (NSTATE, LENGTH), NSTATE ** -0.5, 0.75, ((1, 8),))
    step_cols = draw_step_cols(jax.random.fold_in(arg_keys[15], 71), 0)
    decay_cols = draw_decay_cols(jax.random.fold_in(arg_keys[15], 71), 0)
    skip_cols = jnp.clip(jnp.exp(math.log(2.0) - 1.3862944 * jax.random.uniform(arg_keys[13], (HEADS,), jnp.float32) ** steps_of(arg_keys[13], (HEADS,), ((0, 4),), -0.2, 0.2)), 0.5, 2.0)
    norm_cols = jnp.clip(1.0 + 0.1 * jax.random.normal(arg_keys[14], (INNER,), jnp.float32), 0.5, 1.5)
    return dict(tokens_in=tokens_in, gate_rows=gate_rows, gate_cols=gate_cols, write_rows=write_rows, read_rows=read_rows, step_rows=step_rows, decay_rows=decay_rows, skip_rows=skip_rows, norm_rows=norm_rows, write_cols=write_cols, read_cols=read_cols, step_cols=step_cols, decay_cols=decay_cols, skip_cols=skip_cols, norm_cols=norm_cols)


EPSILON = 1e-05
HIGHEST = lax.Precision.HIGHEST

def block_step(state_in, inputs, gate_blk, write_blk, read_blk, step_blk, decay_blk, skip_vec, gain_vec):
    length = inputs.shape[0]
    causal = lax.broadcasted_iota(jnp.int32, (length, length), 0) >= lax.broadcasted_iota(jnp.int32, (length, length), 1)
    cumulative = jnp.cumsum(decay_blk, axis=1)
    scores = jnp.dot(read_blk.T, write_blk, preferred_element_type=jnp.float32)
    spread = cumulative[:, :, None] - cumulative[:, None, :]
    fading = jnp.where(causal, jnp.exp(jnp.where(causal, spread, 0.0)), 0.0)
    mixing = (fading * scores[None] * step_blk[:, None, :]).astype(jnp.bfloat16)
    wide_in = inputs.astype(jnp.float32)
    inner_part = jnp.einsum('hts,shp->thp', mixing.astype(jnp.float32), wide_in)
    tail_weights = jnp.exp(cumulative[:, -1:] - cumulative) * step_blk
    loaded = (write_blk.astype(jnp.float32)[None] * tail_weights[:, None, :]).astype(jnp.bfloat16)
    gained = jnp.einsum('hns,shp->hnp', loaded.astype(jnp.float32), wide_in)
    from_state = jnp.einsum('nt,hnp->thp', read_blk.astype(jnp.float32), state_in, precision=HIGHEST)
    outputs = inner_part + from_state * jnp.exp(cumulative).T[:, :, None] + skip_vec[:, None] * wide_in
    gated = outputs.reshape(length, -1) * jax.nn.silu(gate_blk.astype(jnp.float32))
    scaled = lax.rsqrt(lax.optimization_barrier(jnp.mean(gated * gated, axis=-1)) + EPSILON)
    result = (gated * scaled[:, None] * gain_vec).astype(jnp.bfloat16)
    new_state = jnp.exp(cumulative[:, -1])[:, None, None] * state_in + gained
    return (new_state, result)

def run_layer(fetch, block_total, write_mat, read_mat, step_mat, decay_mat, skip_vec, gain_vec):
    head_count = step_mat.shape[0]
    state_size = write_mat.shape[0]
    head_width = gain_vec.shape[0] // head_count

    def window_of(matrix, offset):
        return lax.dynamic_slice_in_dim(matrix, offset, BLOCK, 1)

    def advance(state_in, block_index):
        inputs, gate_blk = fetch(block_index)
        offset = (block_index * BLOCK).astype(jnp.int32)
        return block_step(state_in, inputs, gate_blk, window_of(write_mat, offset), window_of(read_mat, offset), window_of(step_mat, offset), window_of(decay_mat, offset), skip_vec, gain_vec)
    initial = jnp.zeros((head_count, state_size, head_width), jnp.float32)
    return lax.scan(advance, initial, jnp.arange(block_total, dtype=jnp.int32))[1]

def reference(tokens_in, gate_rows, gate_cols, write_rows, read_rows, step_rows, decay_rows, skip_rows, norm_rows, write_cols, read_cols, step_cols, decay_cols, skip_cols, norm_cols):
    flat_tokens = tokens_in.reshape(LENGTH, INNER)
    flat_gate = gate_rows.reshape(LENGTH, INNER)

    def fetch_rows(block_index):
        offset = (block_index * BLOCK).astype(jnp.int32)
        token_block = lax.dynamic_slice_in_dim(flat_tokens, offset, BLOCK, 0).reshape(BLOCK, HEADS, HEADDIM)
        return (token_block, lax.dynamic_slice_in_dim(flat_gate, offset, BLOCK, 0))
    first = run_layer(fetch_rows, LENGTH // BLOCK, write_rows, read_rows, step_rows, decay_rows, skip_rows, norm_rows)
    hidden = first.reshape(ROWS, GRID_W, INNER)
    per_col = ROWS // BLOCK

    def fetch_cols(block_index):
        column = (block_index // per_col).astype(jnp.int32)
        row_start = (block_index % per_col * BLOCK).astype(jnp.int32)
        zero_index = jnp.zeros((), jnp.int32)
        token_block = lax.dynamic_slice(hidden, (row_start, column, zero_index), (BLOCK, 1, INNER)).reshape(BLOCK, HEADS, HEADDIM)
        gate_block = lax.dynamic_slice(gate_cols, (row_start, column, zero_index), (BLOCK, 1, INNER)).reshape(BLOCK, INNER)
        return (token_block, gate_block)
    second = run_layer(fetch_cols, LENGTH // BLOCK, write_cols, read_cols, step_cols, decay_cols, skip_cols, norm_cols)
    return second.reshape(GRID_W, per_col, BLOCK, INNER).transpose(1, 2, 0, 3).reshape(ROWS, GRID_W, INNER)
```

```python
import functools
import jax
import jax.numpy as jnp
from jax import lax
from jax.experimental import pallas as pl
from jax.experimental.pallas import tpu as pltpu
from jax.sharding import PartitionSpec as P

BLOCK = 256
HALF = 128
LANES = 128
CHUNK = 2
EPSILON = 1e-05
LOG2E = 1.4426950408889634
HIGHEST = lax.Precision.HIGHEST
MESH = pl.DeviceIdType.MESH
F32 = jnp.float32
BF16 = jnp.bfloat16
VMEM_BYTES = 60 * 1024 * 1024


def contract(a, b, dims, precision=None):
    return lax.dot_general(
        a, b, (dims, ((), ())), precision=precision, preferred_element_type=F32
    )


def iota(shape, axis):
    return lax.broadcasted_iota(jnp.int32, shape, axis)


def round_up(value, step):
    return -(-value // step) * step


def split(value, count):
    parts = []
    for _ in range(count - 1):
        part = value.astype(BF16)
        parts.append(part)
        value = value - part.astype(F32)
    parts.append(value.astype(BF16))
    return parts


def span_of(b):
    return pl.ds(pl.multiple_of(b * BLOCK, BLOCK), BLOCK)


class Layer:
    def __init__(self, **refs):
        self.__dict__.update(refs)


def prepare_sums(layer):
    heads, length = layer.decay.shape
    blocks = length // BLOCK
    padded = layer.cum.shape[1]
    layer.stage[...] = jnp.zeros_like(layer.stage)
    for p, part in enumerate(split(layer.decay[...] * LOG2E, 3)):
        for b in range(blocks):
            layer.stage[b, p, :heads] = part[:, b * BLOCK : (b + 1) * BLOCK]
    upper = (iota((BLOCK, BLOCK), 0) <= iota((BLOCK, BLOCK), 1)).astype(BF16)
    sums = contract(layer.stage[...].reshape(blocks * 3 * padded, BLOCK), upper, ((1,), (0,)))
    sums = sums.reshape(blocks, 3, padded, BLOCK)
    run = jnp.zeros((padded, 1), F32)
    for b in range(blocks):
        cum = sums[b, 0] + sums[b, 1] + sums[b, 2]
        final = cum[:, BLOCK - 1 :]
        layer.cum[b] = cum
        layer.weights[b, :heads] = (
            jnp.exp2(final[:heads] - cum[:heads]) * layer.step[:, b * BLOCK : (b + 1) * BLOCK]
        )
        layer.fades[b] = jnp.broadcast_to(jnp.exp2(final), (padded, LANES))
        layer.before[b] = jnp.broadcast_to(jnp.exp2(run), (padded, LANES))
        run = run + final
    layer.total[...] = jnp.broadcast_to(run, (padded, LANES))


def prepare_scores(layer):
    blocks = layer.cum.shape[0]
    lower = (iota((BLOCK, BLOCK), 0) >= iota((BLOCK, BLOCK), 1)).astype(F32)

    def block(b, carry):
        across = jnp.transpose(layer.cum[b])
        layer.across[b] = across
        layer.lifting[b] = jnp.exp2(across)
        read = layer.read[:, span_of(b)]
        layer.scores[b] = contract(read, layer.write[:, span_of(b)], ((0,), (0,))) * lower
        read32 = read.astype(F32)
        layer.read_t[b] = jnp.transpose(jnp.concatenate([read32, read32], axis=0)).astype(BF16)
        return carry

    lax.fori_loop(0, blocks, block, 0)


def lanes_of(h):
    return slice(h * LANES, (h + 1) * LANES)


def add_state(layer, b, h, write32, own):
    loaded = (write32 * layer.weights[b, h : h + 1, :]).astype(BF16)
    gained = contract(loaded, own, ((1,), (0,)))
    held = layer.state[h]
    layer.local[b, h] = held
    layer.state[h] = layer.fades[b, h : h + 1, :] * held + gained


def inner_block(layer, b, h, own):
    across = layer.across[b, :, h : h + 1]
    cum = layer.cum[b, h : h + 1, :]
    step = layer.step[h : h + 1, span_of(b)]
    top, low = slice(0, HALF), slice(HALF, BLOCK)

    def mix(rows, cols, diagonal):
        spread = across[rows] - cum[:, cols]
        if diagonal:
            spread = jnp.minimum(spread, 0.0)
        return (jnp.exp2(spread) * layer.scores[b, rows, cols] * step[:, cols]).astype(BF16)

    skip = layer.skip[h]
    first = contract(mix(top, top, True), own[top], ((1,), (0,)))
    layer.inner[b, top, lanes_of(h)] = first + skip * own[top].astype(F32)
    both = jnp.concatenate([mix(low, top, False), mix(low, low, True)], axis=1)
    second = contract(both, own, ((1,), (0,)))
    layer.inner[b, low, lanes_of(h)] = second + skip * own[low].astype(F32)


def finish_block(layer, b, hs, store):
    held = jnp.concatenate(
        [layer.before[b, h : h + 1, :] * layer.prior[h] + layer.local[b, h] for h in hs], axis=1
    )
    parts = jnp.concatenate(split(held, 2), axis=0)
    from_state = contract(layer.read_t[b], parts, ((1,), (0,)))
    squares = jnp.zeros((BLOCK, LANES), F32)
    for i, h in enumerate(hs):
        out = layer.inner[b, :, lanes_of(h)]
        out += layer.lifting[b, :, h : h + 1] * from_state[:, i * LANES : (i + 1) * LANES]
        gate = layer.gate[b, :, lanes_of(h)].astype(F32)
        gated = out * (gate / (1.0 + jnp.exp2(gate * -LOG2E)))
        squares += gated * gated
        store(b, h, gated)
    layer.squares[b] += squares


def reduce_squares(layer, rows_ref):
    blocks = layer.squares.shape[0]
    rows_ref[...] = jnp.zeros_like(rows_ref)
    for b in range(blocks):
        parts = jnp.concatenate(split(layer.squares[b], 2), axis=1)
        row = contract(jnp.ones((8, 2 * LANES), BF16), parts, ((1,), (1,)))
        rows_ref[b : b + 1, :] = row[:1]


def column_scale(column, grid_rows, grid_cols, scales):
    high = BLOCK // grid_cols
    shape = (BLOCK, scales.shape[0])
    row = iota(shape, 0)
    depth = scales.shape[0] * grid_rows // BLOCK
    source = (row // grid_rows) * depth + (row % grid_rows) // high
    picked = contract((iota(shape, 1) == source).astype(F32), scales, ((1,), (0,)), HIGHEST)
    lane = (iota((BLOCK, BLOCK), 0) % high) * grid_cols + column
    return jnp.sum(jnp.where(iota((BLOCK, BLOCK), 1) == lane, picked, 0.0), axis=1, keepdims=True)


def greet_signal(axes):
    barrier = pltpu.get_barrier_semaphore()
    for axis, count in axes:
        me = lax.axis_index(axis)
        for hop in range(1, count):
            pl.semaphore_signal(
                barrier, inc=1, device_id={axis: lax.rem(me + hop, count)}, device_id_type=MESH
            )


def greet_wait(axes):
    pl.semaphore_wait(
        pltpu.get_barrier_semaphore(), sum(count - 1 for _, count in axes)
    )


def head_sum(count, own_ref, held, send_sems, recv_sems):
    me = lax.axis_index("head")
    copies = []
    for hop in range(1, count):
        copy = pltpu.make_async_remote_copy(
            src_ref=own_ref,
            dst_ref=held.at[hop - 1],
            send_sem=send_sems.at[hop - 1],
            recv_sem=recv_sems.at[hop - 1],
            device_id={"head": lax.rem(me + hop, count)},
            device_id_type=MESH,
        )
        copy.start()
        copies.append(copy)
    for copy in copies:
        copy.wait()
    total = own_ref[...]
    for hop in range(1, count):
        total += held[hop - 1]
    return total


class Exchange:
    def __init__(self, seq, layer, sent, swapped, passed, came, near, swap_sems, near_sems, pass_sems):
        self.layer, self.sent, self.swapped = layer, sent, swapped
        self.passed, self.came, self.near = passed, came, near
        self.swap_sems, self.near_sems, self.pass_sems = swap_sems, near_sems, pass_sems
        me = lax.axis_index("seq")
        self.place = lax.rem(me, 2)
        self.partner = me + 1 - 2 * self.place
        self.group = me // 2
        self.groups = seq // 2
        self.ahead = lax.rem(me + 2, seq)

    def near_copy(self):
        return pltpu.make_async_remote_copy(
            src_ref=self.layer.total, dst_ref=self.near, send_sem=self.near_sems.at[0],
            recv_sem=self.near_sems.at[1], device_id={"seq": self.partner}, device_id_type=MESH,
        )

    def swap_copy(self, c, part):
        return pltpu.make_async_remote_copy(
            src_ref=self.sent.at[part], dst_ref=self.swapped.at[part],
            send_sem=self.swap_sems.at[0, c], recv_sem=self.swap_sems.at[1, c],
            device_id={"seq": self.partner}, device_id_type=MESH,
        )

    def pass_copy(self, c, part):
        return pltpu.make_async_remote_copy(
            src_ref=self.passed.at[part], dst_ref=self.came.at[part],
            send_sem=self.pass_sems.at[0, c], recv_sem=self.pass_sems.at[1, c],
            device_id={"seq": self.ahead}, device_id_type=MESH,
        )

    def swap(self, c, part):
        for h in range(part.start, part.start + part.size):
            self.sent[h] = self.layer.state[h].astype(BF16)
        self.swap_copy(c, part).start()

    def fades(self):
        self.near_copy().wait()
        mine, other = self.layer.total[...], self.near[...]
        even = self.place == 0
        return jnp.exp2(jnp.where(even, mine, other)), jnp.exp2(jnp.where(even, other, mine))

    def step(self, c, part, fades):
        layer = self.layer
        first_fade, last_fade = fades
        even = self.place == 0
        self.swap_copy(c, part).wait()

        @pl.when(self.group > 0)
        def _():
            self.pass_copy(c, part).wait_recv()

        for h in range(part.start, part.start + part.size):
            mine, other = layer.state[h], self.swapped[h].astype(F32)
            first, last = jnp.where(even, mine, other), jnp.where(even, other, mine)
            before = self.came[h].astype(F32)
            middle = first_fade[h : h + 1] * before + first
            self.passed[h] = (last_fade[h : h + 1] * middle + last).astype(BF16)
            layer.prior[h] = jnp.where(even, before, middle)

        @pl.when(self.group < self.groups - 1)
        def _():
            self.pass_copy(c, part).start()

    def settle(self, parts):
        for c, part in enumerate(parts):

            @pl.when(self.group < self.groups - 1)
            def _(c=c, part=part):
                self.pass_copy(c, part).wait_send()


def fused_kernel(
    seq, head_count, inner, grid_cols, local_cols, per_col,
    skip1, skip2, x_hbm, gate1_hbm, gate2_hbm, write1, read1, step1, decay1, gain1,
    write2, read2, step2, decay2,
    out_hbm, total_ref,
    x, gate1, gate2, sendbuf, recvbuf, hidden, outbuf, innerbuf, turned,
    stage, cum1, cum2, weights, fades1, fades2, before1, before2, total1, total2, across, lifting,
    scores, read_t, state, local, prior, squares, rows1, held1, held2, scale, scales, column,
    sent1, swapped1, passed1, came1, near1, sent2, swapped2, passed2, came2, near2,
    load_sems, bulk_send, bulk_recv, keep_sems, sum1, sum2, scale_send, scale_recv, out_sems,
    swap1_sems, near1_sems, pass1_sems, swap2_sems, near2_sems, pass2_sems,
):
    axes = (("seq", seq), ("head", head_count))
    me = lax.axis_index("seq")
    blocks, _, features = x.shape
    heads = features // LANES
    high = BLOCK // grid_cols
    grid_rows = blocks * high
    slabs = BLOCK // grid_rows
    parts = [pl.ds(c, min(CHUNK, heads - c)) for c in range(0, heads, CHUNK)]
    numbers = [range(part.start, part.start + part.size) for part in parts]
    chunks = len(parts)
    greet_signal(axes)

    def load(b):
        return pltpu.make_async_copy(x_hbm.at[b], x.at[b], load_sems.at[0, b])

    gate_loads = [
        pltpu.make_async_copy(gate1_hbm, gate1, load_sems.at[1, 0]),
        pltpu.make_async_copy(gate2_hbm, gate2, load_sems.at[2, 0]),
    ]
    for b in range(blocks):
        load(b).start()
    for copy in gate_loads:
        copy.start()

    shared = dict(
        stage=stage, weights=weights, across=across, lifting=lifting, scores=scores,
        read_t=read_t, state=state, local=local, prior=prior, squares=squares, inner=innerbuf,
    )
    one = Layer(
        skip=skip1, gate=gate1, write=write1, read=read1, step=step1, decay=decay1, cum=cum1,
        fades=fades1, before=before1, total=total1, **shared,
    )
    two = Layer(
        skip=skip2, gate=gate2, write=write2, read=read2, step=step2, decay=decay2, cum=cum2,
        fades=fades2, before=before2, total=total2, **shared,
    )
    ex1 = Exchange(
        seq, one, sent1, swapped1, passed1, came1, near1, swap1_sems, near1_sems, pass1_sems
    )
    ex2 = Exchange(
        seq, two, sent2, swapped2, passed2, came2, near2, swap2_sems, near2_sems, pass2_sems
    )

    @pl.when(ex1.group == 0)
    def _():
        came1[...] = jnp.zeros_like(came1)
        came2[...] = jnp.zeros_like(came2)

    prepare_sums(one)
    state[...] = jnp.zeros_like(state)

    def states1(b, carry):
        load(b).wait()
        write32 = write1[:, span_of(b)].astype(F32)
        for h in range(heads):
            add_state(one, b, h, write32, x[b, :, lanes_of(h)])
        return carry

    lax.fori_loop(0, blocks, states1, 0)
    greet_wait(axes)
    ex1.near_copy().start()
    for c, part in enumerate(parts):
        ex1.swap(c, part)

    prepare_scores(one)
    squares[...] = jnp.zeros_like(squares)

    def inner1(c):
        def block(b, carry):
            for h in numbers[c]:
                inner_block(one, b, h, x[b, :, lanes_of(h)])
            return carry

        lax.fori_loop(0, blocks, block, 0)

    def store1(b, h, gated):
        slot = turned.at[h % 2]
        slot[...] = gated
        for col in range(grid_cols):
            sendbuf[col // local_cols, col % local_cols, b, :, lanes_of(h)] = slot[
                pl.ds(col, high, stride=grid_cols), :
            ].astype(BF16)

    def finish1(c):
        def block(b, carry):
            finish_block(one, b, numbers[c], store1)
            return carry

        lax.fori_loop(0, blocks, block, 0)

    def wide(c):
        return pl.ds(parts[c].start * LANES, parts[c].size * LANES)

    def bulk(c, hop):
        to = lax.rem(me - hop + seq, seq)
        return pltpu.make_async_remote_copy(
            src_ref=sendbuf.at[to, :, :, :, wide(c)],
            dst_ref=recvbuf.at[me, :, :, :, wide(c)],
            send_sem=bulk_send.at[hop - 1, c],
            recv_sem=bulk_recv.at[hop - 1, c],
            device_id={"seq": to},
            device_id_type=MESH,
        )

    def keep(c):
        return pltpu.make_async_copy(
            sendbuf.at[me, :, :, :, wide(c)], recvbuf.at[me, :, :, :, wide(c)], keep_sems.at[c]
        )

    def send_all(c):
        for hop in range(1, seq):
            bulk(c, hop).start()
        keep(c).start()

    inner1(0)
    fades = ex1.fades()
    for copy in gate_loads:
        copy.wait()
    ex1.step(0, parts[0], fades)
    finish1(0)
    for hop in range(1, seq):

        @pl.when(hop <= me)
        def _(hop=hop):
            bulk(0, hop).start()

    for c in range(1, chunks):
        ex1.step(c, parts[c], fades)
    for hop in range(1, seq):

        @pl.when(hop > me)
        def _(hop=hop):
            bulk(0, hop).start()

    keep(0).start()
    for c in range(1, chunks):
        inner1(c)
        finish1(c)
        if c == 1:
            send_all(c)
    reduce_squares(one, rows1)
    scale[...] = lax.rsqrt(head_sum(head_count, rows1, held1, sum1.at[0], sum1.at[1]) / inner + EPSILON)
    depth = scale.shape[0]
    mine = pl.ds(pl.multiple_of(me * depth, depth), depth)
    scale_copies = []
    for hop in range(1, seq):
        copy = pltpu.make_async_remote_copy(
            src_ref=scale,
            dst_ref=scales.at[mine],
            send_sem=scale_send.at[hop - 1],
            recv_sem=scale_recv.at[hop - 1],
            device_id={"seq": lax.rem(me - hop + seq, seq)},
            device_id_type=MESH,
        )
        copy.start()
        scale_copies.append(copy)
    for c in range(2, chunks):
        send_all(c)
    scales[mine, :] = scale[...]

    prepare_sums(two)
    prepare_scores(two)
    state[...] = jnp.zeros_like(state)
    squares[...] = jnp.zeros_like(squares)
    ex2.near_copy().start()
    for copy in scale_copies:
        copy.wait()

    def columns(b, carry):
        window = pl.ds(
            pl.multiple_of(lax.rem(b, per_col) * slabs * depth, slabs * depth), slabs * depth
        )
        picked = column_scale(me * local_cols + b // per_col, grid_rows, grid_cols, scales[window, :])
        column[b] = jnp.broadcast_to(picked, (BLOCK, LANES))
        return carry

    lax.fori_loop(0, blocks, columns, 0)

    def arrive(c):
        keep(c).wait()
        for hop in range(1, seq):
            bulk(c, hop).wait()

    def states2(c):
        def block(b, carry):
            write32 = write2[:, span_of(b)].astype(F32)
            slab = pl.ds(lax.rem(b, per_col) * slabs, slabs)
            for h in numbers[c]:
                lanes = lanes_of(h)
                own = recvbuf[slab, b // per_col, :, :, lanes].astype(F32).reshape(BLOCK, LANES)
                own = (own * column[b] * gain1[:, lanes]).astype(BF16)
                hidden[b, :, lanes] = own
                add_state(two, b, h, write32, own)
            return carry

        lax.fori_loop(0, blocks, block, 0)

    def inner2(c):
        def block(b, carry):
            for h in numbers[c]:
                inner_block(two, b, h, hidden[b, :, lanes_of(h)])
            return carry

        lax.fori_loop(0, blocks, block, 0)

    def store2(b, h, gated):
        outbuf[b, :, lanes_of(h)] = gated.astype(BF16)

    def put(c):
        return pltpu.make_async_copy(
            outbuf.at[:, :, wide(c)], out_hbm.at[:, :, wide(c)], out_sems.at[c]
        )

    def finish2(c):
        def block(b, carry):
            finish_block(two, b, numbers[c], store2)
            return carry

        lax.fori_loop(0, blocks, block, 0)
        put(c).start()

    last = chunks - 1
    early = max(last - 1, 0)
    fades = None
    for c in range(chunks):
        if c == last and last > 0:
            fades = ex2.fades()
            for e in range(early):
                ex2.step(e, parts[e], fades)
            for e in range(early):
                finish2(e)
        arrive(c)
        states2(c)
        ex2.swap(c, parts[c])
        if c < last:
            inner2(c)
    if fades is None:
        fades = ex2.fades()
    for c in range(early, last):
        ex2.step(c, parts[c], fades)
    inner2(last)
    ex2.step(last, parts[last], fades)
    for c in range(early, chunks):
        finish2(c)
    reduce_squares(two, rows1)
    total_ref[...] = head_sum(head_count, rows1, held2, sum2.at[0], sum2.at[1])
    for c in range(chunks):
        put(c).wait()
    ex1.settle(parts)
    ex2.settle(parts)


def norm_kernel(inner, per_col, gated_ref, squares_ref, gain_ref, out_ref, turned):
    cols, rows, features = gated_ref.shape
    square = (BLOCK, BLOCK)
    start = pl.program_id(0) * rows
    lane = start % BLOCK + iota(square, 0) % rows
    sums = contract((lane == iota(square, 1)).astype(F32), squares_ref[...], ((1,), (1,)), HIGHEST)
    block = (iota(sums.shape, 0) // rows) * per_col + start // BLOCK
    sums = jnp.sum(jnp.where(iota(sums.shape, 1) == block, sums, 0.0), axis=1, keepdims=True)
    scaled = lax.rsqrt(sums / inner + EPSILON)
    for at in range(0, features, LANES):
        lanes = slice(at, at + LANES)
        gated = gated_ref[:, :, lanes].astype(F32).reshape(BLOCK, LANES)
        result = gated * scaled * gain_ref[:, lanes]
        if cols > 1:
            slot = turned.at[at // LANES % 2]
            for c in range(cols):
                slot[pl.ds(c, rows, stride=cols), :] = result[c * rows : (c + 1) * rows]
            out_ref[:, :, lanes] = slot[...].reshape(rows, cols, LANES).astype(BF16)
        else:
            out_ref[:, lanes] = result.astype(BF16)


def body(
    seq, head, tokens_in, gate_rows, gate_cols, write_rows, read_rows, step_rows, decay_rows,
    skip_rows, norm_rows, write_cols, read_cols, step_cols, decay_cols, skip_cols, norm_cols,
):
    grid_rows, grid_cols, features = tokens_in.shape
    blocks = grid_rows * grid_cols // BLOCK
    high = BLOCK // grid_cols
    local_cols = grid_cols // seq
    all_rows = grid_rows * seq
    per_col = all_rows // BLOCK
    inner = features * head
    heads, size = step_rows.shape[0], write_rows.shape[0]
    width = features // heads
    depth = round_up(blocks, 8)
    padded = round_up(heads, 16)
    chunks = -(-heads // CHUNK)
    dma = pltpu.SemaphoreType.DMA
    anywhere = pl.BlockSpec(memory_space=pl.ANY)
    whole = pl.BlockSpec(memory_space=pltpu.VMEM)
    smem = pl.BlockSpec(memory_space=pltpu.SMEM)
    vmem = pltpu.VMEM
    tokens = (blocks, BLOCK, features)
    packed = (seq, local_cols, blocks, high, features)
    sums = (blocks, padded, BLOCK)
    rows = (blocks, padded, LANES)
    total = (padded, LANES)
    tall = (blocks, BLOCK, padded)
    states = (heads, size, width)
    exchange = [vmem(states, BF16)] * 4 + [vmem(total, F32)]
    gate = jnp.transpose(gate_cols, (1, 0, 2)).reshape(tokens)
    gated, squares = pl.pallas_call(
        functools.partial(fused_kernel, seq, head, inner, grid_cols, local_cols, per_col),
        out_shape=(
            jax.ShapeDtypeStruct(tokens, BF16),
            jax.ShapeDtypeStruct((depth, BLOCK), F32),
        ),
        in_specs=[smem, smem] + [anywhere] * 3 + [whole] * 9,
        out_specs=(anywhere, whole),
        scratch_shapes=[
            vmem(tokens, BF16), vmem(tokens, BF16), vmem(tokens, BF16),
            vmem(packed, BF16), vmem(packed, BF16), vmem(tokens, BF16), vmem(tokens, BF16),
            vmem(tokens, F32), vmem((2, BLOCK, LANES), F32),
            vmem((blocks, 3, padded, BLOCK), BF16), vmem(sums, F32), vmem(sums, F32),
            vmem(sums, F32), vmem(rows, F32), vmem(rows, F32), vmem(rows, F32), vmem(rows, F32),
            vmem(total, F32), vmem(total, F32), vmem(tall, F32), vmem(tall, F32),
            vmem((blocks, BLOCK, BLOCK), F32), vmem((blocks, BLOCK, 2 * size), BF16),
            vmem(states, F32), vmem((blocks,) + states, F32), vmem(states, F32),
            vmem((blocks, BLOCK, LANES), F32), vmem((depth, BLOCK), F32),
            vmem((head - 1, depth, BLOCK), F32), vmem((head - 1, depth, BLOCK), F32),
            vmem((depth, BLOCK), F32), vmem((seq * depth, BLOCK), F32),
            vmem((blocks, BLOCK, LANES), F32),
            *exchange, *exchange,
            dma((3, blocks)), dma((seq - 1, chunks)), dma((seq - 1, chunks)), dma((chunks,)),
            dma((2, head - 1)), dma((2, head - 1)), dma((seq - 1,)), dma((seq - 1,)),
            dma((chunks,)),
            dma((2, chunks)), dma((2,)), dma((2, chunks)),
            dma((2, chunks)), dma((2,)), dma((2, chunks)),
        ],
        compiler_params=pltpu.CompilerParams(
            collective_id=0, has_side_effects=True, vmem_limit_bytes=VMEM_BYTES
        ),
        name="fused",
    )(
        skip_rows, skip_cols, tokens_in.reshape(tokens), gate_rows.reshape(tokens), gate,
        write_rows, read_rows, step_rows, decay_rows, norm_rows.reshape(1, features),
        write_cols, read_cols, step_cols, decay_cols,
    )
    part = BLOCK // local_cols
    out_shape, out_spec = (all_rows, local_cols, features), (part, local_cols, features)
    if local_cols == 1:
        out_shape, out_spec = (all_rows, features), (part, features)
    result = pl.pallas_call(
        functools.partial(norm_kernel, inner, per_col),
        grid=(all_rows // part,),
        out_shape=jax.ShapeDtypeStruct(out_shape, BF16),
        in_specs=[
            pl.BlockSpec((local_cols, part, features), lambda q: (0, q, 0)),
            pl.BlockSpec(squares.shape, lambda q: (0, 0)),
            pl.BlockSpec((1, features), lambda q: (0, 0)),
        ],
        out_specs=pl.BlockSpec(out_spec, lambda q: (q,) + (0,) * (len(out_spec) - 1)),
        scratch_shapes=[pltpu.VMEM((2, BLOCK, LANES), F32)],
        compiler_params=pltpu.CompilerParams(vmem_limit_bytes=VMEM_BYTES),
        name="norm",
    )(gated.reshape(local_cols, all_rows, features), squares, norm_cols.reshape(1, features))
    return result.reshape(all_rows, local_cols, features)


def solution(mesh):
    placed = (
        P("seq", None, "head"),
        P("seq", None, "head"),
        P(None, "seq", "head"),
        P(None, "seq"),
        P(None, "seq"),
        P("head", "seq"),
        P("head", "seq"),
        P("head"),
        P("head"),
        P(None, "seq"),
        P(None, "seq"),
        P("head", "seq"),
        P("head", "seq"),
        P("head"),
        P("head"),
    )
    return jax.shard_map(
        functools.partial(body, mesh.shape["seq"], mesh.shape["head"]),
        mesh=mesh, in_specs=placed, out_specs=P(None, "seq", "head"), check_vma=False,
    )
```

```python
import functools
import jax
import jax.numpy as jnp
from jax import lax
from jax.experimental import pallas as pl
from jax.experimental.pallas import tpu as pltpu
from jax.sharding import PartitionSpec as P

BLOCK = 256
HALF = 128
LANES = 128
CHUNK = 2
SMALL = 9
STAGGER = 3
EPSILON = 1e-05
LOG2E = 1.4426950408889634
HIGHEST = lax.Precision.HIGHEST
MESH = pl.DeviceIdType.MESH
F32 = jnp.float32
BF16 = jnp.bfloat16
VMEM_BYTES = 60 * 1024 * 1024


def contract(a, b, dims, precision=None):
    return lax.dot_general(
        a, b, (dims, ((), ())), precision=precision, preferred_element_type=F32
    )


def iota(shape, axis):
    return lax.broadcasted_iota(jnp.int32, shape, axis)


def round_up(value, step):
    return -(-value // step) * step


def split(value, count):
    parts = []
    for _ in range(count - 1):
        part = value.astype(BF16)
        parts.append(part)
        value = value - part.astype(F32)
    parts.append(value.astype(BF16))
    return parts


def span_of(b):
    return pl.ds(pl.multiple_of(b * BLOCK, BLOCK), BLOCK)


class Layer:
    def __init__(self, **refs):
        self.__dict__.update(refs)


def prepare_sums(layer):
    heads, length = layer.decay.shape
    blocks = length // BLOCK
    padded = layer.cum.shape[1]
    layer.stage[...] = jnp.zeros_like(layer.stage)
    for p, part in enumerate(split(layer.decay[...] * LOG2E, 3)):
        for b in range(blocks):
            layer.stage[b, p, :heads] = part[:, b * BLOCK : (b + 1) * BLOCK]
    upper = (iota((BLOCK, BLOCK), 0) <= iota((BLOCK, BLOCK), 1)).astype(BF16)
    sums = contract(layer.stage[...].reshape(blocks * 3 * padded, BLOCK), upper, ((1,), (0,)))
    sums = sums.reshape(blocks, 3, padded, BLOCK)
    run = jnp.zeros((padded, 1), F32)
    for b in range(blocks):
        cum = sums[b, 0] + sums[b, 1] + sums[b, 2]
        final = cum[:, BLOCK - 1 :]
        layer.cum[b] = cum
        layer.weights[b, :heads] = (
            jnp.exp2(final[:heads] - cum[:heads]) * layer.step[:, b * BLOCK : (b + 1) * BLOCK]
        )
        layer.fades[b] = jnp.broadcast_to(jnp.exp2(final), (padded, LANES))
        layer.before[b] = jnp.broadcast_to(jnp.exp2(run), (padded, LANES))
        run = run + final
    layer.total[...] = jnp.broadcast_to(run, (padded, LANES))


def prepare_scores(layer):
    blocks = layer.cum.shape[0]
    lower = (iota((BLOCK, BLOCK), 0) >= iota((BLOCK, BLOCK), 1)).astype(F32)

    def block(b, carry):
        across = jnp.transpose(layer.cum[b])
        layer.across[b] = across
        layer.lifting[b] = jnp.exp2(across)
        read = layer.read[:, span_of(b)]
        layer.scores[b] = contract(read, layer.write[:, span_of(b)], ((0,), (0,))) * lower
        read32 = read.astype(F32)
        layer.read_t[b] = jnp.transpose(jnp.concatenate([read32, read32], axis=0)).astype(BF16)
        return carry

    lax.fori_loop(0, blocks, block, 0)


def lanes_of(h):
    return slice(h * LANES, (h + 1) * LANES)


def add_state(layer, b, h, write32, own):
    loaded = (write32 * layer.weights[b, h : h + 1, :]).astype(BF16)
    gained = contract(loaded, own, ((1,), (0,)))
    held = layer.state[h]
    layer.local[b, h] = held
    layer.state[h] = layer.fades[b, h : h + 1, :] * held + gained


def inner_block(layer, b, h, own):
    across = layer.across[b, :, h : h + 1]
    cum = layer.cum[b, h : h + 1, :]
    step = layer.step[h : h + 1, span_of(b)]
    top, low = slice(0, HALF), slice(HALF, BLOCK)

    def mix(rows, cols, diagonal):
        spread = across[rows] - cum[:, cols]
        if diagonal:
            spread = jnp.minimum(spread, 0.0)
        return (jnp.exp2(spread) * layer.scores[b, rows, cols] * step[:, cols]).astype(BF16)

    skip = layer.skip[h]
    first = contract(mix(top, top, True), own[top], ((1,), (0,)))
    layer.inner[b, top, lanes_of(h)] = first + skip * own[top].astype(F32)
    both = jnp.concatenate([mix(low, top, False), mix(low, low, True)], axis=1)
    second = contract(both, own, ((1,), (0,)))
    layer.inner[b, low, lanes_of(h)] = second + skip * own[low].astype(F32)


def finish_block(layer, b, hs, store):
    held = jnp.concatenate(
        [layer.before[b, h : h + 1, :] * layer.prior[h] + layer.local[b, h] for h in hs], axis=1
    )
    parts = jnp.concatenate(split(held, 2), axis=0)
    from_state = contract(layer.read_t[b], parts, ((1,), (0,)))
    squares = jnp.zeros((BLOCK, LANES), F32)
    for i, h in enumerate(hs):
        out = layer.inner[b, :, lanes_of(h)]
        out += layer.lifting[b, :, h : h + 1] * from_state[:, i * LANES : (i + 1) * LANES]
        gate = layer.gate[b, :, lanes_of(h)].astype(F32)
        gated = out * (gate / (1.0 + jnp.exp2(gate * -LOG2E)))
        squares += gated * gated
        store(b, h, gated)
    layer.squares[b] += squares


def reduce_squares(layer, rows_ref):
    blocks = layer.squares.shape[0]
    rows_ref[...] = jnp.zeros_like(rows_ref)
    for b in range(blocks):
        parts = jnp.concatenate(split(layer.squares[b], 2), axis=1)
        row = contract(jnp.ones((8, 2 * LANES), BF16), parts, ((1,), (1,)))
        rows_ref[b : b + 1, :] = row[:1]


def column_scale(column, grid_rows, grid_cols, scales):
    high = BLOCK // grid_cols
    shape = (BLOCK, scales.shape[0])
    row = iota(shape, 0)
    depth = scales.shape[0] * grid_rows // BLOCK
    source = (row // grid_rows) * depth + (row % grid_rows) // high
    picked = contract((iota(shape, 1) == source).astype(F32), scales, ((1,), (0,)), HIGHEST)
    lane = (iota((BLOCK, BLOCK), 0) % high) * grid_cols + column
    return jnp.sum(jnp.where(iota((BLOCK, BLOCK), 1) == lane, picked, 0.0), axis=1, keepdims=True)


def greet_signal(axes):
    barrier = pltpu.get_barrier_semaphore()
    for axis, count in axes:
        me = lax.axis_index(axis)
        for hop in range(1, count):
            pl.semaphore_signal(
                barrier, inc=1, device_id={axis: lax.rem(me + hop, count)}, device_id_type=MESH
            )


def greet_wait(axes):
    pl.semaphore_wait(
        pltpu.get_barrier_semaphore(), sum(count - 1 for _, count in axes)
    )


def head_sum(count, own_ref, held, send_sems, recv_sems):
    me = lax.axis_index("head")
    copies = []
    for hop in range(1, count):
        copy = pltpu.make_async_remote_copy(
            src_ref=own_ref,
            dst_ref=held.at[hop - 1],
            send_sem=send_sems.at[hop - 1],
            recv_sem=recv_sems.at[hop - 1],
            device_id={"head": lax.rem(me + hop, count)},
            device_id_type=MESH,
        )
        copy.start()
        copies.append(copy)
    for copy in copies:
        copy.wait()
    total = own_ref[...]
    for hop in range(1, count):
        total += held[hop - 1]
    return total


class Exchange:
    def __init__(self, seq, layer, sent, swapped, passed, came, near, swap_sems, near_sems, pass_sems):
        self.layer, self.sent, self.swapped = layer, sent, swapped
        self.passed, self.came, self.near = passed, came, near
        self.swap_sems, self.near_sems, self.pass_sems = swap_sems, near_sems, pass_sems
        me = lax.axis_index("seq")
        self.place = lax.rem(me, 2)
        self.partner = me + 1 - 2 * self.place
        self.group = me // 2
        self.groups = seq // 2
        self.ahead = lax.rem(me + 2, seq)

    def near_copy(self):
        return pltpu.make_async_remote_copy(
            src_ref=self.layer.total, dst_ref=self.near, send_sem=self.near_sems.at[0],
            recv_sem=self.near_sems.at[1], device_id={"seq": self.partner}, device_id_type=MESH,
        )

    def swap_copy(self, c, part):
        return pltpu.make_async_remote_copy(
            src_ref=self.sent.at[part], dst_ref=self.swapped.at[part],
            send_sem=self.swap_sems.at[0, c], recv_sem=self.swap_sems.at[1, c],
            device_id={"seq": self.partner}, device_id_type=MESH,
        )

    def pass_copy(self, c, part):
        return pltpu.make_async_remote_copy(
            src_ref=self.passed.at[part], dst_ref=self.came.at[part],
            send_sem=self.pass_sems.at[0, c], recv_sem=self.pass_sems.at[1, c],
            device_id={"seq": self.ahead}, device_id_type=MESH,
        )

    def swap(self, c, part):
        for h in range(part.start, part.start + part.size):
            self.sent[h] = self.layer.state[h].astype(BF16)
        self.swap_copy(c, part).start()

    def fades(self):
        self.near_copy().wait()
        mine, other = self.layer.total[...], self.near[...]
        even = self.place == 0
        return jnp.exp2(jnp.where(even, mine, other)), jnp.exp2(jnp.where(even, other, mine))

    def step(self, c, part, fades):
        layer = self.layer
        first_fade, last_fade = fades
        even = self.place == 0
        self.swap_copy(c, part).wait()

        @pl.when(self.group > 0)
        def _():
            self.pass_copy(c, part).wait_recv()

        for h in range(part.start, part.start + part.size):
            mine, other = layer.state[h], self.swapped[h].astype(F32)
            first, last = jnp.where(even, mine, other), jnp.where(even, other, mine)
            before = self.came[h].astype(F32)
            middle = first_fade[h : h + 1] * before + first
            self.passed[h] = (last_fade[h : h + 1] * middle + last).astype(BF16)
            layer.prior[h] = jnp.where(even, before, middle)

        @pl.when(self.group < self.groups - 1)
        def _():
            self.pass_copy(c, part).start()

    def settle(self, parts):
        for c, part in enumerate(parts):

            @pl.when(self.group < self.groups - 1)
            def _(c=c, part=part):
                self.pass_copy(c, part).wait_send()


def fused_kernel(
    seq, head_count, inner, grid_cols, local_cols, per_col,
    skip1, skip2, x_hbm, gate1_hbm, gate2_hbm, *refs
):
    small_hbm, refs = refs[:SMALL], refs[SMALL:]
    out_hbm, scale_ref, x, gate1, gate2, sendbuf, recvbuf, hidden, innerbuf, turned, *refs = refs
    small, refs = refs[:SMALL], refs[SMALL:]
    decay1, step1, write1, read1, gain1, decay2, step2, write2, read2 = small
    (
        gate_raw, outbuf, woven,
    stage, cum1, cum2, weights, fades1, fades2, before1, before2, total1, total2, across, lifting,
    scores, read_t, state, local, prior, squares, rows1, held1, held2, scale, scales, column,
    sent1, swapped1, passed1, came1, near1, sent2, swapped2, passed2, came2, near2,
    load_sems, small_sems, bulk_send, bulk_recv, keep_sems, sum1, sum2, scale_send, scale_recv, out_sems,
    swap1_sems, near1_sems, pass1_sems, swap2_sems, near2_sems, pass2_sems,
    ) = refs
    axes = (("seq", seq), ("head", head_count))
    me = lax.axis_index("seq")
    blocks, _, features = x.shape
    heads = features // LANES
    high = BLOCK // grid_cols
    grid_rows = blocks * high
    slabs = BLOCK // grid_rows
    parts = [pl.ds(c, min(CHUNK, heads - c)) for c in range(0, heads, CHUNK)]
    numbers = [range(part.start, part.start + part.size) for part in parts]
    chunks = len(parts)
    greet_signal(axes)

    def load(b):
        return pltpu.make_async_copy(x_hbm.at[b], x.at[b], load_sems.at[0, b])

    gate_loads = [
        pltpu.make_async_copy(gate1_hbm, gate1, load_sems.at[1, 0]),
        pltpu.make_async_copy(
            gate2_hbm, gate_raw if local_cols > 1 else gate2, load_sems.at[2, 0]
        ),
    ]
    small_loads = [
        pltpu.make_async_copy(source, target, small_sems.at[i])
        for i, (source, target) in enumerate(zip(small_hbm, small))
    ]
    for copy in small_loads[:3]:
        copy.start()
    for b in range(blocks):
        load(b).start()
    for copy in small_loads[3:] + gate_loads:
        copy.start()

    shared = dict(
        stage=stage, weights=weights, across=across, lifting=lifting, scores=scores,
        read_t=read_t, state=state, local=local, prior=prior, squares=squares, inner=innerbuf,
    )
    one = Layer(
        skip=skip1, gate=gate1, write=write1, read=read1, step=step1, decay=decay1, cum=cum1,
        fades=fades1, before=before1, total=total1, **shared,
    )
    two = Layer(
        skip=skip2, gate=gate2, write=write2, read=read2, step=step2, decay=decay2, cum=cum2,
        fades=fades2, before=before2, total=total2, **shared,
    )
    ex1 = Exchange(
        seq, one, sent1, swapped1, passed1, came1, near1, swap1_sems, near1_sems, pass1_sems
    )
    ex2 = Exchange(
        seq, two, sent2, swapped2, passed2, came2, near2, swap2_sems, near2_sems, pass2_sems
    )

    @pl.when(ex1.group == 0)
    def _():
        came1[...] = jnp.zeros_like(came1)
        came2[...] = jnp.zeros_like(came2)

    for copy in small_loads[:2]:
        copy.wait()
    prepare_sums(one)
    small_loads[2].wait()
    state[...] = jnp.zeros_like(state)

    def states1(b, carry):
        load(b).wait()
        write32 = write1[:, span_of(b)].astype(F32)
        for h in range(heads):
            add_state(one, b, h, write32, x[b, :, lanes_of(h)])
        return carry

    lax.fori_loop(0, blocks, states1, 0)
    greet_wait(axes)
    ex1.near_copy().start()
    for c, part in enumerate(parts):
        ex1.swap(c, part)

    small_loads[3].wait()
    prepare_scores(one)
    squares[...] = jnp.zeros_like(squares)

    def inner1(c):
        def block(b, carry):
            for h in numbers[c]:
                inner_block(one, b, h, x[b, :, lanes_of(h)])
            return carry

        lax.fori_loop(0, blocks, block, 0)

    def store1(b, h, gated):
        slot = turned.at[h % 2]
        slot[...] = gated
        for col in range(grid_cols):
            sendbuf[col // local_cols, col % local_cols, b, :, lanes_of(h)] = slot[
                pl.ds(col, high, stride=grid_cols), :
            ].astype(BF16)

    def finish1(c):
        def block(b, carry):
            finish_block(one, b, numbers[c], store1)
            return carry

        lax.fori_loop(0, blocks, block, 0)

    def wide(c):
        return pl.ds(parts[c].start * LANES, parts[c].size * LANES)

    def bulk(c, hop):
        to = lax.rem(me - hop + seq, seq)
        return pltpu.make_async_remote_copy(
            src_ref=sendbuf.at[to, :, :, :, wide(c)],
            dst_ref=recvbuf.at[me, :, :, :, wide(c)],
            send_sem=bulk_send.at[hop - 1, c],
            recv_sem=bulk_recv.at[hop - 1, c],
            device_id={"seq": to},
            device_id_type=MESH,
        )

    def keep(c):
        return pltpu.make_async_copy(
            sendbuf.at[me, :, :, :, wide(c)], recvbuf.at[me, :, :, :, wide(c)], keep_sems.at[c]
        )

    def send_all(c):
        for hop in range(1, seq):
            bulk(c, hop).start()
        keep(c).start()

    inner1(0)
    fades = ex1.fades()
    gate_loads[0].wait()
    ex1.step(0, parts[0], fades)
    finish1(0)
    for hop in range(1, seq):

        @pl.when(hop <= me)
        def _(hop=hop):
            bulk(0, hop).start()

    soon = ex1.group < ex1.groups // 2

    @pl.when(soon)
    def _():
        for c in range(1, chunks):
            ex1.step(c, parts[c], fades)

    for hop in range(1, seq):

        @pl.when(hop > me)
        def _(hop=hop):
            bulk(0, hop).start()

    keep(0).start()
    for c in range(1, chunks):
        inner1(c)

        @pl.when(jnp.logical_not(soon))
        def _(c=c):
            ex1.step(c, parts[c], fades)

        finish1(c)
        if c == 1:
            send_all(c)
    reduce_squares(one, rows1)
    scale[...] = lax.rsqrt(head_sum(head_count, rows1, held1, sum1.at[0], sum1.at[1]) / inner + EPSILON)
    depth = scale.shape[0]
    mine = pl.ds(pl.multiple_of(me * depth, depth), depth)
    scale_copies = []
    for hop in range(1, seq):
        copy = pltpu.make_async_remote_copy(
            src_ref=scale,
            dst_ref=scales.at[mine],
            send_sem=scale_send.at[hop - 1],
            recv_sem=scale_recv.at[hop - 1],
            device_id={"seq": lax.rem(me - hop + seq, seq)},
            device_id_type=MESH,
        )
        copy.start()
        scale_copies.append(copy)
    for c in range(2, chunks):
        send_all(c)
    scales[mine, :] = scale[...]

    for copy in small_loads[4:]:
        copy.wait()
    prepare_sums(two)
    prepare_scores(two)
    state[...] = jnp.zeros_like(state)
    squares[...] = jnp.zeros_like(squares)
    ex2.near_copy().start()
    gate_loads[1].wait()
    all_rows = per_col * BLOCK

    def place_of(b):
        return pl.ds(lax.rem(b, per_col) * (BLOCK * local_cols) + b // per_col, BLOCK, stride=local_cols)

    if local_cols > 1:
        for h in range(heads):
            slot = woven.at[h % 2]
            slot[...] = gate_raw[:, :, lanes_of(h)].astype(F32).reshape(all_rows * local_cols, LANES)
            for b in range(blocks):
                at = (b % per_col) * BLOCK * local_cols + b // per_col
                gate2[b, :, lanes_of(h)] = slot[pl.ds(at, BLOCK, stride=local_cols), :].astype(BF16)
    for copy in scale_copies:
        copy.wait()

    def columns(b, carry):
        window = pl.ds(
            pl.multiple_of(lax.rem(b, per_col) * slabs * depth, slabs * depth), slabs * depth
        )
        picked = column_scale(me * local_cols + b // per_col, grid_rows, grid_cols, scales[window, :])
        column[b] = jnp.broadcast_to(picked, (BLOCK, LANES))
        return carry

    lax.fori_loop(0, blocks, columns, 0)

    def arrive(c):
        keep(c).wait()
        for hop in range(1, seq):
            bulk(c, hop).wait()

    def states2(c):
        def block(b, carry):
            write32 = write2[:, span_of(b)].astype(F32)
            slab = pl.ds(lax.rem(b, per_col) * slabs, slabs)
            for h in numbers[c]:
                lanes = lanes_of(h)
                own = recvbuf[slab, b // per_col, :, :, lanes].astype(F32).reshape(BLOCK, LANES)
                own = (own * column[b] * gain1[h : h + 1, :]).astype(BF16)
                hidden[b, :, lanes] = own
                add_state(two, b, h, write32, own)
            return carry

        lax.fori_loop(0, blocks, block, 0)

    def inner2(c):
        def block(b, carry):
            for h in numbers[c]:
                inner_block(two, b, h, hidden[b, :, lanes_of(h)])
            return carry

        lax.fori_loop(0, blocks, block, 0)

    def store2(b, h, gated):
        if local_cols > 1:
            woven[h % CHUNK, place_of(b), :] = gated
        else:
            outbuf[pl.ds(pl.multiple_of(b * BLOCK, BLOCK), BLOCK), lanes_of(h)] = gated.astype(BF16)

    def put(c):
        span = (slice(None),) * (len(outbuf.shape) - 1) + (wide(c),)
        return pltpu.make_async_copy(outbuf.at[span], out_hbm.at[span], out_sems.at[c])

    def finish2(c):
        def block(b, carry):
            finish_block(two, b, numbers[c], store2)
            return carry

        lax.fori_loop(0, blocks, block, 0)
        if local_cols > 1:
            for h in numbers[c]:
                outbuf[:, :, lanes_of(h)] = (
                    woven[h % CHUNK].reshape(all_rows, local_cols, LANES).astype(BF16)
                )
        put(c).start()

    lag = jnp.minimum(ex2.group, STAGGER)
    fades = ex2.fades()

    def chain(slot):
        for late in range(STAGGER + 1):
            c = slot - 1 - late
            if 0 <= c < chunks:

                @pl.when(lag == late)
                def _(c=c):
                    ex2.step(c, parts[c], fades)

    for c in range(chunks):
        arrive(c)
        states2(c)
        ex2.swap(c, parts[c])
        inner2(c)
        chain(c)
    done = 0
    for slot in range(chunks, chunks + STAGGER + 1):
        chain(slot)
        while done < slot - STAGGER - 1 or (slot == chunks + STAGGER and done < chunks):
            finish2(done)
            done += 1
    reduce_squares(two, rows1)
    total = head_sum(head_count, rows1, held2, sum2.at[0], sum2.at[1])
    total = jnp.transpose(lax.rsqrt(total / inner + EPSILON))
    for b in range(blocks):
        at = (b % per_col) * BLOCK * local_cols + b // per_col
        scale_ref[pl.ds(at, BLOCK, stride=local_cols), :] = jnp.broadcast_to(
            total[:, b : b + 1], (BLOCK, LANES)
        )
    for c in range(chunks):
        put(c).wait()
    ex1.settle(parts)
    ex2.settle(parts)


def norm_kernel(gated_ref, scale_ref, gain_ref, out_ref):
    shape = gated_ref.shape[:-1] + (LANES,)
    scale = scale_ref[...].reshape(shape)
    for h in range(gated_ref.shape[-1] // LANES):
        lanes = lanes_of(h)
        gated = gated_ref[..., lanes].astype(F32)
        out_ref[..., lanes] = (gated * scale * gain_ref[h : h + 1, :]).astype(BF16)


def body(
    seq, head, tokens_in, gate_rows, gate_cols, write_rows, read_rows, step_rows, decay_rows,
    skip_rows, norm_rows, write_cols, read_cols, step_cols, decay_cols, skip_cols, norm_cols,
):
    grid_rows, grid_cols, features = tokens_in.shape
    blocks = grid_rows * grid_cols // BLOCK
    high = BLOCK // grid_cols
    local_cols = grid_cols // seq
    all_rows = grid_rows * seq
    per_col = all_rows // BLOCK
    inner = features * head
    heads, size = step_rows.shape[0], write_rows.shape[0]
    width = features // heads
    depth = round_up(blocks, 8)
    padded = round_up(heads, 16)
    chunks = -(-heads // CHUNK)
    dma = pltpu.SemaphoreType.DMA
    anywhere = pl.BlockSpec(memory_space=pl.ANY)
    whole = pl.BlockSpec(memory_space=pltpu.VMEM)
    smem = pl.BlockSpec(memory_space=pltpu.SMEM)
    vmem = pltpu.VMEM
    tokens = (blocks, BLOCK, features)
    packed = (seq, local_cols, blocks, high, features)
    sums = (blocks, padded, BLOCK)
    rows = (blocks, padded, LANES)
    total = (padded, LANES)
    tall = (blocks, BLOCK, padded)
    states = (heads, size, width)
    exchange = [vmem(states, BF16)] * 4 + [vmem(total, F32)]
    small = (
        decay_rows, step_rows, write_rows, read_rows, norm_rows.reshape(heads, width),
        decay_cols, step_cols, write_cols, read_cols,
    )
    raw = (all_rows, local_cols, features)
    flat = raw if local_cols > 1 else (all_rows, features)
    gate = gate_cols if local_cols > 1 else gate_cols.reshape(tokens)
    gated, scale = pl.pallas_call(
        functools.partial(fused_kernel, seq, head, inner, grid_cols, local_cols, per_col),
        out_shape=(
            jax.ShapeDtypeStruct(flat, BF16),
            jax.ShapeDtypeStruct((all_rows * local_cols, LANES), F32),
        ),
        in_specs=[smem, smem] + [anywhere] * (3 + SMALL),
        out_specs=(anywhere, whole),
        scratch_shapes=[
            vmem(tokens, BF16), vmem(tokens, BF16), vmem(tokens, BF16),
            vmem(packed, BF16), vmem(packed, BF16), vmem(tokens, BF16),
            vmem(tokens, F32), vmem((2, BLOCK, LANES), F32),
            *(vmem(array.shape, array.dtype) for array in small),
            vmem(raw if local_cols > 1 else (1, LANES), BF16), vmem(flat, BF16),
            vmem((CHUNK, all_rows * local_cols if local_cols > 1 else 8, LANES), F32),
            vmem((blocks, 3, padded, BLOCK), BF16), vmem(sums, F32), vmem(sums, F32),
            vmem(sums, F32), vmem(rows, F32), vmem(rows, F32), vmem(rows, F32), vmem(rows, F32),
            vmem(total, F32), vmem(total, F32), vmem(tall, F32), vmem(tall, F32),
            vmem((blocks, BLOCK, BLOCK), F32), vmem((blocks, BLOCK, 2 * size), BF16),
            vmem(states, F32), vmem((blocks,) + states, F32), vmem(states, F32),
            vmem((blocks, BLOCK, LANES), F32), vmem((depth, BLOCK), F32),
            vmem((head - 1, depth, BLOCK), F32), vmem((head - 1, depth, BLOCK), F32),
            vmem((depth, BLOCK), F32), vmem((seq * depth, BLOCK), F32),
            vmem((blocks, BLOCK, LANES), F32),
            *exchange, *exchange,
            dma((3, blocks)), dma((SMALL,)), dma((seq - 1, chunks)), dma((seq - 1, chunks)), dma((chunks,)),
            dma((2, head - 1)), dma((2, head - 1)), dma((seq - 1,)), dma((seq - 1,)),
            dma((chunks,)),
            dma((2, chunks)), dma((2,)), dma((2, chunks)),
            dma((2, chunks)), dma((2,)), dma((2, chunks)),
        ],
        compiler_params=pltpu.CompilerParams(
            collective_id=0, has_side_effects=True, vmem_limit_bytes=VMEM_BYTES
        ),
        name="fused",
    )(
        skip_rows, skip_cols, tokens_in.reshape(tokens), gate_rows.reshape(tokens), gate, *small
    )
    part = min(all_rows, BLOCK // local_cols // 2)
    block = (part,) + flat[1:]
    spec = pl.BlockSpec(block, lambda q: (q,) + (0,) * (len(block) - 1))
    result = pl.pallas_call(
        norm_kernel,
        grid=(all_rows // part,),
        out_shape=jax.ShapeDtypeStruct(flat, BF16),
        in_specs=[
            spec,
            pl.BlockSpec((part * local_cols, LANES), lambda q: (q, 0)),
            pl.BlockSpec((heads, width), lambda q: (0, 0)),
        ],
        out_specs=spec,
        compiler_params=pltpu.CompilerParams(vmem_limit_bytes=VMEM_BYTES),
        name="norm",
    )(gated, scale, norm_cols.reshape(heads, width))
    return result.reshape(all_rows, local_cols, features)


def solution(mesh):
    placed = (
        P("seq", None, "head"),
        P("seq", None, "head"),
        P(None, "seq", "head"),
        P(None, "seq"),
        P(None, "seq"),
        P("head", "seq"),
        P("head", "seq"),
        P("head"),
        P("head"),
        P(None, "seq"),
        P(None, "seq"),
        P("head", "seq"),
        P("head", "seq"),
        P("head"),
        P("head"),
    )
    return jax.shard_map(
        functools.partial(body, mesh.shape["seq"], mesh.shape["head"]),
        mesh=mesh, in_specs=placed, out_specs=P(None, "seq", "head"), check_vma=False,
    )
```

```python
import functools
import jax
import jax.numpy as jnp
from jax import lax
from jax.experimental import pallas as pl
from jax.experimental.pallas import tpu as pltpu
from jax.sharding import PartitionSpec as P

BLOCK = 256
HALF = 128
LANES = 128
CHUNK = 2
SMALL = 9
EPSILON = 1e-05
LOG2E = 1.4426950408889634
HIGHEST = lax.Precision.HIGHEST
MESH = pl.DeviceIdType.MESH
F32 = jnp.float32
BF16 = jnp.bfloat16
VMEM_BYTES = 60 * 1024 * 1024


def contract(a, b, dims, precision=None):
    return lax.dot_general(
        a, b, (dims, ((), ())), precision=precision, preferred_element_type=F32
    )


def iota(shape, axis):
    return lax.broadcasted_iota(jnp.int32, shape, axis)


def round_up(value, step):
    return -(-value // step) * step


def split(value, count):
    parts = []
    for _ in range(count - 1):
        part = value.astype(BF16)
        parts.append(part)
        value = value - part.astype(F32)
    parts.append(value.astype(BF16))
    return parts


def span_of(b):
    return pl.ds(pl.multiple_of(b * BLOCK, BLOCK), BLOCK)


class Layer:
    def __init__(self, **refs):
        self.__dict__.update(refs)


def prepare_sums(layer):
    heads, length = layer.decay.shape
    blocks = length // BLOCK
    padded = layer.cum.shape[1]
    layer.stage[...] = jnp.zeros_like(layer.stage)
    for p, part in enumerate(split(layer.decay[...] * LOG2E, 3)):
        for b in range(blocks):
            layer.stage[b, p, :heads] = part[:, b * BLOCK : (b + 1) * BLOCK]
    upper = (iota((BLOCK, BLOCK), 0) <= iota((BLOCK, BLOCK), 1)).astype(BF16)
    sums = contract(layer.stage[...].reshape(blocks * 3 * padded, BLOCK), upper, ((1,), (0,)))
    sums = sums.reshape(blocks, 3, padded, BLOCK)
    run = jnp.zeros((padded, 1), F32)
    for b in range(blocks):
        cum = sums[b, 0] + sums[b, 1] + sums[b, 2]
        final = cum[:, BLOCK - 1 :]
        layer.cum[b] = cum
        layer.weights[b, :heads] = (
            jnp.exp2(final[:heads] - cum[:heads]) * layer.step[:, b * BLOCK : (b + 1) * BLOCK]
        )
        layer.fades[b] = jnp.broadcast_to(jnp.exp2(final), (padded, LANES))
        layer.before[b] = jnp.broadcast_to(jnp.exp2(run), (padded, LANES))
        run = run + final
    layer.total[...] = jnp.broadcast_to(run, (padded, LANES))


def prepare_scores(layer):
    blocks = layer.cum.shape[0]
    lower = (iota((BLOCK, BLOCK), 0) >= iota((BLOCK, BLOCK), 1)).astype(F32)

    def block(b, carry):
        across = jnp.transpose(layer.cum[b])
        layer.across[b] = across
        layer.lifting[b] = jnp.exp2(across)
        read = layer.read[:, span_of(b)]
        layer.scores[b] = contract(read, layer.write[:, span_of(b)], ((0,), (0,))) * lower
        read32 = read.astype(F32)
        layer.read_t[b] = jnp.transpose(jnp.concatenate([read32, read32], axis=0)).astype(BF16)
        return carry

    lax.fori_loop(0, blocks, block, 0)


def lanes_of(h):
    return slice(h * LANES, (h + 1) * LANES)


def add_state(layer, b, h, write32, own):
    loaded = (write32 * layer.weights[b, h : h + 1, :]).astype(BF16)
    gained = contract(loaded, own, ((1,), (0,)))
    held = layer.state[h]
    layer.local[b, h] = held
    layer.state[h] = layer.fades[b, h : h + 1, :] * held + gained


def inner_block(layer, b, h, own):
    across = layer.across[b, :, h : h + 1]
    cum = layer.cum[b, h : h + 1, :]
    step = layer.step[h : h + 1, span_of(b)]
    top, low = slice(0, HALF), slice(HALF, BLOCK)

    def mix(rows, cols, diagonal):
        spread = across[rows] - cum[:, cols]
        if diagonal:
            spread = jnp.minimum(spread, 0.0)
        return (jnp.exp2(spread) * layer.scores[b, rows, cols] * step[:, cols]).astype(BF16)

    skip = layer.skip[h]
    first = contract(mix(top, top, True), own[top], ((1,), (0,)))
    layer.inner[b, top, lanes_of(h)] = first + skip * own[top].astype(F32)
    both = jnp.concatenate([mix(low, top, False), mix(low, low, True)], axis=1)
    second = contract(both, own, ((1,), (0,)))
    layer.inner[b, low, lanes_of(h)] = second + skip * own[low].astype(F32)


def finish_block(layer, b, hs, store):
    held = jnp.concatenate(
        [layer.before[b, h : h + 1, :] * layer.prior[h] + layer.local[b, h] for h in hs], axis=1
    )
    parts = jnp.concatenate(split(held, 2), axis=0)
    from_state = contract(layer.read_t[b], parts, ((1,), (0,)))
    squares = jnp.zeros((BLOCK, LANES), F32)
    for i, h in enumerate(hs):
        out = layer.inner[b, :, lanes_of(h)]
        out += layer.lifting[b, :, h : h + 1] * from_state[:, i * LANES : (i + 1) * LANES]
        gated = out * layer.silu[b, :, lanes_of(h)]
        squares += gated * gated
        store(b, h, gated)
    layer.squares[b] += squares


def silu(gate):
    gate = gate.astype(F32)
    return gate / (1.0 + jnp.exp2(gate * -LOG2E))


def reduce_squares(layer, rows_ref):
    blocks = layer.squares.shape[0]
    rows_ref[...] = jnp.zeros_like(rows_ref)
    for b in range(blocks):
        parts = jnp.concatenate(split(layer.squares[b], 2), axis=1)
        row = contract(jnp.ones((8, 2 * LANES), BF16), parts, ((1,), (1,)))
        rows_ref[b : b + 1, :] = row[:1]


def column_scale(column, grid_rows, grid_cols, scales):
    high = BLOCK // grid_cols
    shape = (BLOCK, scales.shape[0])
    row = iota(shape, 0)
    depth = scales.shape[0] * grid_rows // BLOCK
    source = (row // grid_rows) * depth + (row % grid_rows) // high
    picked = contract((iota(shape, 1) == source).astype(F32), scales, ((1,), (0,)), HIGHEST)
    lane = (iota((BLOCK, BLOCK), 0) % high) * grid_cols + column
    return jnp.sum(jnp.where(iota((BLOCK, BLOCK), 1) == lane, picked, 0.0), axis=1, keepdims=True)


def greet_signal(axes):
    barrier = pltpu.get_barrier_semaphore()
    for axis, count in axes:
        me = lax.axis_index(axis)
        for hop in range(1, count):
            pl.semaphore_signal(
                barrier, inc=1, device_id={axis: lax.rem(me + hop, count)}, device_id_type=MESH
            )


def greet_wait(axes):
    pl.semaphore_wait(
        pltpu.get_barrier_semaphore(), sum(count - 1 for _, count in axes)
    )


def head_sum(count, own_ref, held, send_sems, recv_sems):
    me = lax.axis_index("head")
    copies = []
    for hop in range(1, count):
        copy = pltpu.make_async_remote_copy(
            src_ref=own_ref,
            dst_ref=held.at[hop - 1],
            send_sem=send_sems.at[hop - 1],
            recv_sem=recv_sems.at[hop - 1],
            device_id={"head": lax.rem(me + hop, count)},
            device_id_type=MESH,
        )
        copy.start()
        copies.append(copy)
    for copy in copies:
        copy.wait()
    total = own_ref[...]
    for hop in range(1, count):
        total += held[hop - 1]
    return total


class Exchange:
    def __init__(self, seq, layer, refs, sems):
        self.layer = layer
        self.sent, self.swapped, self.passed, self.came, self.near, *refs = refs
        self.own, self.landed, self.pair_total, self.pair_totals, self.span = refs
        self.swap_sems, self.near_sems, self.pass_sems, self.own_sems, self.total_sems = sems
        self.seq, self.me = seq, lax.axis_index("seq")
        me = lax.axis_index("seq")
        self.place = lax.rem(me, 2)
        self.partner = me + 1 - 2 * self.place
        self.group = me // 2
        self.groups = seq // 2
        self.ahead = lax.rem(me + 2, seq)

    def near_copy(self):
        return pltpu.make_async_remote_copy(
            src_ref=self.layer.total, dst_ref=self.near, send_sem=self.near_sems.at[0],
            recv_sem=self.near_sems.at[1], device_id={"seq": self.partner}, device_id_type=MESH,
        )

    def swap_copy(self, c, part):
        return pltpu.make_async_remote_copy(
            src_ref=self.sent.at[part], dst_ref=self.swapped.at[part],
            send_sem=self.swap_sems.at[0, c], recv_sem=self.swap_sems.at[1, c],
            device_id={"seq": self.partner}, device_id_type=MESH,
        )

    def pass_copy(self, c, part):
        return pltpu.make_async_remote_copy(
            src_ref=self.passed.at[part], dst_ref=self.came.at[part],
            send_sem=self.pass_sems.at[0, c], recv_sem=self.pass_sems.at[1, c],
            device_id={"seq": self.ahead}, device_id_type=MESH,
        )

    def swap(self, c, part):
        for h in range(part.start, part.start + part.size):
            self.sent[h] = self.layer.state[h].astype(BF16)
        self.swap_copy(c, part).start()

    def fades(self):
        self.near_copy().wait()
        mine, other = self.layer.total[...], self.near[...]
        even = self.place == 0
        return jnp.exp2(jnp.where(even, mine, other)), jnp.exp2(jnp.where(even, other, mine))

    def step(self, c, part, fades):
        layer = self.layer
        first_fade, last_fade = fades
        even = self.place == 0
        self.swap_copy(c, part).wait()

        @pl.when(self.group > 0)
        def _():
            self.pass_copy(c, part).wait_recv()

        for h in range(part.start, part.start + part.size):
            first, last = self.pair_of(h)
            before = self.came[h].astype(F32)
            middle = first_fade[h : h + 1] * before + first
            self.passed[h] = (last_fade[h : h + 1] * middle + last).astype(BF16)
            layer.prior[h] = jnp.where(even, before, middle)

        @pl.when(self.group < self.groups - 1)
        def _():
            self.pass_copy(c, part).start()

    def own_copy(self, hop):
        return pltpu.make_async_remote_copy(
            src_ref=self.own, dst_ref=self.landed.at[hop - 1], send_sem=self.own_sems.at[0, hop - 1],
            recv_sem=self.own_sems.at[1, hop - 1],
            device_id={"seq": lax.rem(self.me + 2 * hop, self.seq)}, device_id_type=MESH,
        )

    def total_copy(self, hop):
        return pltpu.make_async_remote_copy(
            src_ref=self.pair_total, dst_ref=self.pair_totals.at[hop - 1],
            send_sem=self.total_sems.at[0, hop - 1], recv_sem=self.total_sems.at[1, hop - 1],
            device_id={"seq": lax.rem(self.me + 2 * hop, self.seq)}, device_id_type=MESH,
        )

    def announce(self):
        self.pair_total[...] = self.layer.total[...] + self.near[...]
        for hop in range(1, self.groups):

            @pl.when(self.group + hop < self.groups)
            def _(hop=hop):
                self.total_copy(hop).start()

    def pair_of(self, h):
        mine, other = self.layer.state[h], self.swapped[h].astype(F32)
        even = self.place == 0
        return jnp.where(even, mine, other), jnp.where(even, other, mine)

    def send_own(self, c, part, fades):
        self.swap_copy(c, part).wait()
        for i, h in enumerate(range(part.start, part.start + part.size)):
            first, last = self.pair_of(h)
            self.own[i] = (fades[1][h : h + 1] * first + last).astype(BF16)
        for hop in range(1, self.groups):

            @pl.when(self.group + hop < self.groups)
            def _(hop=hop):
                self.own_copy(hop).start()

    def take_own(self, part, fades):
        prior = self.layer.prior
        heads = range(part.start, part.start + part.size)
        self.span[...] = jnp.zeros_like(self.span)
        for h in heads:
            prior[h] = jnp.zeros(prior.shape[1:], F32)
        for hop in range(1, self.groups):

            @pl.when(self.group >= hop)
            def _(hop=hop):
                self.total_copy(hop).wait_recv()
                self.own_copy(hop).wait_recv()
                factor = jnp.exp2(self.span[...])
                for i, h in enumerate(heads):
                    prior[h] += factor[h : h + 1] * self.landed[hop - 1, i].astype(F32)
                self.span[...] += self.pair_totals[hop - 1]

        for h in heads:
            before = prior[h]
            middle = fades[0][h : h + 1] * before + self.pair_of(h)[0]
            prior[h] = jnp.where(self.place == 0, before, middle)

    def settle(self, parts):
        for c, part in parts:

            @pl.when(self.group < self.groups - 1)
            def _(c=c, part=part):
                self.pass_copy(c, part).wait_send()

        for hop in range(1, self.groups):

            @pl.when(self.group + hop < self.groups)
            def _(hop=hop):
                self.total_copy(hop).wait_send()
                self.own_copy(hop).wait_send()


def fused_kernel(
    seq, head_count, inner, grid_cols, local_cols, per_col,
    skip1, skip2, x_hbm, gate1_hbm, gate2_hbm, *refs
):
    small_hbm, refs = refs[:SMALL], refs[SMALL:]
    out_hbm, scale_ref, x, gate1, gate2, sendbuf, recvbuf, hidden, innerbuf, turned, *refs = refs
    small, refs = refs[:SMALL], refs[SMALL:]
    decay1, step1, write1, read1, gain1, decay2, step2, write2, read2 = small
    (
        gate_raw, flat, woven, silus,
    stage, cum1, cum2, weights, fades1, fades2, before1, before2, total1, total2, across, lifting,
    scores, read_t, state, local, prior, squares, rows1, held1, held2, scale, scales, column,
    *refs,
    ) = refs
    ex1_refs, ex2_refs, refs = refs[:10], refs[10:20], refs[20:]
    (
        load_sems, small_sems, bulk_send, bulk_recv, keep_sems, sum1, sum2, scale_send, scale_recv,
        out_sems, *refs,
    ) = refs
    ex1_sems, ex2_sems = refs[:5], refs[5:]
    axes = (("seq", seq), ("head", head_count))
    me = lax.axis_index("seq")
    blocks, _, features = x.shape
    heads = features // LANES
    high = BLOCK // grid_cols
    grid_rows = blocks * high
    slabs = BLOCK // grid_rows
    parts = [pl.ds(c, min(CHUNK, heads - c)) for c in range(0, heads, CHUNK)]
    numbers = [range(part.start, part.start + part.size) for part in parts]
    chunks = len(parts)
    greet_signal(axes)

    def load(b):
        return pltpu.make_async_copy(x_hbm.at[b], x.at[b], load_sems.at[0, b])

    gate_loads = [
        pltpu.make_async_copy(gate1_hbm, gate1, load_sems.at[1, 0]),
        pltpu.make_async_copy(
            gate2_hbm, gate_raw if local_cols > 1 else gate2, load_sems.at[2, 0]
        ),
    ]
    small_loads = [
        pltpu.make_async_copy(source, target, small_sems.at[i])
        for i, (source, target) in enumerate(zip(small_hbm, small))
    ]
    for copy in small_loads[:3]:
        copy.start()
    for b in range(blocks):
        load(b).start()
    for copy in small_loads[3:] + gate_loads:
        copy.start()

    shared = dict(
        stage=stage, weights=weights, across=across, lifting=lifting, scores=scores,
        read_t=read_t, state=state, local=local, prior=prior, squares=squares, inner=innerbuf,
        silu=silus,
    )
    one = Layer(
        skip=skip1, write=write1, read=read1, step=step1, decay=decay1, cum=cum1,
        fades=fades1, before=before1, total=total1, **shared,
    )
    two = Layer(
        skip=skip2, write=write2, read=read2, step=step2, decay=decay2, cum=cum2,
        fades=fades2, before=before2, total=total2, **shared,
    )
    ex1 = Exchange(seq, one, ex1_refs, ex1_sems)
    ex2 = Exchange(seq, two, ex2_refs, ex2_sems)

    @pl.when(ex1.group == 0)
    def _():
        ex1.came[...] = jnp.zeros_like(ex1.came)
        ex2.came[...] = jnp.zeros_like(ex2.came)

    for copy in small_loads[:2]:
        copy.wait()
    prepare_sums(one)
    small_loads[2].wait()
    state[...] = jnp.zeros_like(state)

    def states1(b, carry):
        load(b).wait()
        write32 = write1[:, span_of(b)].astype(F32)
        for h in range(heads):
            add_state(one, b, h, write32, x[b, :, lanes_of(h)])
        return carry

    lax.fori_loop(0, blocks, states1, 0)
    greet_wait(axes)
    ex1.near_copy().start()
    for c, part in enumerate(parts):
        ex1.swap(c, part)
    fades = ex1.fades()
    ex1.announce()
    ex1.send_own(0, parts[0], fades)

    small_loads[3].wait()
    prepare_scores(one)
    squares[...] = jnp.zeros_like(squares)

    def inner1(c):
        def block(b, carry):
            for h in numbers[c]:
                inner_block(one, b, h, x[b, :, lanes_of(h)])
                silus[b, :, lanes_of(h)] = silu(gate1[b, :, lanes_of(h)])
            return carry

        lax.fori_loop(0, blocks, block, 0)

    def store1(b, h, gated):
        slot = turned.at[h % 2]
        slot[...] = gated
        for col in range(grid_cols):
            sendbuf[col // local_cols, col % local_cols, b, :, lanes_of(h)] = slot[
                pl.ds(col, high, stride=grid_cols), :
            ].astype(BF16)

    def finish1(c):
        def block(b, carry):
            finish_block(one, b, numbers[c], store1)
            return carry

        lax.fori_loop(0, blocks, block, 0)

    def wide(c):
        return pl.ds(parts[c].start * LANES, parts[c].size * LANES)

    def bulk(c, hop):
        to = lax.rem(me - hop + seq, seq)
        return pltpu.make_async_remote_copy(
            src_ref=sendbuf.at[to, :, :, :, wide(c)],
            dst_ref=recvbuf.at[me, :, :, :, wide(c)],
            send_sem=bulk_send.at[hop - 1, c],
            recv_sem=bulk_recv.at[hop - 1, c],
            device_id={"seq": to},
            device_id_type=MESH,
        )

    def keep(c):
        return pltpu.make_async_copy(
            sendbuf.at[me, :, :, :, wide(c)], recvbuf.at[me, :, :, :, wide(c)], keep_sems.at[c]
        )

    def send_all(c):
        for hop in range(1, seq):
            bulk(c, hop).start()
        keep(c).start()

    gate_loads[0].wait()
    inner1(0)
    ex1.take_own(parts[0], fades)
    finish1(0)
    for hop in range(1, seq):

        @pl.when(hop <= me)
        def _(hop=hop):
            bulk(0, hop).start()

    soon = ex1.group < ex1.groups // 2

    @pl.when(soon)
    def _():
        for c in range(1, chunks):
            ex1.step(c, parts[c], fades)

    for hop in range(1, seq):

        @pl.when(hop > me)
        def _(hop=hop):
            bulk(0, hop).start()

    keep(0).start()
    for c in range(1, chunks):
        inner1(c)

        @pl.when(jnp.logical_not(soon))
        def _(c=c):
            ex1.step(c, parts[c], fades)

        finish1(c)
        if c == 1:
            send_all(c)
    reduce_squares(one, rows1)
    scale[...] = lax.rsqrt(head_sum(head_count, rows1, held1, sum1.at[0], sum1.at[1]) / inner + EPSILON)
    depth = scale.shape[0]
    mine = pl.ds(pl.multiple_of(me * depth, depth), depth)
    scale_copies = []
    for hop in range(1, seq):
        copy = pltpu.make_async_remote_copy(
            src_ref=scale,
            dst_ref=scales.at[mine],
            send_sem=scale_send.at[hop - 1],
            recv_sem=scale_recv.at[hop - 1],
            device_id={"seq": lax.rem(me - hop + seq, seq)},
            device_id_type=MESH,
        )
        copy.start()
        scale_copies.append(copy)
    for c in range(2, chunks):
        send_all(c)
    scales[mine, :] = scale[...]

    for copy in small_loads[4:]:
        copy.wait()
    prepare_sums(two)
    prepare_scores(two)
    state[...] = jnp.zeros_like(state)
    squares[...] = jnp.zeros_like(squares)
    ex2.near_copy().start()
    ex2_fades = ex2.fades()
    ex2.announce()
    gate_loads[1].wait()
    all_rows = per_col * BLOCK

    def place_of(b):
        return pl.ds(lax.rem(b, per_col) * (BLOCK * local_cols) + b // per_col, BLOCK, stride=local_cols)

    if local_cols > 1:
        for h in range(heads):
            slot = woven.at[h % 2]
            slot[...] = gate_raw[:, :, lanes_of(h)].astype(F32).reshape(all_rows * local_cols, LANES)
            for b in range(blocks):
                at = (b % per_col) * BLOCK * local_cols + b // per_col
                silus[b, :, lanes_of(h)] = silu(slot[pl.ds(at, BLOCK, stride=local_cols), :])
    else:
        for h in range(heads):
            for b in range(blocks):
                silus[b, :, lanes_of(h)] = silu(gate2[b, :, lanes_of(h)])
    for copy in scale_copies:
        copy.wait()

    def columns(b, carry):
        window = pl.ds(
            pl.multiple_of(lax.rem(b, per_col) * slabs * depth, slabs * depth), slabs * depth
        )
        picked = column_scale(me * local_cols + b // per_col, grid_rows, grid_cols, scales[window, :])
        column[b] = jnp.broadcast_to(picked, (BLOCK, LANES))
        return carry

    lax.fori_loop(0, blocks, columns, 0)

    def arrive(c):
        keep(c).wait()
        for hop in range(1, seq):
            bulk(c, hop).wait()

    def states2(c):
        def block(b, carry):
            write32 = write2[:, span_of(b)].astype(F32)
            slab = pl.ds(lax.rem(b, per_col) * slabs, slabs)
            for h in numbers[c]:
                lanes = lanes_of(h)
                own = recvbuf[slab, b // per_col, :, :, lanes].astype(F32).reshape(BLOCK, LANES)
                own = (own * column[b] * gain1[h : h + 1, :]).astype(BF16)
                hidden[b, :, lanes] = own
                add_state(two, b, h, write32, own)
            return carry

        lax.fori_loop(0, blocks, block, 0)

    def inner2(c):
        def block(b, carry):
            for h in numbers[c]:
                inner_block(two, b, h, hidden[b, :, lanes_of(h)])
            return carry

        lax.fori_loop(0, blocks, block, 0)

    def store2(b, h, gated):
        flat[h, place_of(b), :] = gated

    def put(c):
        return pltpu.make_async_copy(flat.at[parts[c]], out_hbm.at[parts[c]], out_sems.at[c])

    def finish2(c):
        def block(b, carry):
            finish_block(two, b, numbers[c], store2)
            return carry

        lax.fori_loop(0, blocks, block, 0)
        put(c).start()

    last = chunks - 1
    fades = ex2_fades

    def chain(slot):
        for late in range(2):
            c = slot - 1 - late
            if 0 <= c < last:

                @pl.when(soon & (jnp.minimum(ex2.group, 1) == late))
                def _(c=c):
                    ex2.step(c, parts[c], fades)

    for c in range(chunks):
        if c == last:
            chain(last)
            chain(last + 1)

            @pl.when(soon)
            def _():
                for e in range(last - 1):
                    finish2(e)

        arrive(c)
        states2(c)
        ex2.swap(c, parts[c])
        inner2(c)
        if c < last:
            chain(c)
    ex2.send_own(last, parts[last], fades)

    @pl.when(jnp.logical_not(soon))
    def _():
        for e in range(last):
            ex2.step(e, parts[e], fades)
        for e in range(last - 1):
            finish2(e)

    if last > 0:
        finish2(last - 1)
    ex2.take_own(parts[last], fades)
    finish2(last)
    reduce_squares(two, rows1)
    total = head_sum(head_count, rows1, held2, sum2.at[0], sum2.at[1])
    total = jnp.transpose(lax.rsqrt(total / inner + EPSILON))
    for b in range(blocks):
        at = (b % per_col) * BLOCK * local_cols + b // per_col
        scale_ref[pl.ds(at, BLOCK, stride=local_cols), :] = jnp.broadcast_to(
            total[:, b : b + 1], (BLOCK, LANES)
        )
    for c in range(chunks):
        put(c).wait()
    numbered = list(enumerate(parts))
    ex1.settle(numbered[1:])
    ex2.settle(numbered[:-1])


def norm_kernel(steps, gated_hbm, scale_hbm, gain_ref, out_hbm, gated, scale, out, load_sems, out_sems):
    heads, rows, _ = gated.shape
    part = rows // steps
    tall = out.shape[0] // steps
    loads = [
        pltpu.make_async_copy(scale_hbm, scale, load_sems.at[steps]),
        *(
            pltpu.make_async_copy(
                gated_hbm.at[:, pl.ds(i * part, part)], gated.at[:, pl.ds(i * part, part)],
                load_sems.at[i],
            )
            for i in range(steps)
        ),
    ]
    puts = [
        pltpu.make_async_copy(
            out.at[pl.ds(i * tall, tall)], out_hbm.at[pl.ds(i * tall, tall)], out_sems.at[i]
        )
        for i in range(steps)
    ]
    for copy in loads:
        copy.start()
    loads[0].wait()
    for i in range(steps):
        loads[i + 1].wait()
        span = pl.ds(i * part, part)
        for h in range(heads):
            lanes = lanes_of(h)
            result = gated[h, span, :] * scale[span, :] * gain_ref[h : h + 1, :]
            shape = (tall,) + out.shape[1:-1] + (LANES,)
            out[pl.ds(i * tall, tall), ..., lanes] = result.reshape(shape).astype(BF16)
        puts[i].start()
    for copy in puts:
        copy.wait()


def body(
    seq, head, tokens_in, gate_rows, gate_cols, write_rows, read_rows, step_rows, decay_rows,
    skip_rows, norm_rows, write_cols, read_cols, step_cols, decay_cols, skip_cols, norm_cols,
):
    grid_rows, grid_cols, features = tokens_in.shape
    blocks = grid_rows * grid_cols // BLOCK
    high = BLOCK // grid_cols
    local_cols = grid_cols // seq
    all_rows = grid_rows * seq
    per_col = all_rows // BLOCK
    inner = features * head
    heads, size = step_rows.shape[0], write_rows.shape[0]
    width = features // heads
    depth = round_up(blocks, 8)
    padded = round_up(heads, 16)
    chunks = -(-heads // CHUNK)
    dma = pltpu.SemaphoreType.DMA
    anywhere = pl.BlockSpec(memory_space=pl.ANY)
    whole = pl.BlockSpec(memory_space=pltpu.VMEM)
    smem = pl.BlockSpec(memory_space=pltpu.SMEM)
    vmem = pltpu.VMEM
    tokens = (blocks, BLOCK, features)
    packed = (seq, local_cols, blocks, high, features)
    sums = (blocks, padded, BLOCK)
    rows = (blocks, padded, LANES)
    total = (padded, LANES)
    tall = (blocks, BLOCK, padded)
    states = (heads, size, width)
    groups = seq // 2
    held = (min(CHUNK, heads), size, width)
    far = max(groups - 1, 1)
    exchange = [vmem(states, BF16)] * 4 + [
        vmem(total, F32), vmem(held, BF16), vmem((far,) + held, BF16), vmem(total, F32),
        vmem((far,) + total, F32), vmem(total, F32),
    ]
    exchange_sems = [dma((2, chunks)), dma((2,)), dma((2, chunks)), dma((2, far)), dma((2, far))]
    small = (
        decay_rows, step_rows, write_rows, read_rows, norm_rows.reshape(heads, width),
        decay_cols, step_cols, write_cols, read_cols,
    )
    raw = (all_rows, local_cols, features)
    flat = raw if local_cols > 1 else (all_rows, features)
    gate = gate_cols if local_cols > 1 else gate_cols.reshape(tokens)
    gated, scale = pl.pallas_call(
        functools.partial(fused_kernel, seq, head, inner, grid_cols, local_cols, per_col),
        out_shape=(
            jax.ShapeDtypeStruct((heads, all_rows * local_cols, LANES), F32),
            jax.ShapeDtypeStruct((all_rows * local_cols, LANES), F32),
        ),
        in_specs=[smem, smem] + [anywhere] * (3 + SMALL),
        out_specs=(anywhere, whole),
        scratch_shapes=[
            vmem(tokens, BF16), vmem(tokens, BF16),
            vmem(tokens if local_cols == 1 else (1, BLOCK, LANES), BF16),
            vmem(packed, BF16), vmem(packed, BF16), vmem(tokens, BF16),
            vmem(tokens, F32), vmem((2, BLOCK, LANES), F32),
            *(vmem(array.shape, array.dtype) for array in small),
            vmem(raw if local_cols > 1 else (1, LANES), BF16),
            vmem((heads, all_rows * local_cols, LANES), F32),
            vmem((2, all_rows * local_cols if local_cols > 1 else 8, LANES), F32),
            vmem(tokens, F32),
            vmem((blocks, 3, padded, BLOCK), BF16), vmem(sums, F32), vmem(sums, F32),
            vmem(sums, F32), vmem(rows, F32), vmem(rows, F32), vmem(rows, F32), vmem(rows, F32),
            vmem(total, F32), vmem(total, F32), vmem(tall, F32), vmem(tall, F32),
            vmem((blocks, BLOCK, BLOCK), F32), vmem((blocks, BLOCK, 2 * size), BF16),
            vmem(states, F32), vmem((blocks,) + states, F32), vmem(states, F32),
            vmem((blocks, BLOCK, LANES), F32), vmem((depth, BLOCK), F32),
            vmem((head - 1, depth, BLOCK), F32), vmem((head - 1, depth, BLOCK), F32),
            vmem((depth, BLOCK), F32), vmem((seq * depth, BLOCK), F32),
            vmem((blocks, BLOCK, LANES), F32),
            *exchange, *exchange,
            dma((3, blocks)), dma((SMALL,)), dma((seq - 1, chunks)), dma((seq - 1, chunks)), dma((chunks,)),
            dma((2, head - 1)), dma((2, head - 1)), dma((seq - 1,)), dma((seq - 1,)),
            dma((chunks,)),
            *exchange_sems, *exchange_sems,
        ],
        compiler_params=pltpu.CompilerParams(
            collective_id=0, has_side_effects=True, vmem_limit_bytes=VMEM_BYTES
        ),
        name="fused",
    )(
        skip_rows, skip_cols, tokens_in.reshape(tokens), gate_rows.reshape(tokens), gate, *small
    )
    steps = 8
    result = pl.pallas_call(
        functools.partial(norm_kernel, steps),
        out_shape=jax.ShapeDtypeStruct(flat, BF16),
        in_specs=[anywhere, anywhere, whole],
        out_specs=anywhere,
        scratch_shapes=[
            vmem(gated.shape, F32), vmem(scale.shape, F32), vmem(flat, BF16),
            dma((steps + 1,)), dma((steps,)),
        ],
        compiler_params=pltpu.CompilerParams(vmem_limit_bytes=VMEM_BYTES),
        name="norm",
    )(gated, scale, norm_cols.reshape(heads, width))
    return result.reshape(all_rows, local_cols, features)


def solution(mesh):
    placed = (
        P("seq", None, "head"),
        P("seq", None, "head"),
        P(None, "seq", "head"),
        P(None, "seq"),
        P(None, "seq"),
        P("head", "seq"),
        P("head", "seq"),
        P("head"),
        P("head"),
        P(None, "seq"),
        P(None, "seq"),
        P("head", "seq"),
        P("head", "seq"),
        P("head"),
        P("head"),
    )
    return jax.shard_map(
        functools.partial(body, mesh.shape["seq"], mesh.shape["head"]),
        mesh=mesh, in_specs=placed, out_specs=P(None, "seq", "head"), check_vma=False,
    )
```

```python
import functools
import jax
import jax.numpy as jnp
from jax import lax
from jax.experimental import pallas as pl
from jax.experimental.pallas import tpu as pltpu
from jax.sharding import PartitionSpec as P

BLOCK = 256
HALF = 128
LANES = 128
CHUNK = 2
SMALL = 9
EPSILON = 1e-05
LOG2E = 1.4426950408889634
HIGHEST = lax.Precision.HIGHEST
MESH = pl.DeviceIdType.MESH
F32 = jnp.float32
BF16 = jnp.bfloat16
VMEM_BYTES = 60 * 1024 * 1024


def contract(a, b, dims, precision=None):
    return lax.dot_general(
        a, b, (dims, ((), ())), precision=precision, preferred_element_type=F32
    )


def iota(shape, axis):
    return lax.broadcasted_iota(jnp.int32, shape, axis)


def round_up(value, step):
    return -(-value // step) * step


def split(value, count):
    parts = []
    for _ in range(count - 1):
        part = value.astype(BF16)
        parts.append(part)
        value = value - part.astype(F32)
    parts.append(value.astype(BF16))
    return parts


def span_of(b):
    return pl.ds(pl.multiple_of(b * BLOCK, BLOCK), BLOCK)


class Layer:
    def __init__(self, **refs):
        self.__dict__.update(refs)


def prepare_sums(layer):
    heads, length = layer.decay.shape
    blocks = length // BLOCK
    padded = layer.cum.shape[1]
    layer.stage[...] = jnp.zeros_like(layer.stage)
    for p, part in enumerate(split(layer.decay[...] * LOG2E, 3)):
        for b in range(blocks):
            layer.stage[b, p, :heads] = part[:, b * BLOCK : (b + 1) * BLOCK]
    upper = (iota((BLOCK, BLOCK), 0) <= iota((BLOCK, BLOCK), 1)).astype(BF16)
    sums = contract(layer.stage[...].reshape(blocks * 3 * padded, BLOCK), upper, ((1,), (0,)))
    sums = sums.reshape(blocks, 3, padded, BLOCK)
    run = jnp.zeros((padded, 1), F32)
    for b in range(blocks):
        cum = sums[b, 0] + sums[b, 1] + sums[b, 2]
        final = cum[:, BLOCK - 1 :]
        layer.cum[b] = cum
        layer.weights[b, :heads] = (
            jnp.exp2(final[:heads] - cum[:heads]) * layer.step[:, b * BLOCK : (b + 1) * BLOCK]
        )
        layer.fades[b] = jnp.broadcast_to(jnp.exp2(final), (padded, LANES))
        layer.before[b] = jnp.broadcast_to(jnp.exp2(run), (padded, LANES))
        run = run + final
    layer.total[...] = jnp.broadcast_to(run, (padded, LANES))


def prepare_scores(layer):
    blocks = layer.cum.shape[0]
    lower = (iota((BLOCK, BLOCK), 0) >= iota((BLOCK, BLOCK), 1)).astype(F32)

    def block(b, carry):
        across = jnp.transpose(layer.cum[b])
        layer.across[b] = across
        layer.lifting[b] = jnp.exp2(across)
        read = layer.read[:, span_of(b)]
        layer.scores[b] = contract(read, layer.write[:, span_of(b)], ((0,), (0,))) * lower
        read32 = read.astype(F32)
        layer.read_t[b] = jnp.transpose(jnp.concatenate([read32, read32], axis=0)).astype(BF16)
        return carry

    lax.fori_loop(0, blocks, block, 0)


def lanes_of(h):
    return slice(h * LANES, (h + 1) * LANES)


def add_state(layer, b, h, write32, own):
    loaded = (write32 * layer.weights[b, h : h + 1, :]).astype(BF16)
    gained = contract(loaded, own, ((1,), (0,)))
    held = layer.state[h]
    layer.local[b, h] = held
    layer.state[h] = layer.fades[b, h : h + 1, :] * held + gained


def inner_block(layer, b, h, own):
    across = layer.across[b, :, h : h + 1]
    cum = layer.cum[b, h : h + 1, :]
    step = layer.step[h : h + 1, span_of(b)]
    top, low = slice(0, HALF), slice(HALF, BLOCK)

    def mix(rows, cols, diagonal):
        spread = across[rows] - cum[:, cols]
        if diagonal:
            spread = jnp.minimum(spread, 0.0)
        return (jnp.exp2(spread) * layer.scores[b, rows, cols] * step[:, cols]).astype(BF16)

    skip = layer.skip[h]
    first = contract(mix(top, top, True), own[top], ((1,), (0,)))
    layer.inner[b, top, lanes_of(h)] = first + skip * own[top].astype(F32)
    both = jnp.concatenate([mix(low, top, False), mix(low, low, True)], axis=1)
    second = contract(both, own, ((1,), (0,)))
    layer.inner[b, low, lanes_of(h)] = second + skip * own[low].astype(F32)


def finish_block(layer, b, hs, store):
    held = jnp.concatenate(
        [layer.before[b, h : h + 1, :] * layer.prior[h] + layer.local[b, h] for h in hs], axis=1
    )
    parts = jnp.concatenate(split(held, 2), axis=0)
    from_state = contract(layer.read_t[b], parts, ((1,), (0,)))
    squares = jnp.zeros((BLOCK, LANES), F32)
    for i, h in enumerate(hs):
        out = layer.inner[b, :, lanes_of(h)]
        out += layer.lifting[b, :, h : h + 1] * from_state[:, i * LANES : (i + 1) * LANES]
        gated = out * layer.silu[b, :, lanes_of(h)]
        squares += gated * gated
        store(b, h, gated)
    layer.squares[b] += squares


def silu(gate):
    gate = gate.astype(F32)
    return gate / (1.0 + jnp.exp2(gate * -LOG2E))


def reduce_squares(layer, rows_ref):
    blocks = layer.squares.shape[0]
    rows_ref[...] = jnp.zeros_like(rows_ref)
    for b in range(blocks):
        parts = jnp.concatenate(split(layer.squares[b], 2), axis=1)
        row = contract(jnp.ones((8, 2 * LANES), BF16), parts, ((1,), (1,)))
        rows_ref[b : b + 1, :] = row[:1]


def column_scale(column, grid_rows, grid_cols, scales):
    high = BLOCK // grid_cols
    shape = (BLOCK, scales.shape[0])
    row = iota(shape, 0)
    depth = scales.shape[0] * grid_rows // BLOCK
    source = (row // grid_rows) * depth + (row % grid_rows) // high
    picked = contract((iota(shape, 1) == source).astype(F32), scales, ((1,), (0,)), HIGHEST)
    lane = (iota((BLOCK, BLOCK), 0) % high) * grid_cols + column
    return jnp.sum(jnp.where(iota((BLOCK, BLOCK), 1) == lane, picked, 0.0), axis=1, keepdims=True)


def greet_signal(axes):
    barrier = pltpu.get_barrier_semaphore()
    for axis, count in axes:
        me = lax.axis_index(axis)
        for hop in range(1, count):
            pl.semaphore_signal(
                barrier, inc=1, device_id={axis: lax.rem(me + hop, count)}, device_id_type=MESH
            )


def greet_wait(axes):
    pl.semaphore_wait(
        pltpu.get_barrier_semaphore(), sum(count - 1 for _, count in axes)
    )


def head_sum(count, own_ref, held, send_sems, recv_sems):
    me = lax.axis_index("head")
    copies = []
    for hop in range(1, count):
        copy = pltpu.make_async_remote_copy(
            src_ref=own_ref,
            dst_ref=held.at[hop - 1],
            send_sem=send_sems.at[hop - 1],
            recv_sem=recv_sems.at[hop - 1],
            device_id={"head": lax.rem(me + hop, count)},
            device_id_type=MESH,
        )
        copy.start()
        copies.append(copy)
    for copy in copies:
        copy.wait()
    total = own_ref[...]
    for hop in range(1, count):
        total += held[hop - 1]
    return total


class Exchange:
    def __init__(self, seq, layer, refs, sems):
        self.layer = layer
        self.sent, self.swapped, self.passed, self.came, self.near, *refs = refs
        self.own, self.landed, self.pair_total, self.pair_totals, self.span = refs
        self.swap_sems, self.near_sems, self.pass_sems, self.own_sems, self.total_sems = sems
        self.seq, self.me = seq, lax.axis_index("seq")
        me = lax.axis_index("seq")
        self.place = lax.rem(me, 2)
        self.partner = me + 1 - 2 * self.place
        self.group = me // 2
        self.groups = seq // 2
        self.ahead = lax.rem(me + 2, seq)

    def near_copy(self):
        return pltpu.make_async_remote_copy(
            src_ref=self.layer.total, dst_ref=self.near, send_sem=self.near_sems.at[0],
            recv_sem=self.near_sems.at[1], device_id={"seq": self.partner}, device_id_type=MESH,
        )

    def swap_copy(self, c, part):
        return pltpu.make_async_remote_copy(
            src_ref=self.sent.at[part], dst_ref=self.swapped.at[part],
            send_sem=self.swap_sems.at[0, c], recv_sem=self.swap_sems.at[1, c],
            device_id={"seq": self.partner}, device_id_type=MESH,
        )

    def pass_copy(self, c, part):
        return pltpu.make_async_remote_copy(
            src_ref=self.passed.at[part], dst_ref=self.came.at[part],
            send_sem=self.pass_sems.at[0, c], recv_sem=self.pass_sems.at[1, c],
            device_id={"seq": self.ahead}, device_id_type=MESH,
        )

    def swap(self, c, part):
        for h in range(part.start, part.start + part.size):
            self.sent[h] = self.layer.state[h].astype(BF16)
        self.swap_copy(c, part).start()

    def fades(self):
        self.near_copy().wait()
        mine, other = self.layer.total[...], self.near[...]
        even = self.place == 0
        return jnp.exp2(jnp.where(even, mine, other)), jnp.exp2(jnp.where(even, other, mine))

    def step(self, c, part, fades):
        layer = self.layer
        first_fade, last_fade = fades
        even = self.place == 0
        self.swap_copy(c, part).wait()

        @pl.when(self.group > 0)
        def _():
            self.pass_copy(c, part).wait_recv()

        for h in range(part.start, part.start + part.size):
            first, last = self.pair_of(h)
            before = self.came[h].astype(F32)
            middle = first_fade[h : h + 1] * before + first
            self.passed[h] = (last_fade[h : h + 1] * middle + last).astype(BF16)
            layer.prior[h] = jnp.where(even, before, middle)

        @pl.when(self.group < self.groups - 1)
        def _():
            self.pass_copy(c, part).start()

    def own_copy(self, hop):
        return pltpu.make_async_remote_copy(
            src_ref=self.own, dst_ref=self.landed.at[hop - 1], send_sem=self.own_sems.at[0, hop - 1],
            recv_sem=self.own_sems.at[1, hop - 1],
            device_id={"seq": lax.rem(self.me + 2 * hop, self.seq)}, device_id_type=MESH,
        )

    def total_copy(self, hop):
        return pltpu.make_async_remote_copy(
            src_ref=self.pair_total, dst_ref=self.pair_totals.at[hop - 1],
            send_sem=self.total_sems.at[0, hop - 1], recv_sem=self.total_sems.at[1, hop - 1],
            device_id={"seq": lax.rem(self.me + 2 * hop, self.seq)}, device_id_type=MESH,
        )

    def announce(self):
        self.pair_total[...] = self.layer.total[...] + self.near[...]
        for hop in range(1, self.groups):

            @pl.when(self.group + hop < self.groups)
            def _(hop=hop):
                self.total_copy(hop).start()

    def pair_of(self, h):
        mine, other = self.layer.state[h], self.swapped[h].astype(F32)
        even = self.place == 0
        return jnp.where(even, mine, other), jnp.where(even, other, mine)

    def send_own(self, c, part, fades):
        self.swap_copy(c, part).wait()
        for i, h in enumerate(range(part.start, part.start + part.size)):
            first, last = self.pair_of(h)
            self.own[i] = (fades[1][h : h + 1] * first + last).astype(BF16)
        for hop in range(1, self.groups):

            @pl.when(self.group + hop < self.groups)
            def _(hop=hop):
                self.own_copy(hop).start()

    def take_own(self, part, fades):
        prior = self.layer.prior
        heads = range(part.start, part.start + part.size)
        self.span[...] = jnp.zeros_like(self.span)
        for h in heads:
            prior[h] = jnp.zeros(prior.shape[1:], F32)
        for hop in range(1, self.groups):

            @pl.when(self.group >= hop)
            def _(hop=hop):
                self.total_copy(hop).wait_recv()
                self.own_copy(hop).wait_recv()
                factor = jnp.exp2(self.span[...])
                for i, h in enumerate(heads):
                    prior[h] += factor[h : h + 1] * self.landed[hop - 1, i].astype(F32)
                self.span[...] += self.pair_totals[hop - 1]

        for h in heads:
            before = prior[h]
            middle = fades[0][h : h + 1] * before + self.pair_of(h)[0]
            prior[h] = jnp.where(self.place == 0, before, middle)

    def settle(self, parts):
        for c, part in parts:

            @pl.when(self.group < self.groups - 1)
            def _(c=c, part=part):
                self.pass_copy(c, part).wait_send()

        for hop in range(1, self.groups):

            @pl.when(self.group + hop < self.groups)
            def _(hop=hop):
                self.total_copy(hop).wait_send()
                self.own_copy(hop).wait_send()


def fused_kernel(
    seq, head_count, inner, grid_cols, local_cols, per_col,
    skip1, skip2, x_hbm, gate1_hbm, gate2_hbm, *refs
):
    small_hbm, refs = refs[:SMALL], refs[SMALL:]
    out_hbm, scale_ref, x, gate1, gate2, sendbuf, recvbuf, hidden, innerbuf, turned, *refs = refs
    small, refs = refs[:SMALL], refs[SMALL:]
    decay1, step1, write1, read1, gain1, decay2, step2, write2, read2 = small
    (
        gate_raw, flat, woven, silus,
    stage, cum1, cum2, weights, fades1, fades2, before1, before2, total1, total2, across, lifting,
    scores, read_t, state, local, prior, squares, rows1, held1, held2, scale, scales, column,
    *refs,
    ) = refs
    ex1_refs, ex2_refs, refs = refs[:10], refs[10:20], refs[20:]
    (
        load_sems, small_sems, bulk_send, bulk_recv, keep_sems, sum1, sum2, scale_send, scale_recv,
        out_sems, *refs,
    ) = refs
    ex1_sems, ex2_sems = refs[:5], refs[5:]
    axes = (("seq", seq), ("head", head_count))
    me = lax.axis_index("seq")
    blocks, _, features = x.shape
    heads = features // LANES
    high = BLOCK // grid_cols
    grid_rows = blocks * high
    slabs = BLOCK // grid_rows
    parts = [pl.ds(c, min(CHUNK, heads - c)) for c in range(0, heads, CHUNK)]
    numbers = [range(part.start, part.start + part.size) for part in parts]
    chunks = len(parts)
    greet_signal(axes)

    def load(b):
        return pltpu.make_async_copy(x_hbm.at[b], x.at[b], load_sems.at[0, b])

    gate_loads = [
        pltpu.make_async_copy(gate1_hbm, gate1, load_sems.at[1, 0]),
        pltpu.make_async_copy(
            gate2_hbm, gate_raw if local_cols > 1 else gate2, load_sems.at[2, 0]
        ),
    ]
    small_loads = [
        pltpu.make_async_copy(source, target, small_sems.at[i])
        for i, (source, target) in enumerate(zip(small_hbm, small))
    ]
    for copy in small_loads[:3]:
        copy.start()
    for b in range(blocks):
        load(b).start()
    for copy in small_loads[3:] + gate_loads:
        copy.start()

    shared = dict(
        stage=stage, weights=weights, across=across, lifting=lifting, scores=scores,
        read_t=read_t, state=state, local=local, prior=prior, squares=squares, inner=innerbuf,
        silu=silus,
    )
    one = Layer(
        skip=skip1, write=write1, read=read1, step=step1, decay=decay1, cum=cum1,
        fades=fades1, before=before1, total=total1, **shared,
    )
    two = Layer(
        skip=skip2, write=write2, read=read2, step=step2, decay=decay2, cum=cum2,
        fades=fades2, before=before2, total=total2, **shared,
    )
    ex1 = Exchange(seq, one, ex1_refs, ex1_sems)
    ex2 = Exchange(seq, two, ex2_refs, ex2_sems)

    @pl.when(ex1.group == 0)
    def _():
        ex1.came[...] = jnp.zeros_like(ex1.came)
        ex2.came[...] = jnp.zeros_like(ex2.came)

    for copy in small_loads[:2]:
        copy.wait()
    prepare_sums(one)
    small_loads[2].wait()
    state[...] = jnp.zeros_like(state)

    def states1(b, carry):
        load(b).wait()
        write32 = write1[:, span_of(b)].astype(F32)
        for h in range(heads):
            add_state(one, b, h, write32, x[b, :, lanes_of(h)])
        return carry

    lax.fori_loop(0, blocks, states1, 0)
    def inner1(c):
        def block(b, carry):
            for h in numbers[c]:
                inner_block(one, b, h, x[b, :, lanes_of(h)])
                silus[b, :, lanes_of(h)] = silu(gate1[b, :, lanes_of(h)])
            return carry

        lax.fori_loop(0, blocks, block, 0)

    small_loads[3].wait()
    prepare_scores(one)
    squares[...] = jnp.zeros_like(squares)
    gate_loads[0].wait()
    inner1(0)
    greet_wait(axes)
    ex1.near_copy().start()
    for c, part in enumerate(parts):
        ex1.swap(c, part)
    fades = ex1.fades()
    ex1.announce()
    ex1.send_own(0, parts[0], fades)
    soon = ex1.group < ex1.groups // 2

    @pl.when(ex1.group == 0)
    def _():
        for c in range(1, chunks):
            ex1.step(c, parts[c], fades)

    def store1(b, h, gated):
        slot = turned.at[h % 2]
        slot[...] = gated
        for col in range(grid_cols):
            sendbuf[col // local_cols, col % local_cols, b, :, lanes_of(h)] = slot[
                pl.ds(col, high, stride=grid_cols), :
            ].astype(BF16)

    def finish1(c):
        def block(b, carry):
            finish_block(one, b, numbers[c], store1)
            return carry

        lax.fori_loop(0, blocks, block, 0)

    def wide(c):
        return pl.ds(parts[c].start * LANES, parts[c].size * LANES)

    def bulk(c, hop):
        to = lax.rem(me - hop + seq, seq)
        return pltpu.make_async_remote_copy(
            src_ref=sendbuf.at[to, :, :, :, wide(c)],
            dst_ref=recvbuf.at[me, :, :, :, wide(c)],
            send_sem=bulk_send.at[hop - 1, c],
            recv_sem=bulk_recv.at[hop - 1, c],
            device_id={"seq": to},
            device_id_type=MESH,
        )

    def keep(c):
        return pltpu.make_async_copy(
            sendbuf.at[me, :, :, :, wide(c)], recvbuf.at[me, :, :, :, wide(c)], keep_sems.at[c]
        )

    def send_all(c):
        for hop in range(1, seq):
            bulk(c, hop).start()
        keep(c).start()

    ex1.take_own(parts[0], fades)
    finish1(0)
    for hop in range(1, seq):

        @pl.when(hop <= me)
        def _(hop=hop):
            bulk(0, hop).start()


    @pl.when(soon & (ex1.group > 0))
    def _():
        for c in range(1, chunks):
            ex1.step(c, parts[c], fades)

    for hop in range(1, seq):

        @pl.when(hop > me)
        def _(hop=hop):
            bulk(0, hop).start()

    keep(0).start()
    for c in range(1, chunks):
        inner1(c)

        @pl.when(jnp.logical_not(soon))
        def _(c=c):
            ex1.step(c, parts[c], fades)

        finish1(c)
        if c == 1:
            send_all(c)
    reduce_squares(one, rows1)
    scale[...] = lax.rsqrt(head_sum(head_count, rows1, held1, sum1.at[0], sum1.at[1]) / inner + EPSILON)
    depth = scale.shape[0]
    mine = pl.ds(pl.multiple_of(me * depth, depth), depth)
    scale_copies = []
    for hop in range(1, seq):
        copy = pltpu.make_async_remote_copy(
            src_ref=scale,
            dst_ref=scales.at[mine],
            send_sem=scale_send.at[hop - 1],
            recv_sem=scale_recv.at[hop - 1],
            device_id={"seq": lax.rem(me - hop + seq, seq)},
            device_id_type=MESH,
        )
        copy.start()
        scale_copies.append(copy)
    for c in range(2, chunks):
        send_all(c)
    scales[mine, :] = scale[...]

    for copy in small_loads[4:]:
        copy.wait()
    prepare_sums(two)
    prepare_scores(two)
    state[...] = jnp.zeros_like(state)
    squares[...] = jnp.zeros_like(squares)
    ex2.near_copy().start()
    ex2_fades = ex2.fades()
    ex2.announce()
    gate_loads[1].wait()
    all_rows = per_col * BLOCK

    def place_of(b):
        return pl.ds(lax.rem(b, per_col) * (BLOCK * local_cols) + b // per_col, BLOCK, stride=local_cols)

    if local_cols > 1:
        for h in range(heads):
            slot = woven.at[h % 2]
            slot[...] = gate_raw[:, :, lanes_of(h)].astype(F32).reshape(all_rows * local_cols, LANES)
            for b in range(blocks):
                at = (b % per_col) * BLOCK * local_cols + b // per_col
                silus[b, :, lanes_of(h)] = silu(slot[pl.ds(at, BLOCK, stride=local_cols), :])
    else:
        for h in range(heads):
            for b in range(blocks):
                silus[b, :, lanes_of(h)] = silu(gate2[b, :, lanes_of(h)])
    for copy in scale_copies:
        copy.wait()

    def columns(b, carry):
        window = pl.ds(
            pl.multiple_of(lax.rem(b, per_col) * slabs * depth, slabs * depth), slabs * depth
        )
        picked = column_scale(me * local_cols + b // per_col, grid_rows, grid_cols, scales[window, :])
        column[b] = jnp.broadcast_to(picked, (BLOCK, LANES))
        return carry

    lax.fori_loop(0, blocks, columns, 0)

    def arrive(c):
        keep(c).wait()
        for hop in range(1, seq):
            bulk(c, hop).wait()

    def states2(c):
        def block(b, carry):
            write32 = write2[:, span_of(b)].astype(F32)
            slab = pl.ds(lax.rem(b, per_col) * slabs, slabs)
            for h in numbers[c]:
                lanes = lanes_of(h)
                own = recvbuf[slab, b // per_col, :, :, lanes].astype(F32).reshape(BLOCK, LANES)
                own = (own * column[b] * gain1[h : h + 1, :]).astype(BF16)
                hidden[b, :, lanes] = own
                add_state(two, b, h, write32, own)
            return carry

        lax.fori_loop(0, blocks, block, 0)

    def inner2(c):
        def block(b, carry):
            for h in numbers[c]:
                inner_block(two, b, h, hidden[b, :, lanes_of(h)])
            return carry

        lax.fori_loop(0, blocks, block, 0)

    def store2(b, h, gated):
        flat[h, place_of(b), :] = gated

    def put(c):
        return pltpu.make_async_copy(flat.at[parts[c]], out_hbm.at[parts[c]], out_sems.at[c])

    def finish2(c):
        def block(b, carry):
            finish_block(two, b, numbers[c], store2)
            return carry

        lax.fori_loop(0, blocks, block, 0)
        put(c).start()

    last = chunks - 1
    fades = ex2_fades

    def chain(slot):
        for late in range(2):
            c = slot - 1 - late
            if 0 <= c < last:

                @pl.when(soon & (jnp.minimum(ex2.group, 1) == late))
                def _(c=c):
                    ex2.step(c, parts[c], fades)

    for c in range(chunks):
        if c == last:
            chain(last)
            chain(last + 1)
        if c == last - 1:

            @pl.when(soon)
            def _():
                for e in range(last - 3):
                    finish2(e)

        arrive(c)
        states2(c)
        ex2.swap(c, parts[c])
        inner2(c)
        if c < last:
            chain(c)
    ends = ex2.group == ex2.groups - 1

    @pl.when(jnp.logical_not(soon | ends))
    def _():
        for e in range(last):
            ex2.step(e, parts[e], fades)

    ex2.send_own(last, parts[last], fades)
    for e in range(last):

        @pl.when(ends)
        def _(e=e):
            ex2.step(e, parts[e], fades)

        if e < last - 3:

            @pl.when(jnp.logical_not(soon))
            def _(e=e):
                finish2(e)

        else:
            finish2(e)
    ex2.take_own(parts[last], fades)
    finish2(last)
    reduce_squares(two, rows1)
    total = head_sum(head_count, rows1, held2, sum2.at[0], sum2.at[1])
    total = jnp.transpose(lax.rsqrt(total / inner + EPSILON))
    for b in range(blocks):
        at = (b % per_col) * BLOCK * local_cols + b // per_col
        scale_ref[pl.ds(at, BLOCK, stride=local_cols), :] = jnp.broadcast_to(
            total[:, b : b + 1], (BLOCK, LANES)
        )
    for c in range(chunks):
        put(c).wait()
    numbered = list(enumerate(parts))
    ex1.settle(numbered[1:])
    ex2.settle(numbered[:-1])


def norm_kernel(steps, gated_hbm, scale_hbm, gain_ref, out_hbm, gated, scale, out, load_sems, out_sems):
    heads, rows, _ = gated.shape
    part = rows // steps
    tall = out.shape[0] // steps
    loads = [
        pltpu.make_async_copy(scale_hbm, scale, load_sems.at[steps]),
        *(
            pltpu.make_async_copy(
                gated_hbm.at[:, pl.ds(i * part, part)], gated.at[:, pl.ds(i * part, part)],
                load_sems.at[i],
            )
            for i in range(steps)
        ),
    ]
    puts = [
        pltpu.make_async_copy(
            out.at[pl.ds(i * tall, tall)], out_hbm.at[pl.ds(i * tall, tall)], out_sems.at[i]
        )
        for i in range(steps)
    ]
    for copy in loads:
        copy.start()
    loads[0].wait()
    for i in range(steps):
        loads[i + 1].wait()
        span = pl.ds(i * part, part)
        for h in range(heads):
            lanes = lanes_of(h)
            result = gated[h, span, :] * scale[span, :] * gain_ref[h : h + 1, :]
            shape = (tall,) + out.shape[1:-1] + (LANES,)
            out[pl.ds(i * tall, tall), ..., lanes] = result.reshape(shape).astype(BF16)
        puts[i].start()
    for copy in puts:
        copy.wait()


def body(
    seq, head, tokens_in, gate_rows, gate_cols, write_rows, read_rows, step_rows, decay_rows,
    skip_rows, norm_rows, write_cols, read_cols, step_cols, decay_cols, skip_cols, norm_cols,
):
    grid_rows, grid_cols, features = tokens_in.shape
    blocks = grid_rows * grid_cols // BLOCK
    high = BLOCK // grid_cols
    local_cols = grid_cols // seq
    all_rows = grid_rows * seq
    per_col = all_rows // BLOCK
    inner = features * head
    heads, size = step_rows.shape[0], write_rows.shape[0]
    width = features // heads
    depth = round_up(blocks, 8)
    padded = round_up(heads, 16)
    chunks = -(-heads // CHUNK)
    dma = pltpu.SemaphoreType.DMA
    anywhere = pl.BlockSpec(memory_space=pl.ANY)
    whole = pl.BlockSpec(memory_space=pltpu.VMEM)
    smem = pl.BlockSpec(memory_space=pltpu.SMEM)
    vmem = pltpu.VMEM
    tokens = (blocks, BLOCK, features)
    packed = (seq, local_cols, blocks, high, features)
    sums = (blocks, padded, BLOCK)
    rows = (blocks, padded, LANES)
    total = (padded, LANES)
    tall = (blocks, BLOCK, padded)
    states = (heads, size, width)
    groups = seq // 2
    held = (min(CHUNK, heads), size, width)
    far = max(groups - 1, 1)
    exchange = [vmem(states, BF16)] * 4 + [
        vmem(total, F32), vmem(held, BF16), vmem((far,) + held, BF16), vmem(total, F32),
        vmem((far,) + total, F32), vmem(total, F32),
    ]
    exchange_sems = [dma((2, chunks)), dma((2,)), dma((2, chunks)), dma((2, far)), dma((2, far))]
    small = (
        decay_rows, step_rows, write_rows, read_rows, norm_rows.reshape(heads, width),
        decay_cols, step_cols, write_cols, read_cols,
    )
    raw = (all_rows, local_cols, features)
    flat = raw if local_cols > 1 else (all_rows, features)
    gate = gate_cols if local_cols > 1 else gate_cols.reshape(tokens)
    gated, scale = pl.pallas_call(
        functools.partial(fused_kernel, seq, head, inner, grid_cols, local_cols, per_col),
        out_shape=(
            jax.ShapeDtypeStruct((heads, all_rows * local_cols, LANES), F32),
            jax.ShapeDtypeStruct((all_rows * local_cols, LANES), F32),
        ),
        in_specs=[smem, smem] + [anywhere] * (3 + SMALL),
        out_specs=(anywhere, whole),
        scratch_shapes=[
            vmem(tokens, BF16), vmem(tokens, BF16),
            vmem(tokens if local_cols == 1 else (1, BLOCK, LANES), BF16),
            vmem(packed, BF16), vmem(packed, BF16), vmem(tokens, BF16),
            vmem(tokens, F32), vmem((2, BLOCK, LANES), F32),
            *(vmem(array.shape, array.dtype) for array in small),
            vmem(raw if local_cols > 1 else (1, LANES), BF16),
            vmem((heads, all_rows * local_cols, LANES), F32),
            vmem((2, all_rows * local_cols if local_cols > 1 else 8, LANES), F32),
            vmem(tokens, F32),
            vmem((blocks, 3, padded, BLOCK), BF16), vmem(sums, F32), vmem(sums, F32),
            vmem(sums, F32), vmem(rows, F32), vmem(rows, F32), vmem(rows, F32), vmem(rows, F32),
            vmem(total, F32), vmem(total, F32), vmem(tall, F32), vmem(tall, F32),
            vmem((blocks, BLOCK, BLOCK), F32), vmem((blocks, BLOCK, 2 * size), BF16),
            vmem(states, F32), vmem((blocks,) + states, F32), vmem(states, F32),
            vmem((blocks, BLOCK, LANES), F32), vmem((depth, BLOCK), F32),
            vmem((head - 1, depth, BLOCK), F32), vmem((head - 1, depth, BLOCK), F32),
            vmem((depth, BLOCK), F32), vmem((seq * depth, BLOCK), F32),
            vmem((blocks, BLOCK, LANES), F32),
            *exchange, *exchange,
            dma((3, blocks)), dma((SMALL,)), dma((seq - 1, chunks)), dma((seq - 1, chunks)), dma((chunks,)),
            dma((2, head - 1)), dma((2, head - 1)), dma((seq - 1,)), dma((seq - 1,)),
            dma((chunks,)),
            *exchange_sems, *exchange_sems,
        ],
        compiler_params=pltpu.CompilerParams(
            collective_id=0, has_side_effects=True, vmem_limit_bytes=VMEM_BYTES
        ),
        name="fused",
    )(
        skip_rows, skip_cols, tokens_in.reshape(tokens), gate_rows.reshape(tokens), gate, *small
    )
    steps = 8
    result = pl.pallas_call(
        functools.partial(norm_kernel, steps),
        out_shape=jax.ShapeDtypeStruct(flat, BF16),
        in_specs=[anywhere, anywhere, whole],
        out_specs=anywhere,
        scratch_shapes=[
            vmem(gated.shape, F32), vmem(scale.shape, F32), vmem(flat, BF16),
            dma((steps + 1,)), dma((steps,)),
        ],
        compiler_params=pltpu.CompilerParams(vmem_limit_bytes=VMEM_BYTES),
        name="norm",
    )(gated, scale, norm_cols.reshape(heads, width))
    return result.reshape(all_rows, local_cols, features)


def solution(mesh):
    placed = (
        P("seq", None, "head"),
        P("seq", None, "head"),
        P(None, "seq", "head"),
        P(None, "seq"),
        P(None, "seq"),
        P("head", "seq"),
        P("head", "seq"),
        P("head"),
        P("head"),
        P(None, "seq"),
        P(None, "seq"),
        P("head", "seq"),
        P("head", "seq"),
        P("head"),
        P("head"),
    )
    return jax.shard_map(
        functools.partial(body, mesh.shape["seq"], mesh.shape["head"]),
        mesh=mesh, in_specs=placed, out_specs=P(None, "seq", "head"), check_vma=False,
    )
```

```python
import functools
import jax
import jax.numpy as jnp
from jax import lax
from jax.experimental import pallas as pl
from jax.experimental.pallas import tpu as pltpu
from jax.sharding import PartitionSpec as P

BLOCK = 256
HALF = 128
LANES = 128
CHUNK = 2
SMALL = 9
EPSILON = 1e-05
LOG2E = 1.4426950408889634
HIGHEST = lax.Precision.HIGHEST
MESH = pl.DeviceIdType.MESH
F32 = jnp.float32
BF16 = jnp.bfloat16
VMEM_BYTES = 60 * 1024 * 1024


def contract(a, b, dims, precision=None):
    return lax.dot_general(
        a, b, (dims, ((), ())), precision=precision, preferred_element_type=F32
    )


def iota(shape, axis):
    return lax.broadcasted_iota(jnp.int32, shape, axis)


def round_up(value, step):
    return -(-value // step) * step


def split(value, count):
    parts = []
    for _ in range(count - 1):
        part = value.astype(BF16)
        parts.append(part)
        value = value - part.astype(F32)
    parts.append(value.astype(BF16))
    return parts


def span_of(b):
    return pl.ds(pl.multiple_of(b * BLOCK, BLOCK), BLOCK)


class Layer:
    def __init__(self, **refs):
        self.__dict__.update(refs)


def prepare_sums(layer):
    heads, length = layer.decay.shape
    blocks = length // BLOCK
    padded = layer.cum.shape[1]
    layer.stage[...] = jnp.zeros_like(layer.stage)
    for p, part in enumerate(split(layer.decay[...] * LOG2E, 3)):
        for b in range(blocks):
            layer.stage[b, p, :heads] = part[:, b * BLOCK : (b + 1) * BLOCK]
    upper = (iota((BLOCK, BLOCK), 0) <= iota((BLOCK, BLOCK), 1)).astype(BF16)
    sums = contract(layer.stage[...].reshape(blocks * 3 * padded, BLOCK), upper, ((1,), (0,)))
    sums = sums.reshape(blocks, 3, padded, BLOCK)
    run = jnp.zeros((padded, 1), F32)
    for b in range(blocks):
        cum = sums[b, 0] + sums[b, 1] + sums[b, 2]
        final = cum[:, BLOCK - 1 :]
        layer.cum[b] = cum
        layer.weights[b, :heads] = (
            jnp.exp2(final[:heads] - cum[:heads]) * layer.step[:, b * BLOCK : (b + 1) * BLOCK]
        )
        layer.fades[b] = jnp.broadcast_to(jnp.exp2(final), (padded, LANES))
        layer.before[b] = jnp.broadcast_to(jnp.exp2(run), (padded, LANES))
        run = run + final
    layer.total[...] = jnp.broadcast_to(run, (padded, LANES))


def prepare_scores(layer):
    blocks = layer.cum.shape[0]
    lower = (iota((BLOCK, BLOCK), 0) >= iota((BLOCK, BLOCK), 1)).astype(F32)

    def block(b, carry):
        across = jnp.transpose(layer.cum[b])
        layer.across[b] = across
        layer.lifting[b] = jnp.exp2(across)
        read = layer.read[:, span_of(b)]
        layer.scores[b] = contract(read, layer.write[:, span_of(b)], ((0,), (0,))) * lower
        read32 = read.astype(F32)
        layer.read_t[b] = jnp.transpose(jnp.concatenate([read32, read32], axis=0)).astype(BF16)
        return carry

    lax.fori_loop(0, blocks, block, 0)


def lanes_of(h):
    return slice(h * LANES, (h + 1) * LANES)


def add_state(layer, b, h, write32, own):
    loaded = (write32 * layer.weights[b, h : h + 1, :]).astype(BF16)
    gained = contract(loaded, own, ((1,), (0,)))
    held = layer.state[h]
    layer.local[b, h] = held
    layer.state[h] = layer.fades[b, h : h + 1, :] * held + gained


def inner_block(layer, b, h, own):
    across = layer.across[b, :, h : h + 1]
    cum = layer.cum[b, h : h + 1, :]
    step = layer.step[h : h + 1, span_of(b)]
    top, low = slice(0, HALF), slice(HALF, BLOCK)

    def mix(rows, cols, diagonal):
        spread = across[rows] - cum[:, cols]
        if diagonal:
            spread = jnp.minimum(spread, 0.0)
        return (jnp.exp2(spread) * layer.scores[b, rows, cols] * step[:, cols]).astype(BF16)

    skip = layer.skip[h]
    first = contract(mix(top, top, True), own[top], ((1,), (0,)))
    layer.inner[b, top, lanes_of(h)] = first + skip * own[top].astype(F32)
    both = jnp.concatenate([mix(low, top, False), mix(low, low, True)], axis=1)
    second = contract(both, own, ((1,), (0,)))
    layer.inner[b, low, lanes_of(h)] = second + skip * own[low].astype(F32)


def finish_block(layer, b, hs, store):
    held = jnp.concatenate(
        [layer.before[b, h : h + 1, :] * layer.prior[h] + layer.local[b, h] for h in hs], axis=1
    )
    parts = jnp.concatenate(split(held, 2), axis=0)
    from_state = contract(layer.read_t[b], parts, ((1,), (0,)))
    squares = jnp.zeros((BLOCK, LANES), F32)
    for i, h in enumerate(hs):
        out = layer.inner[b, :, lanes_of(h)]
        out += layer.lifting[b, :, h : h + 1] * from_state[:, i * LANES : (i + 1) * LANES]
        gated = out * layer.silu[b, :, lanes_of(h)]
        squares += gated * gated
        store(b, h, gated)
    layer.squares[b] += squares


def silu(gate):
    gate = gate.astype(F32)
    return gate / (1.0 + jnp.exp2(gate * -LOG2E))


def reduce_squares(layer, rows_ref):
    blocks = layer.squares.shape[0]
    rows_ref[...] = jnp.zeros_like(rows_ref)
    for b in range(blocks):
        parts = jnp.concatenate(split(layer.squares[b], 2), axis=1)
        row = contract(jnp.ones((8, 2 * LANES), BF16), parts, ((1,), (1,)))
        rows_ref[b : b + 1, :] = row[:1]


def column_scale(column, grid_rows, grid_cols, scales):
    high = BLOCK // grid_cols
    shape = (BLOCK, scales.shape[0])
    row = iota(shape, 0)
    depth = scales.shape[0] * grid_rows // BLOCK
    source = (row // grid_rows) * depth + (row % grid_rows) // high
    picked = contract((iota(shape, 1) == source).astype(F32), scales, ((1,), (0,)), HIGHEST)
    lane = (iota((BLOCK, BLOCK), 0) % high) * grid_cols + column
    return jnp.sum(jnp.where(iota((BLOCK, BLOCK), 1) == lane, picked, 0.0), axis=1, keepdims=True)


def greet_signal(axes):
    barrier = pltpu.get_barrier_semaphore()
    for axis, count in axes:
        me = lax.axis_index(axis)
        for hop in range(1, count):
            pl.semaphore_signal(
                barrier, inc=1, device_id={axis: lax.rem(me + hop, count)}, device_id_type=MESH
            )


def greet_wait(axes):
    pl.semaphore_wait(
        pltpu.get_barrier_semaphore(), sum(count - 1 for _, count in axes)
    )


def head_sum(count, own_ref, held, sems):
    me = lax.axis_index("head")

    def copy(source, target, hop):
        return pltpu.make_async_remote_copy(
            src_ref=source, dst_ref=target, send_sem=sems.at[0], recv_sem=sems.at[1],
            device_id={"head": lax.rem(me + hop, count)}, device_id_type=MESH,
        )

    for hop in range(1, count):
        copy(own_ref, held.at[hop - 1], hop).start()
    copy(held, held, 1).wait()
    total = own_ref[...]
    for hop in range(1, count):
        total += held[hop - 1]
    return total


class Exchange:
    def __init__(self, seq, layer, refs, sems):
        self.layer = layer
        self.sent, self.swapped, self.passed, self.came, self.near, *refs = refs
        self.own, self.landed, self.pair_total, self.pair_totals, self.span = refs
        self.swap_sems, self.near_sems, self.pass_sems, self.own_sems, self.total_sems = sems
        self.seq, self.me = seq, lax.axis_index("seq")
        self.chunks = self.swap_sems.shape[0] - 1
        me = lax.axis_index("seq")
        self.place = lax.rem(me, 2)
        self.partner = me + 1 - 2 * self.place
        self.group = me // 2
        self.groups = seq // 2
        self.ahead = lax.rem(me + 2, seq)

    def near_copy(self):
        return pltpu.make_async_remote_copy(
            src_ref=self.layer.total, dst_ref=self.near, send_sem=self.near_sems.at[0],
            recv_sem=self.near_sems.at[1], device_id={"seq": self.partner}, device_id_type=MESH,
        )

    def swap_copy(self, c, part):
        return pltpu.make_async_remote_copy(
            src_ref=self.sent.at[part], dst_ref=self.swapped.at[part],
            send_sem=self.swap_sems.at[self.chunks], recv_sem=self.swap_sems.at[c],
            device_id={"seq": self.partner}, device_id_type=MESH,
        )

    def pass_copy(self, c, part):
        return pltpu.make_async_remote_copy(
            src_ref=self.passed.at[part], dst_ref=self.came.at[part],
            send_sem=self.pass_sems.at[self.chunks], recv_sem=self.pass_sems.at[c],
            device_id={"seq": self.ahead}, device_id_type=MESH,
        )

    def swap(self, c, part):
        for h in range(part.start, part.start + part.size):
            self.sent[h] = self.layer.state[h].astype(BF16)
        self.swap_copy(c, part).start()

    def fades(self):
        self.near_copy().wait()
        mine, other = self.layer.total[...], self.near[...]
        even = self.place == 0
        return jnp.exp2(jnp.where(even, mine, other)), jnp.exp2(jnp.where(even, other, mine))

    def step(self, c, part, fades):
        layer = self.layer
        first_fade, last_fade = fades
        even = self.place == 0
        self.swap_copy(c, part).wait_recv()

        @pl.when(self.group > 0)
        def _():
            self.pass_copy(c, part).wait_recv()

        for h in range(part.start, part.start + part.size):
            first, last = self.pair_of(h)
            before = self.came[h].astype(F32)
            middle = first_fade[h : h + 1] * before + first
            self.passed[h] = (last_fade[h : h + 1] * middle + last).astype(BF16)
            layer.prior[h] = jnp.where(even, before, middle)

        @pl.when(self.group < self.groups - 1)
        def _():
            self.pass_copy(c, part).start()

    def own_copy(self, hop):
        return pltpu.make_async_remote_copy(
            src_ref=self.own, dst_ref=self.landed.at[hop - 1], send_sem=self.own_sems.at[0, hop - 1],
            recv_sem=self.own_sems.at[1, hop - 1],
            device_id={"seq": lax.rem(self.me + 2 * hop, self.seq)}, device_id_type=MESH,
        )

    def total_copy(self, hop):
        return pltpu.make_async_remote_copy(
            src_ref=self.pair_total, dst_ref=self.pair_totals.at[hop - 1],
            send_sem=self.total_sems.at[0, hop - 1], recv_sem=self.total_sems.at[1, hop - 1],
            device_id={"seq": lax.rem(self.me + 2 * hop, self.seq)}, device_id_type=MESH,
        )

    def announce(self):
        self.pair_total[...] = self.layer.total[...] + self.near[...]
        for hop in range(1, self.groups):

            @pl.when(self.group + hop < self.groups)
            def _(hop=hop):
                self.total_copy(hop).start()

    def pair_of(self, h):
        mine, other = self.layer.state[h], self.swapped[h].astype(F32)
        even = self.place == 0
        return jnp.where(even, mine, other), jnp.where(even, other, mine)

    def send_own(self, c, part, fades):
        self.swap_copy(c, part).wait_recv()
        for i, h in enumerate(range(part.start, part.start + part.size)):
            first, last = self.pair_of(h)
            self.own[i] = (fades[1][h : h + 1] * first + last).astype(BF16)
        for hop in range(1, self.groups):

            @pl.when(self.group + hop < self.groups)
            def _(hop=hop):
                self.own_copy(hop).start()

    def take_own(self, part, fades):
        prior = self.layer.prior
        heads = range(part.start, part.start + part.size)
        self.span[...] = jnp.zeros_like(self.span)
        for h in heads:
            prior[h] = jnp.zeros(prior.shape[1:], F32)
        for hop in range(1, self.groups):

            @pl.when(self.group >= hop)
            def _(hop=hop):
                self.total_copy(hop).wait_recv()
                self.own_copy(hop).wait_recv()
                factor = jnp.exp2(self.span[...])
                for i, h in enumerate(heads):
                    prior[h] += factor[h : h + 1] * self.landed[hop - 1, i].astype(F32)
                self.span[...] += self.pair_totals[hop - 1]

        for h in heads:
            before = prior[h]
            middle = fades[0][h : h + 1] * before + self.pair_of(h)[0]
            prior[h] = jnp.where(self.place == 0, before, middle)

    def settle(self, start, stop):
        self.swap_copy(0, pl.ds(0, self.sent.shape[0])).wait_send()
        if stop > start:

            @pl.when(self.group < self.groups - 1)
            def _():
                self.pass_copy(0, pl.ds(start, stop - start)).wait_send()

        for hop in range(1, self.groups):

            @pl.when(self.group + hop < self.groups)
            def _(hop=hop):
                self.total_copy(hop).wait_send()
                self.own_copy(hop).wait_send()


def fused_kernel(
    seq, head_count, inner, grid_cols, local_cols, per_col,
    skip1, skip2, x_hbm, gate1_hbm, gate2_hbm, *refs
):
    small_hbm, refs = refs[:SMALL], refs[SMALL:]
    out_hbm, total_ref, x, gate1, gate2, sendbuf, recvbuf, hidden, innerbuf, turned, *refs = refs
    small, refs = refs[:SMALL], refs[SMALL:]
    decay1, step1, write1, read1, gain1, decay2, step2, write2, read2 = small
    (
        gate_raw, flat, woven, silus,
    stage, cum1, cum2, weights, fades1, fades2, before1, before2, total1, total2, across, lifting,
    scores, read_t, state, local, prior, squares, rows1, held1, held2, scale, scales, column,
    *refs,
    ) = refs
    ex1_refs, ex2_refs, refs = refs[:10], refs[10:20], refs[20:]
    (
        load_sems, small_sems, bulk_sems, sum1, sum2, scale_sems, out_sem, *refs,
    ) = refs
    ex1_sems, ex2_sems = refs[:5], refs[5:]
    axes = (("seq", seq), ("head", head_count))
    me = lax.axis_index("seq")
    blocks, _, features = x.shape
    heads = features // LANES
    high = BLOCK // grid_cols
    grid_rows = blocks * high
    slabs = BLOCK // grid_rows
    parts = [pl.ds(c, min(CHUNK, heads - c)) for c in range(0, heads, CHUNK)]
    numbers = [range(part.start, part.start + part.size) for part in parts]
    chunks = len(parts)
    greet_signal(axes)

    def load(b):
        return pltpu.make_async_copy(x_hbm.at[b], x.at[b], load_sems.at[b])

    gate_loads = [
        pltpu.make_async_copy(gate1_hbm, gate1, load_sems.at[blocks]),
        pltpu.make_async_copy(
            gate2_hbm, gate_raw if local_cols > 1 else gate2, load_sems.at[blocks + 1]
        ),
    ]
    small_loads = [
        pltpu.make_async_copy(source, target, small_sems.at[i])
        for i, (source, target) in enumerate(zip(small_hbm, small))
    ]
    for copy in small_loads[:3]:
        copy.start()
    for b in range(blocks):
        load(b).start()
    for copy in small_loads[3:] + gate_loads:
        copy.start()

    shared = dict(
        stage=stage, weights=weights, across=across, lifting=lifting, scores=scores,
        read_t=read_t, state=state, local=local, prior=prior, squares=squares, inner=innerbuf,
        silu=silus,
    )
    one = Layer(
        skip=skip1, write=write1, read=read1, step=step1, decay=decay1, cum=cum1,
        fades=fades1, before=before1, total=total1, **shared,
    )
    two = Layer(
        skip=skip2, write=write2, read=read2, step=step2, decay=decay2, cum=cum2,
        fades=fades2, before=before2, total=total2, **shared,
    )
    ex1 = Exchange(seq, one, ex1_refs, ex1_sems)
    ex2 = Exchange(seq, two, ex2_refs, ex2_sems)

    @pl.when(ex1.group == 0)
    def _():
        ex1.came[...] = jnp.zeros_like(ex1.came)
        ex2.came[...] = jnp.zeros_like(ex2.came)

    for copy in small_loads[:2]:
        copy.wait()
    prepare_sums(one)
    small_loads[2].wait()
    state[...] = jnp.zeros_like(state)

    def states1(b, carry):
        load(b).wait()
        write32 = write1[:, span_of(b)].astype(F32)
        for h in range(heads):
            add_state(one, b, h, write32, x[b, :, lanes_of(h)])
        return carry

    lax.fori_loop(0, blocks, states1, 0)
    def inner1(c):
        def block(b, carry):
            for h in numbers[c]:
                inner_block(one, b, h, x[b, :, lanes_of(h)])
                silus[b, :, lanes_of(h)] = silu(gate1[b, :, lanes_of(h)])
            return carry

        lax.fori_loop(0, blocks, block, 0)

    small_loads[3].wait()
    prepare_scores(one)
    squares[...] = jnp.zeros_like(squares)
    gate_loads[0].wait()
    inner1(0)
    greet_wait(axes)
    ex1.near_copy().start()
    for c, part in enumerate(parts):
        ex1.swap(c, part)
    fades = ex1.fades()
    ex1.announce()
    ex1.send_own(0, parts[0], fades)
    soon = ex1.group < ex1.groups // 2

    @pl.when(ex1.group == 0)
    def _():
        for c in range(1, chunks):
            ex1.step(c, parts[c], fades)

    def store1(b, h, gated):
        slot = turned.at[h % 2]
        slot[...] = gated
        for col in range(grid_cols):
            sendbuf[col // local_cols, col % local_cols, b, :, lanes_of(h)] = slot[
                pl.ds(col, high, stride=grid_cols), :
            ].astype(BF16)

    def finish1(c):
        def block(b, carry):
            finish_block(one, b, numbers[c], store1)
            return carry

        lax.fori_loop(0, blocks, block, 0)

    def wide(c):
        return pl.ds(parts[c].start * LANES, parts[c].size * LANES)

    def bulk(c, hop):
        to = lax.rem(me - hop + seq, seq)
        return pltpu.make_async_remote_copy(
            src_ref=sendbuf.at[to, :, :, :, wide(c)],
            dst_ref=recvbuf.at[me, :, :, :, wide(c)],
            send_sem=bulk_sems.at[0, c],
            recv_sem=bulk_sems.at[1, c],
            device_id={"seq": to},
            device_id_type=MESH,
        )

    def keep(c):
        return pltpu.make_async_copy(
            sendbuf.at[me, :, :, :, wide(c)], recvbuf.at[me, :, :, :, wide(c)], bulk_sems.at[1, c]
        )

    def send_all(c):
        for hop in range(1, seq):
            bulk(c, hop).start()
        keep(c).start()

    ex1.take_own(parts[0], fades)
    finish1(0)
    for hop in range(1, seq):

        @pl.when(hop <= me)
        def _(hop=hop):
            bulk(0, hop).start()


    @pl.when(soon & (ex1.group > 0))
    def _():
        for c in range(1, chunks):
            ex1.step(c, parts[c], fades)

    for hop in range(seq - 1, 0, -1):

        @pl.when(hop > me)
        def _(hop=hop):
            bulk(0, hop).start()

    keep(0).start()
    for c in range(1, chunks):
        inner1(c)

        @pl.when(jnp.logical_not(soon))
        def _(c=c):
            ex1.step(c, parts[c], fades)

        finish1(c)
        if c == 1:
            send_all(c)
    reduce_squares(one, rows1)
    scale[...] = lax.rsqrt(head_sum(head_count, rows1, held1, sum1) / inner + EPSILON)
    depth = scale.shape[0]
    mine = pl.ds(pl.multiple_of(me * depth, depth), depth)

    def scale_copy(source, target, hop):
        return pltpu.make_async_remote_copy(
            src_ref=source, dst_ref=target, send_sem=scale_sems.at[0], recv_sem=scale_sems.at[1],
            device_id={"seq": lax.rem(me - hop + seq, seq)}, device_id_type=MESH,
        )

    for hop in range(1, seq):
        scale_copy(scale, scales.at[mine], hop).start()
    for c in range(2, chunks):
        send_all(c)
    scales[mine, :] = scale[...]

    for copy in small_loads[4:]:
        copy.wait()
    prepare_sums(two)
    prepare_scores(two)
    state[...] = jnp.zeros_like(state)
    squares[...] = jnp.zeros_like(squares)
    ex2.near_copy().start()
    ex2_fades = ex2.fades()
    ex2.announce()
    gate_loads[1].wait()
    all_rows = per_col * BLOCK

    def place_of(b):
        return pl.ds(lax.rem(b, per_col) * (BLOCK * local_cols) + b // per_col, BLOCK, stride=local_cols)

    if local_cols > 1:
        for h in range(heads):
            slot = woven.at[h % CHUNK]
            slot[...] = gate_raw[:, :, lanes_of(h)].astype(F32).reshape(all_rows * local_cols, LANES)
            for b in range(blocks):
                at = (b % per_col) * BLOCK * local_cols + b // per_col
                silus[b, :, lanes_of(h)] = silu(slot[pl.ds(at, BLOCK, stride=local_cols), :])
    else:
        for h in range(heads):
            for b in range(blocks):
                silus[b, :, lanes_of(h)] = silu(gate2[b, :, lanes_of(h)])
    others = scales.at[pl.ds(0, (seq - 1) * depth)]
    scale_copy(others, others, 1).wait()

    def columns(b, carry):
        window = pl.ds(
            pl.multiple_of(lax.rem(b, per_col) * slabs * depth, slabs * depth), slabs * depth
        )
        picked = column_scale(me * local_cols + b // per_col, grid_rows, grid_cols, scales[window, :])
        column[b] = jnp.broadcast_to(picked, (BLOCK, LANES))
        return carry

    lax.fori_loop(0, blocks, columns, 0)

    def bulk_all(c, count):
        some = pl.ds(0, count)
        return pltpu.make_async_remote_copy(
            src_ref=sendbuf.at[some, :, :, :, wide(c)],
            dst_ref=recvbuf.at[some, :, :, :, wide(c)],
            send_sem=bulk_sems.at[0, c],
            recv_sem=bulk_sems.at[1, c],
            device_id={"seq": lax.rem(me + 1, seq)},
            device_id_type=MESH,
        )

    def arrive(c):
        bulk_all(c, seq).wait_recv()

    def states2(c):
        def block(b, carry):
            write32 = write2[:, span_of(b)].astype(F32)
            slab = pl.ds(lax.rem(b, per_col) * slabs, slabs)
            for h in numbers[c]:
                lanes = lanes_of(h)
                own = recvbuf[slab, b // per_col, :, :, lanes].astype(F32).reshape(BLOCK, LANES)
                own = (own * column[b] * gain1[h : h + 1, :]).astype(BF16)
                hidden[b, :, lanes] = own
                add_state(two, b, h, write32, own)
            return carry

        lax.fori_loop(0, blocks, block, 0)

    def inner2(c):
        def block(b, carry):
            for h in numbers[c]:
                inner_block(two, b, h, hidden[b, :, lanes_of(h)])
            return carry

        lax.fori_loop(0, blocks, block, 0)

    def store2(b, h, gated):
        woven[h % CHUNK, place_of(b), :] = gated

    def put(c):
        return pltpu.make_async_copy(flat.at[parts[c]], out_hbm.at[parts[c]], out_sem.at[0])

    def finish2(c):
        def block(b, carry):
            finish_block(two, b, numbers[c], store2)
            return carry

        lax.fori_loop(0, blocks, block, 0)
        for h in numbers[c]:
            flat[h] = woven[h % CHUNK].astype(BF16)
        put(c).start()

    last = chunks - 1
    fades = ex2_fades
    ends = ex2.group == ex2.groups - 1

    def chain(slot):
        for late in range(2):
            c = slot - 1 - late
            if 0 <= c < last:

                @pl.when(soon & (jnp.minimum(ex2.group, 1) == late))
                def _(c=c):
                    ex2.step(c, parts[c], fades)

    for c in range(chunks):
        if c == last:
            chain(last)
            chain(last + 1)
        if c == last - 1:

            @pl.when(soon)
            def _():
                for e in range(last - 3):
                    finish2(e)

        arrive(c)
        states2(c)
        ex2.swap(c, parts[c])
        if c == last:

            @pl.when(jnp.logical_not(soon | ends))
            def _():
                for e in range(last):
                    ex2.step(e, parts[e], fades)

        inner2(c)
        if c < last:
            chain(c)
    ex2.send_own(last, parts[last], fades)
    for e in range(last):

        @pl.when(ends)
        def _(e=e):
            ex2.step(e, parts[e], fades)

        if e < last - 3:

            @pl.when(jnp.logical_not(soon))
            def _(e=e):
                finish2(e)

        else:
            finish2(e)
    ex2.take_own(parts[last], fades)
    finish2(last)
    reduce_squares(two, rows1)
    total_ref[...] = head_sum(head_count, rows1, held2, sum2)
    pltpu.make_async_copy(flat, out_hbm, out_sem.at[0]).wait()
    for c in range(chunks):
        bulk_all(c, seq - 1).wait_send()
    ex1.settle(numbers[0][-1] + 1, heads)
    ex2.settle(0, numbers[last][0])


def norm_kernel(
    steps, inner, per_col, gated_hbm, total_hbm, gain_hbm, out_hbm, gated, total, gain, scale, out,
    load_sems, out_sems,
):
    heads, rows, _ = gated.shape
    part = rows // steps
    tall = out.shape[0] // steps
    local_cols = rows // (per_col * BLOCK)
    small = [
        pltpu.make_async_copy(total_hbm, total, load_sems.at[steps]),
        pltpu.make_async_copy(gain_hbm, gain, load_sems.at[steps + 1]),
    ]
    loads = [
        pltpu.make_async_copy(
            gated_hbm.at[:, pl.ds(i * part, part)], gated.at[:, pl.ds(i * part, part)], load_sems.at[i]
        )
        for i in range(steps)
    ]
    puts = [
        pltpu.make_async_copy(
            out.at[pl.ds(i * tall, tall)], out_hbm.at[pl.ds(i * tall, tall)], out_sems.at[i]
        )
        for i in range(steps)
    ]
    for copy in small + loads:
        copy.start()
    for copy in small:
        copy.wait()
    columns = jnp.transpose(lax.rsqrt(total[...] / inner + EPSILON))
    for b in range(rows // BLOCK):
        at = (b % per_col) * BLOCK * local_cols + b // per_col
        scale[pl.ds(at, BLOCK, stride=local_cols), :] = jnp.broadcast_to(
            columns[:, b : b + 1], (BLOCK, LANES)
        )
    for i in range(steps):
        loads[i].wait()
        span = pl.ds(i * part, part)
        for h in range(heads):
            result = gated[h, span, :].astype(F32) * scale[span, :] * gain[h : h + 1, :]
            shape = (tall,) + out.shape[1:-1] + (LANES,)
            out[pl.ds(i * tall, tall), ..., lanes_of(h)] = result.reshape(shape).astype(BF16)
        puts[i].start()
    for copy in puts:
        copy.wait()


def body(
    seq, head, tokens_in, gate_rows, gate_cols, write_rows, read_rows, step_rows, decay_rows,
    skip_rows, norm_rows, write_cols, read_cols, step_cols, decay_cols, skip_cols, norm_cols,
):
    grid_rows, grid_cols, features = tokens_in.shape
    blocks = grid_rows * grid_cols // BLOCK
    high = BLOCK // grid_cols
    local_cols = grid_cols // seq
    all_rows = grid_rows * seq
    per_col = all_rows // BLOCK
    inner = features * head
    heads, size = step_rows.shape[0], write_rows.shape[0]
    width = features // heads
    depth = round_up(blocks, 8)
    padded = round_up(heads, 16)
    chunks = -(-heads // CHUNK)
    dma = pltpu.SemaphoreType.DMA
    anywhere = pl.BlockSpec(memory_space=pl.ANY)
    whole = pl.BlockSpec(memory_space=pltpu.VMEM)
    smem = pl.BlockSpec(memory_space=pltpu.SMEM)
    vmem = pltpu.VMEM
    tokens = (blocks, BLOCK, features)
    packed = (seq, local_cols, blocks, high, features)
    sums = (blocks, padded, BLOCK)
    rows = (blocks, padded, LANES)
    total = (padded, LANES)
    tall = (blocks, BLOCK, padded)
    states = (heads, size, width)
    groups = seq // 2
    held = (min(CHUNK, heads), size, width)
    far = max(groups - 1, 1)
    exchange = [vmem(states, BF16)] * 4 + [
        vmem(total, F32), vmem(held, BF16), vmem((far,) + held, BF16), vmem(total, F32),
        vmem((far,) + total, F32), vmem(total, F32),
    ]
    exchange_sems = [dma((chunks + 1,)), dma((2,)), dma((chunks + 1,)), dma((2, far)), dma((2, far))]
    small = (
        decay_rows, step_rows, write_rows, read_rows, norm_rows.reshape(heads, width),
        decay_cols, step_cols, write_cols, read_cols,
    )
    raw = (all_rows, local_cols, features)
    flat = raw if local_cols > 1 else (all_rows, features)
    gate = gate_cols if local_cols > 1 else gate_cols.reshape(tokens)
    gated, squares = pl.pallas_call(
        functools.partial(fused_kernel, seq, head, inner, grid_cols, local_cols, per_col),
        out_shape=(
            jax.ShapeDtypeStruct((heads, all_rows * local_cols, LANES), BF16),
            jax.ShapeDtypeStruct((depth, BLOCK), F32),
        ),
        in_specs=[smem, smem] + [anywhere] * (3 + SMALL),
        out_specs=(anywhere, whole),
        scratch_shapes=[
            vmem(tokens, BF16), vmem(tokens, BF16),
            vmem(tokens if local_cols == 1 else (1, BLOCK, LANES), BF16),
            vmem(packed, BF16), vmem(packed, BF16), vmem(tokens, BF16),
            vmem(tokens, F32), vmem((2, BLOCK, LANES), F32),
            *(vmem(array.shape, array.dtype) for array in small),
            vmem(raw if local_cols > 1 else (1, LANES), BF16),
            vmem((heads, all_rows * local_cols, LANES), BF16),
            vmem((CHUNK, all_rows * local_cols, LANES), F32),
            vmem(tokens, F32),
            vmem((blocks, 3, padded, BLOCK), BF16), vmem(sums, F32), vmem(sums, F32),
            vmem(sums, F32), vmem(rows, F32), vmem(rows, F32), vmem(rows, F32), vmem(rows, F32),
            vmem(total, F32), vmem(total, F32), vmem(tall, F32), vmem(tall, F32),
            vmem((blocks, BLOCK, BLOCK), F32), vmem((blocks, BLOCK, 2 * size), BF16),
            vmem(states, F32), vmem((blocks,) + states, F32), vmem(states, F32),
            vmem((blocks, BLOCK, LANES), F32), vmem((depth, BLOCK), F32),
            vmem((head - 1, depth, BLOCK), F32), vmem((head - 1, depth, BLOCK), F32),
            vmem((depth, BLOCK), F32), vmem((seq * depth, BLOCK), F32),
            vmem((blocks, BLOCK, LANES), F32),
            *exchange, *exchange,
            dma((blocks + 2,)), dma((SMALL,)), dma((2, chunks)),
            dma((2,)), dma((2,)), dma((2,)),
            dma((1,)),
            *exchange_sems, *exchange_sems,
        ],
        compiler_params=pltpu.CompilerParams(
            collective_id=0, has_side_effects=True, vmem_limit_bytes=VMEM_BYTES
        ),
        name="fused",
    )(
        skip_rows, skip_cols, tokens_in.reshape(tokens), gate_rows.reshape(tokens), gate, *small
    )
    steps = 8
    result = pl.pallas_call(
        functools.partial(norm_kernel, steps, inner, per_col),
        out_shape=jax.ShapeDtypeStruct(flat, BF16),
        in_specs=[anywhere] * 3,
        out_specs=anywhere,
        scratch_shapes=[
            vmem(gated.shape, BF16), vmem(squares.shape, F32), vmem((heads, width), F32),
            vmem((all_rows * local_cols, LANES), F32), vmem(flat, BF16),
            dma((steps + 2,)), dma((steps,)),
        ],
        compiler_params=pltpu.CompilerParams(vmem_limit_bytes=VMEM_BYTES),
        name="norm",
    )(gated, squares, norm_cols.reshape(heads, width))
    return result.reshape(all_rows, local_cols, features)


def solution(mesh):
    placed = (
        P("seq", None, "head"),
        P("seq", None, "head"),
        P(None, "seq", "head"),
        P(None, "seq"),
        P(None, "seq"),
        P("head", "seq"),
        P("head", "seq"),
        P("head"),
        P("head"),
        P(None, "seq"),
        P(None, "seq"),
        P("head", "seq"),
        P("head", "seq"),
        P("head"),
        P("head"),
    )
    return jax.shard_map(
        functools.partial(body, mesh.shape["seq"], mesh.shape["head"]),
        mesh=mesh, in_specs=placed, out_specs=P(None, "seq", "head"), check_vma=False,
    )
```

```python
import functools
import jax
import jax.numpy as jnp
from jax import lax
from jax.experimental import pallas as pl
from jax.experimental.pallas import tpu as pltpu
from jax.sharding import PartitionSpec as P

BLOCK = 256
HALF = 128
LANES = 128
CHUNK = 2
SMALL = 9
EPSILON = 1e-05
LOG2E = 1.4426950408889634
HIGHEST = lax.Precision.HIGHEST
MESH = pl.DeviceIdType.MESH
F32 = jnp.float32
BF16 = jnp.bfloat16
VMEM_BYTES = 60 * 1024 * 1024


def contract(a, b, dims, precision=None):
    return lax.dot_general(
        a, b, (dims, ((), ())), precision=precision, preferred_element_type=F32
    )


def iota(shape, axis):
    return lax.broadcasted_iota(jnp.int32, shape, axis)


def round_up(value, step):
    return -(-value // step) * step


def split(value, count):
    parts = []
    for _ in range(count - 1):
        part = value.astype(BF16)
        parts.append(part)
        value = value - part.astype(F32)
    parts.append(value.astype(BF16))
    return parts


def span_of(b):
    return pl.ds(pl.multiple_of(b * BLOCK, BLOCK), BLOCK)


class Layer:
    def __init__(self, **refs):
        self.__dict__.update(refs)


def prepare_sums(layer):
    heads, length = layer.decay.shape
    blocks = length // BLOCK
    padded = layer.cum.shape[1]
    layer.stage[...] = jnp.zeros_like(layer.stage)
    for p, part in enumerate(split(layer.decay[...] * LOG2E, 3)):
        for b in range(blocks):
            layer.stage[b, p, :heads] = part[:, b * BLOCK : (b + 1) * BLOCK]
    upper = (iota((BLOCK, BLOCK), 0) <= iota((BLOCK, BLOCK), 1)).astype(BF16)
    sums = contract(layer.stage[...].reshape(blocks * 3 * padded, BLOCK), upper, ((1,), (0,)))
    sums = sums.reshape(blocks, 3, padded, BLOCK)
    run = jnp.zeros((padded, 1), F32)
    for b in range(blocks):
        cum = sums[b, 0] + sums[b, 1] + sums[b, 2]
        final = cum[:, BLOCK - 1 :]
        layer.cum[b] = cum
        layer.weights[b, :heads] = (
            jnp.exp2(final[:heads] - cum[:heads]) * layer.step[:, b * BLOCK : (b + 1) * BLOCK]
        )
        layer.fades[b] = jnp.broadcast_to(jnp.exp2(final), (padded, LANES))
        layer.before[b] = jnp.broadcast_to(jnp.exp2(run), (padded, LANES))
        run = run + final
    layer.total[...] = jnp.broadcast_to(run, (padded, LANES))


def prepare_scores(layer):
    blocks = layer.cum.shape[0]
    lower = (iota((BLOCK, BLOCK), 0) >= iota((BLOCK, BLOCK), 1)).astype(F32)

    def block(b, carry):
        across = jnp.transpose(layer.cum[b])
        layer.across[b] = across
        layer.lifting[b] = jnp.exp2(across)
        read = layer.read[:, span_of(b)]
        layer.scores[b] = contract(read, layer.write[:, span_of(b)], ((0,), (0,))) * lower
        read32 = read.astype(F32)
        layer.read_t[b] = jnp.transpose(jnp.concatenate([read32, read32], axis=0)).astype(BF16)
        return carry

    lax.fori_loop(0, blocks, block, 0)


def lanes_of(h):
    return slice(h * LANES, (h + 1) * LANES)


def add_state(layer, b, h, write32, own):
    loaded = (write32 * layer.weights[b, h : h + 1, :]).astype(BF16)
    gained = contract(loaded, own, ((1,), (0,)))
    held = layer.state[h]
    layer.local[b, h] = held
    layer.state[h] = layer.fades[b, h : h + 1, :] * held + gained


def inner_block(layer, b, h, own):
    across = layer.across[b, :, h : h + 1]
    cum = layer.cum[b, h : h + 1, :]
    step = layer.step[h : h + 1, span_of(b)]
    top, low = slice(0, HALF), slice(HALF, BLOCK)

    def mix(rows, cols, diagonal):
        spread = across[rows] - cum[:, cols]
        if diagonal:
            spread = jnp.minimum(spread, 0.0)
        return (jnp.exp2(spread) * layer.scores[b, rows, cols] * step[:, cols]).astype(BF16)

    skip = layer.skip[h]
    first = contract(mix(top, top, True), own[top], ((1,), (0,)))
    lanes = lanes_of(h)
    gate = layer.silu[b, :, lanes]
    layer.silu[b, :, lanes] = gate * layer.lifting[b, :, h : h + 1]
    layer.inner[b, top, lanes] = (first + skip * own[top].astype(F32)) * gate[top]
    both = jnp.concatenate([mix(low, top, False), mix(low, low, True)], axis=1)
    second = contract(both, own, ((1,), (0,)))
    layer.inner[b, low, lanes] = (second + skip * own[low].astype(F32)) * gate[low]


def finish_block(layer, b, hs, store):
    held = jnp.concatenate(
        [layer.before[b, h : h + 1, :] * layer.prior[h] + layer.local[b, h] for h in hs], axis=1
    )
    parts = jnp.concatenate(split(held, 2), axis=0)
    from_state = contract(layer.read_t[b], parts, ((1,), (0,)))
    squares = jnp.zeros((BLOCK, LANES), F32)
    for i, h in enumerate(hs):
        lanes = lanes_of(h)
        gated = layer.silu[b, :, lanes] * from_state[:, i * LANES : (i + 1) * LANES]
        gated += layer.inner[b, :, lanes]
        squares += gated * gated
        store(b, h, gated)
    layer.squares[b] += squares


def silu(gate):
    gate = gate.astype(F32)
    return gate / (1.0 + jnp.exp2(gate * -LOG2E))


def reduce_squares(layer, rows_ref):
    blocks = layer.squares.shape[0]
    rows_ref[...] = jnp.zeros_like(rows_ref)
    for b in range(blocks):
        parts = jnp.concatenate(split(layer.squares[b], 2), axis=1)
        row = contract(jnp.ones((8, 2 * LANES), BF16), parts, ((1,), (1,)))
        rows_ref[b : b + 1, :] = row[:1]


def column_scale(column, grid_rows, grid_cols, scales):
    high = BLOCK // grid_cols
    shape = (BLOCK, scales.shape[0])
    row = iota(shape, 0)
    depth = scales.shape[0] * grid_rows // BLOCK
    source = (row // grid_rows) * depth + (row % grid_rows) // high
    picked = contract((iota(shape, 1) == source).astype(F32), scales, ((1,), (0,)), HIGHEST)
    lane = (iota((BLOCK, BLOCK), 0) % high) * grid_cols + column
    return jnp.sum(jnp.where(iota((BLOCK, BLOCK), 1) == lane, picked, 0.0), axis=1, keepdims=True)


def greet_signal(axes):
    barrier = pltpu.get_barrier_semaphore()
    for axis, count in axes:
        me = lax.axis_index(axis)
        for hop in range(1, count):
            pl.semaphore_signal(
                barrier, inc=1, device_id={axis: lax.rem(me + hop, count)}, device_id_type=MESH
            )


def greet_wait(axes):
    pl.semaphore_wait(
        pltpu.get_barrier_semaphore(), sum(count - 1 for _, count in axes)
    )


def head_sum(count, own_ref, held, sems):
    me = lax.axis_index("head")

    def copy(source, target, hop):
        return pltpu.make_async_remote_copy(
            src_ref=source, dst_ref=target, send_sem=sems.at[0], recv_sem=sems.at[1],
            device_id={"head": lax.rem(me + hop, count)}, device_id_type=MESH,
        )

    for hop in range(1, count):
        copy(own_ref, held.at[hop - 1], hop).start()
    copy(held, held, 1).wait()
    total = own_ref[...]
    for hop in range(1, count):
        total += held[hop - 1]
    return total


class Exchange:
    def __init__(self, seq, layer, refs, sems):
        self.layer = layer
        self.sent, self.swapped, self.passed, self.came, self.near, *refs = refs
        self.own, self.landed, self.pair_total, self.pair_totals, self.span = refs
        self.swap_sems, self.near_sems, self.pass_sems, self.own_sems, self.total_sems = sems
        self.seq, self.me = seq, lax.axis_index("seq")
        self.chunks = self.swap_sems.shape[0] - 1
        me = lax.axis_index("seq")
        self.place = lax.rem(me, 2)
        self.partner = me + 1 - 2 * self.place
        self.group = me // 2
        self.groups = seq // 2
        self.ahead = lax.rem(me + 2, seq)

    def near_copy(self):
        return pltpu.make_async_remote_copy(
            src_ref=self.layer.total, dst_ref=self.near, send_sem=self.near_sems.at[0],
            recv_sem=self.near_sems.at[1], device_id={"seq": self.partner}, device_id_type=MESH,
        )

    def swap_copy(self, c, part):
        return pltpu.make_async_remote_copy(
            src_ref=self.sent.at[part], dst_ref=self.swapped.at[part],
            send_sem=self.swap_sems.at[self.chunks], recv_sem=self.swap_sems.at[c],
            device_id={"seq": self.partner}, device_id_type=MESH,
        )

    def pass_copy(self, c, part):
        return pltpu.make_async_remote_copy(
            src_ref=self.passed.at[part], dst_ref=self.came.at[part],
            send_sem=self.pass_sems.at[self.chunks], recv_sem=self.pass_sems.at[c],
            device_id={"seq": self.ahead}, device_id_type=MESH,
        )

    def swap(self, c, part):
        for h in range(part.start, part.start + part.size):
            self.sent[h] = self.layer.state[h].astype(BF16)
        self.swap_copy(c, part).start()

    def fades(self):
        self.near_copy().wait()
        mine, other = self.layer.total[...], self.near[...]
        even = self.place == 0
        return jnp.exp2(jnp.where(even, mine, other)), jnp.exp2(jnp.where(even, other, mine))

    def step(self, c, part, fades):
        layer = self.layer
        first_fade, last_fade = fades
        even = self.place == 0
        self.swap_copy(c, part).wait_recv()

        @pl.when(self.group > 0)
        def _():
            self.pass_copy(c, part).wait_recv()

        for h in range(part.start, part.start + part.size):
            first, last = self.pair_of(h)
            before = self.came[h].astype(F32)
            middle = first_fade[h : h + 1] * before + first
            self.passed[h] = (last_fade[h : h + 1] * middle + last).astype(BF16)
            layer.prior[h] = jnp.where(even, before, middle)

        @pl.when(self.group < self.groups - 1)
        def _():
            self.pass_copy(c, part).start()

    def own_copy(self, hop):
        return pltpu.make_async_remote_copy(
            src_ref=self.own, dst_ref=self.landed.at[hop - 1], send_sem=self.own_sems.at[0, hop - 1],
            recv_sem=self.own_sems.at[1, hop - 1],
            device_id={"seq": lax.rem(self.me + 2 * hop, self.seq)}, device_id_type=MESH,
        )

    def total_copy(self, hop):
        return pltpu.make_async_remote_copy(
            src_ref=self.pair_total, dst_ref=self.pair_totals.at[hop - 1],
            send_sem=self.total_sems.at[0, hop - 1], recv_sem=self.total_sems.at[1, hop - 1],
            device_id={"seq": lax.rem(self.me + 2 * hop, self.seq)}, device_id_type=MESH,
        )

    def announce(self):
        self.pair_total[...] = self.layer.total[...] + self.near[...]
        for hop in range(1, self.groups):

            @pl.when(self.group + hop < self.groups)
            def _(hop=hop):
                self.total_copy(hop).start()

    def pair_of(self, h):
        mine, other = self.layer.state[h], self.swapped[h].astype(F32)
        even = self.place == 0
        return jnp.where(even, mine, other), jnp.where(even, other, mine)

    def send_own(self, c, part, fades):
        self.swap_copy(c, part).wait_recv()
        for i, h in enumerate(range(part.start, part.start + part.size)):
            first, last = self.pair_of(h)
            self.own[i] = (fades[1][h : h + 1] * first + last).astype(BF16)
        for hop in range(1, self.groups):

            @pl.when(self.group + hop < self.groups)
            def _(hop=hop):
                self.own_copy(hop).start()

    def take_own(self, part, fades):
        prior = self.layer.prior
        heads = range(part.start, part.start + part.size)
        self.span[...] = jnp.zeros_like(self.span)
        for h in heads:
            prior[h] = jnp.zeros(prior.shape[1:], F32)
        for hop in range(1, self.groups):

            @pl.when(self.group >= hop)
            def _(hop=hop):
                self.total_copy(hop).wait_recv()
                self.own_copy(hop).wait_recv()
                factor = jnp.exp2(self.span[...])
                for i, h in enumerate(heads):
                    prior[h] += factor[h : h + 1] * self.landed[hop - 1, i].astype(F32)
                self.span[...] += self.pair_totals[hop - 1]

        for h in heads:
            before = prior[h]
            middle = fades[0][h : h + 1] * before + self.pair_of(h)[0]
            prior[h] = jnp.where(self.place == 0, before, middle)

    def settle(self, start, stop):
        self.swap_copy(0, pl.ds(0, self.sent.shape[0])).wait_send()
        if stop > start:

            @pl.when(self.group < self.groups - 1)
            def _():
                self.pass_copy(0, pl.ds(start, stop - start)).wait_send()

        for hop in range(1, self.groups):

            @pl.when(self.group + hop < self.groups)
            def _(hop=hop):
                self.total_copy(hop).wait_send()
                self.own_copy(hop).wait_send()


def fused_kernel(
    seq, head_count, inner, grid_cols, local_cols, per_col,
    skip1, skip2, x_hbm, gate1_hbm, gate2_hbm, *refs
):
    small_hbm, refs = refs[:SMALL], refs[SMALL:]
    out_hbm, total_ref, x, gate1, gate2, sendbuf, recvbuf, hidden, innerbuf, turned, *refs = refs
    small, refs = refs[:SMALL], refs[SMALL:]
    decay1, step1, write1, read1, gain1, decay2, step2, write2, read2 = small
    (
        gate_raw, flat, woven, silus,
    stage, cum1, cum2, weights, fades1, fades2, before1, before2, total1, total2, across, lifting,
    scores, read_t, state, local, prior, squares, rows1, held1, held2, scale, scales, column,
    *refs,
    ) = refs
    ex1_refs, ex2_refs, refs = refs[:10], refs[10:20], refs[20:]
    (
        load_sems, small_sems, bulk_sems, sum1, sum2, scale_sems, out_sem, *refs,
    ) = refs
    ex1_sems, ex2_sems = refs[:5], refs[5:]
    axes = (("seq", seq), ("head", head_count))
    me = lax.axis_index("seq")
    blocks, _, features = x.shape
    heads = features // LANES
    high = BLOCK // grid_cols
    grid_rows = blocks * high
    slabs = BLOCK // grid_rows
    parts = [pl.ds(c, min(CHUNK, heads - c)) for c in range(0, heads, CHUNK)]
    numbers = [range(part.start, part.start + part.size) for part in parts]
    chunks = len(parts)
    greet_signal(axes)

    def load(b):
        return pltpu.make_async_copy(x_hbm.at[b], x.at[b], load_sems.at[b])

    gate_loads = [
        pltpu.make_async_copy(gate1_hbm, gate1, load_sems.at[blocks]),
        pltpu.make_async_copy(
            gate2_hbm, gate_raw if local_cols > 1 else gate2, load_sems.at[blocks + 1]
        ),
    ]
    small_loads = [
        pltpu.make_async_copy(source, target, small_sems.at[i])
        for i, (source, target) in enumerate(zip(small_hbm, small))
    ]
    for copy in small_loads[:3]:
        copy.start()
    for b in range(blocks):
        load(b).start()
    for copy in small_loads[3:] + gate_loads:
        copy.start()

    shared = dict(
        stage=stage, weights=weights, across=across, lifting=lifting, scores=scores,
        read_t=read_t, state=state, local=local, prior=prior, squares=squares, inner=innerbuf,
        silu=silus,
    )
    one = Layer(
        skip=skip1, write=write1, read=read1, step=step1, decay=decay1, cum=cum1,
        fades=fades1, before=before1, total=total1, **shared,
    )
    two = Layer(
        skip=skip2, write=write2, read=read2, step=step2, decay=decay2, cum=cum2,
        fades=fades2, before=before2, total=total2, **shared,
    )
    ex1 = Exchange(seq, one, ex1_refs, ex1_sems)
    ex2 = Exchange(seq, two, ex2_refs, ex2_sems)

    @pl.when(ex1.group == 0)
    def _():
        ex1.came[...] = jnp.zeros_like(ex1.came)
        ex2.came[...] = jnp.zeros_like(ex2.came)

    for copy in small_loads[:2]:
        copy.wait()
    prepare_sums(one)
    small_loads[2].wait()
    state[...] = jnp.zeros_like(state)

    def states1(b, carry):
        load(b).wait()
        write32 = write1[:, span_of(b)].astype(F32)
        for h in range(heads):
            add_state(one, b, h, write32, x[b, :, lanes_of(h)])
        return carry

    lax.fori_loop(0, blocks, states1, 0)
    def inner1(c):
        def block(b, carry):
            for h in numbers[c]:
                silus[b, :, lanes_of(h)] = silu(gate1[b, :, lanes_of(h)])
                inner_block(one, b, h, x[b, :, lanes_of(h)])
            return carry

        lax.fori_loop(0, blocks, block, 0)

    small_loads[3].wait()
    prepare_scores(one)
    squares[...] = jnp.zeros_like(squares)
    gate_loads[0].wait()
    inner1(0)
    greet_wait(axes)
    ex1.near_copy().start()
    for c, part in enumerate(parts):
        ex1.swap(c, part)
    fades = ex1.fades()
    ex1.announce()
    ex1.send_own(0, parts[0], fades)
    soon = ex1.group < ex1.groups // 2

    @pl.when(ex1.group == 0)
    def _():
        for c in range(1, chunks):
            ex1.step(c, parts[c], fades)

    def store1(b, h, gated):
        slot = turned.at[h % 2]
        slot[...] = gated
        for col in range(grid_cols):
            sendbuf[col // local_cols, col % local_cols, b, :, lanes_of(h)] = slot[
                pl.ds(col, high, stride=grid_cols), :
            ].astype(BF16)

    def finish1(c):
        def block(b, carry):
            finish_block(one, b, numbers[c], store1)
            return carry

        lax.fori_loop(0, blocks, block, 0)

    def wide(c):
        return pl.ds(parts[c].start * LANES, parts[c].size * LANES)

    def bulk(c, hop):
        to = lax.rem(me - hop + seq, seq)
        return pltpu.make_async_remote_copy(
            src_ref=sendbuf.at[to, :, :, :, wide(c)],
            dst_ref=recvbuf.at[me, :, :, :, wide(c)],
            send_sem=bulk_sems.at[0, c],
            recv_sem=bulk_sems.at[1, c],
            device_id={"seq": to},
            device_id_type=MESH,
        )

    def keep(c):
        return pltpu.make_async_copy(
            sendbuf.at[me, :, :, :, wide(c)], recvbuf.at[me, :, :, :, wide(c)], bulk_sems.at[1, c]
        )

    def send_all(c):
        for hop in range(1, seq):
            bulk(c, hop).start()
        keep(c).start()

    ex1.take_own(parts[0], fades)
    finish1(0)
    for hop in range(1, seq):

        @pl.when(hop <= me)
        def _(hop=hop):
            bulk(0, hop).start()


    @pl.when(soon & (ex1.group > 0))
    def _():
        for c in range(1, chunks):
            ex1.step(c, parts[c], fades)

    for hop in range(seq - 1, 0, -1):

        @pl.when(hop > me)
        def _(hop=hop):
            bulk(0, hop).start()

    keep(0).start()
    for c in range(1, chunks):
        inner1(c)

        @pl.when(jnp.logical_not(soon))
        def _(c=c):
            ex1.step(c, parts[c], fades)

        finish1(c)
        if c == 1:
            send_all(c)
    reduce_squares(one, rows1)
    scale[...] = lax.rsqrt(head_sum(head_count, rows1, held1, sum1) / inner + EPSILON)
    depth = scale.shape[0]
    mine = pl.ds(pl.multiple_of(me * depth, depth), depth)

    def scale_copy(source, target, hop):
        return pltpu.make_async_remote_copy(
            src_ref=source, dst_ref=target, send_sem=scale_sems.at[0], recv_sem=scale_sems.at[1],
            device_id={"seq": lax.rem(me - hop + seq, seq)}, device_id_type=MESH,
        )

    for hop in range(1, seq):
        scale_copy(scale, scales.at[mine], hop).start()
    for c in range(2, chunks):
        send_all(c)
    scales[mine, :] = scale[...]

    for copy in small_loads[4:]:
        copy.wait()
    prepare_sums(two)
    prepare_scores(two)
    state[...] = jnp.zeros_like(state)
    squares[...] = jnp.zeros_like(squares)
    ex2.near_copy().start()
    ex2_fades = ex2.fades()
    ex2.announce()
    gate_loads[1].wait()
    all_rows = per_col * BLOCK

    def place_of(b):
        return pl.ds(lax.rem(b, per_col) * (BLOCK * local_cols) + b // per_col, BLOCK, stride=local_cols)

    if local_cols > 1:
        for h in range(heads):
            slot = woven.at[h % CHUNK]
            slot[...] = gate_raw[:, :, lanes_of(h)].astype(F32).reshape(all_rows * local_cols, LANES)
            for b in range(blocks):
                at = (b % per_col) * BLOCK * local_cols + b // per_col
                silus[b, :, lanes_of(h)] = silu(slot[pl.ds(at, BLOCK, stride=local_cols), :])
    else:
        for h in range(heads):
            for b in range(blocks):
                silus[b, :, lanes_of(h)] = silu(gate2[b, :, lanes_of(h)])
    others = scales.at[pl.ds(0, (seq - 1) * depth)]
    scale_copy(others, others, 1).wait()

    def columns(b, carry):
        window = pl.ds(
            pl.multiple_of(lax.rem(b, per_col) * slabs * depth, slabs * depth), slabs * depth
        )
        picked = column_scale(me * local_cols + b // per_col, grid_rows, grid_cols, scales[window, :])
        column[b] = jnp.broadcast_to(picked, (BLOCK, LANES))
        return carry

    lax.fori_loop(0, blocks, columns, 0)

    def bulk_all(c, count):
        some = pl.ds(0, count)
        return pltpu.make_async_remote_copy(
            src_ref=sendbuf.at[some, :, :, :, wide(c)],
            dst_ref=recvbuf.at[some, :, :, :, wide(c)],
            send_sem=bulk_sems.at[0, c],
            recv_sem=bulk_sems.at[1, c],
            device_id={"seq": lax.rem(me + 1, seq)},
            device_id_type=MESH,
        )

    def arrive(c):
        bulk_all(c, seq).wait_recv()

    def states2(c):
        def block(b, carry):
            write32 = write2[:, span_of(b)].astype(F32)
            slab = pl.ds(lax.rem(b, per_col) * slabs, slabs)
            for h in numbers[c]:
                lanes = lanes_of(h)
                own = recvbuf[slab, b // per_col, :, :, lanes].astype(F32).reshape(BLOCK, LANES)
                own = (own * column[b] * gain1[h : h + 1, :]).astype(BF16)
                hidden[b, :, lanes] = own
                add_state(two, b, h, write32, own)
            return carry

        lax.fori_loop(0, blocks, block, 0)

    def inner2(c):
        def block(b, carry):
            for h in numbers[c]:
                inner_block(two, b, h, hidden[b, :, lanes_of(h)])
            return carry

        lax.fori_loop(0, blocks, block, 0)

    def store2(b, h, gated):
        woven[h % CHUNK, place_of(b), :] = gated

    def put(c):
        return pltpu.make_async_copy(flat.at[parts[c]], out_hbm.at[parts[c]], out_sem.at[0])

    def finish2(c):
        def block(b, carry):
            finish_block(two, b, numbers[c], store2)
            return carry

        lax.fori_loop(0, blocks, block, 0, unroll=True)
        for h in numbers[c]:
            flat[h] = woven[h % CHUNK].astype(BF16)
        put(c).start()

    last = chunks - 1
    fades = ex2_fades
    ends = ex2.group == ex2.groups - 1

    def chain(slot):
        for late in range(2):
            c = slot - 1 - late
            if 0 <= c < last:

                @pl.when(soon & (jnp.minimum(ex2.group, 1) == late))
                def _(c=c):
                    ex2.step(c, parts[c], fades)

    for c in range(chunks):
        if c == last:
            chain(last)
            chain(last + 1)
        if c == last - 1:

            @pl.when(soon)
            def _():
                for e in range(last - 3):
                    finish2(e)

        arrive(c)
        states2(c)
        ex2.swap(c, parts[c])
        if c == last:

            @pl.when(jnp.logical_not(soon | ends))
            def _():
                for e in range(last):
                    ex2.step(e, parts[e], fades)

        inner2(c)
        if c < last:
            chain(c)
    ex2.send_own(last, parts[last], fades)
    for e in range(last):

        @pl.when(ends)
        def _(e=e):
            ex2.step(e, parts[e], fades)

        if e < last - 3:

            @pl.when(jnp.logical_not(soon))
            def _(e=e):
                finish2(e)

        else:
            finish2(e)
    ex2.take_own(parts[last], fades)
    finish2(last)
    reduce_squares(two, rows1)
    total_ref[...] = head_sum(head_count, rows1, held2, sum2)
    pltpu.make_async_copy(flat, out_hbm, out_sem.at[0]).wait()
    for c in range(chunks):
        bulk_all(c, seq - 1).wait_send()
    ex1.settle(numbers[0][-1] + 1, heads)
    ex2.settle(0, numbers[last][0])


def norm_kernel(
    steps, inner, per_col, gated_hbm, total_hbm, gain_hbm, out_hbm, gated, total, gain, scale, out,
    load_sems, out_sems,
):
    heads, rows, _ = gated.shape
    part = rows // steps
    tall = out.shape[0] // steps
    local_cols = rows // (per_col * BLOCK)
    small = [
        pltpu.make_async_copy(total_hbm, total, load_sems.at[steps]),
        pltpu.make_async_copy(gain_hbm, gain, load_sems.at[steps + 1]),
    ]
    loads = [
        pltpu.make_async_copy(
            gated_hbm.at[:, pl.ds(i * part, part)], gated.at[:, pl.ds(i * part, part)], load_sems.at[i]
        )
        for i in range(steps)
    ]
    puts = [
        pltpu.make_async_copy(
            out.at[pl.ds(i * tall, tall)], out_hbm.at[pl.ds(i * tall, tall)], out_sems.at[i]
        )
        for i in range(steps)
    ]
    for copy in small + loads:
        copy.start()
    for copy in small:
        copy.wait()
    columns = jnp.transpose(lax.rsqrt(total[...] / inner + EPSILON))
    for b in range(rows // BLOCK):
        at = (b % per_col) * BLOCK * local_cols + b // per_col
        scale[pl.ds(at, BLOCK, stride=local_cols), :] = jnp.broadcast_to(
            columns[:, b : b + 1], (BLOCK, LANES)
        )
    for i in range(steps):
        loads[i].wait()
        span = pl.ds(i * part, part)
        for h in range(heads):
            result = gated[h, span, :].astype(F32) * scale[span, :] * gain[h : h + 1, :]
            shape = (tall,) + out.shape[1:-1] + (LANES,)
            out[pl.ds(i * tall, tall), ..., lanes_of(h)] = result.reshape(shape).astype(BF16)
        puts[i].start()
    for copy in puts:
        copy.wait()


def body(
    seq, head, tokens_in, gate_rows, gate_cols, write_rows, read_rows, step_rows, decay_rows,
    skip_rows, norm_rows, write_cols, read_cols, step_cols, decay_cols, skip_cols, norm_cols,
):
    grid_rows, grid_cols, features = tokens_in.shape
    blocks = grid_rows * grid_cols // BLOCK
    high = BLOCK // grid_cols
    local_cols = grid_cols // seq
    all_rows = grid_rows * seq
    per_col = all_rows // BLOCK
    inner = features * head
    heads, size = step_rows.shape[0], write_rows.shape[0]
    width = features // heads
    depth = round_up(blocks, 8)
    padded = round_up(heads, 16)
    chunks = -(-heads // CHUNK)
    dma = pltpu.SemaphoreType.DMA
    anywhere = pl.BlockSpec(memory_space=pl.ANY)
    whole = pl.BlockSpec(memory_space=pltpu.VMEM)
    smem = pl.BlockSpec(memory_space=pltpu.SMEM)
    vmem = pltpu.VMEM
    tokens = (blocks, BLOCK, features)
    packed = (seq, local_cols, blocks, high, features)
    sums = (blocks, padded, BLOCK)
    rows = (blocks, padded, LANES)
    total = (padded, LANES)
    tall = (blocks, BLOCK, padded)
    states = (heads, size, width)
    groups = seq // 2
    held = (min(CHUNK, heads), size, width)
    far = max(groups - 1, 1)
    exchange = [vmem(states, BF16)] * 4 + [
        vmem(total, F32), vmem(held, BF16), vmem((far,) + held, BF16), vmem(total, F32),
        vmem((far,) + total, F32), vmem(total, F32),
    ]
    exchange_sems = [dma((chunks + 1,)), dma((2,)), dma((chunks + 1,)), dma((2, far)), dma((2, far))]
    small = (
        decay_rows, step_rows, write_rows, read_rows, norm_rows.reshape(heads, width),
        decay_cols, step_cols, write_cols, read_cols,
    )
    raw = (all_rows, local_cols, features)
    flat = raw if local_cols > 1 else (all_rows, features)
    gate = gate_cols if local_cols > 1 else gate_cols.reshape(tokens)
    gated, squares = pl.pallas_call(
        functools.partial(fused_kernel, seq, head, inner, grid_cols, local_cols, per_col),
        out_shape=(
            jax.ShapeDtypeStruct((heads, all_rows * local_cols, LANES), BF16),
            jax.ShapeDtypeStruct((depth, BLOCK), F32),
        ),
        in_specs=[smem, smem] + [anywhere] * (3 + SMALL),
        out_specs=(anywhere, whole),
        scratch_shapes=[
            vmem(tokens, BF16), vmem(tokens, BF16),
            vmem(tokens if local_cols == 1 else (1, BLOCK, LANES), BF16),
            vmem(packed, BF16), vmem(packed, BF16), vmem(tokens, BF16),
            vmem(tokens, F32), vmem((2, BLOCK, LANES), F32),
            *(vmem(array.shape, array.dtype) for array in small),
            vmem(raw if local_cols > 1 else (1, LANES), BF16),
            vmem((heads, all_rows * local_cols, LANES), BF16),
            vmem((CHUNK, all_rows * local_cols, LANES), F32),
            vmem(tokens, F32),
            vmem((blocks, 3, padded, BLOCK), BF16), vmem(sums, F32), vmem(sums, F32),
            vmem(sums, F32), vmem(rows, F32), vmem(rows, F32), vmem(rows, F32), vmem(rows, F32),
            vmem(total, F32), vmem(total, F32), vmem(tall, F32), vmem(tall, F32),
            vmem((blocks, BLOCK, BLOCK), F32), vmem((blocks, BLOCK, 2 * size), BF16),
            vmem(states, F32), vmem((blocks,) + states, F32), vmem(states, F32),
            vmem((blocks, BLOCK, LANES), F32), vmem((depth, BLOCK), F32),
            vmem((head - 1, depth, BLOCK), F32), vmem((head - 1, depth, BLOCK), F32),
            vmem((depth, BLOCK), F32), vmem((seq * depth, BLOCK), F32),
            vmem((blocks, BLOCK, LANES), F32),
            *exchange, *exchange,
            dma((blocks + 2,)), dma((SMALL,)), dma((2, chunks)),
            dma((2,)), dma((2,)), dma((2,)),
            dma((1,)),
            *exchange_sems, *exchange_sems,
        ],
        compiler_params=pltpu.CompilerParams(
            collective_id=0, has_side_effects=True, vmem_limit_bytes=VMEM_BYTES
        ),
        name="fused",
    )(
        skip_rows, skip_cols, tokens_in.reshape(tokens), gate_rows.reshape(tokens), gate, *small
    )
    steps = 8
    result = pl.pallas_call(
        functools.partial(norm_kernel, steps, inner, per_col),
        out_shape=jax.ShapeDtypeStruct(flat, BF16),
        in_specs=[anywhere] * 3,
        out_specs=anywhere,
        scratch_shapes=[
            vmem(gated.shape, BF16), vmem(squares.shape, F32), vmem((heads, width), F32),
            vmem((all_rows * local_cols, LANES), F32), vmem(flat, BF16),
            dma((steps + 2,)), dma((steps,)),
        ],
        compiler_params=pltpu.CompilerParams(vmem_limit_bytes=VMEM_BYTES),
        name="norm",
    )(gated, squares, norm_cols.reshape(heads, width))
    return result.reshape(all_rows, local_cols, features)


def solution(mesh):
    placed = (
        P("seq", None, "head"),
        P("seq", None, "head"),
        P(None, "seq", "head"),
        P(None, "seq"),
        P(None, "seq"),
        P("head", "seq"),
        P("head", "seq"),
        P("head"),
        P("head"),
        P(None, "seq"),
        P(None, "seq"),
        P("head", "seq"),
        P("head", "seq"),
        P("head"),
        P("head"),
    )
    return jax.shard_map(
        functools.partial(body, mesh.shape["seq"], mesh.shape["head"]),
        mesh=mesh, in_specs=placed, out_specs=P(None, "seq", "head"), check_vma=False,
    )
```

```python
import functools
import jax
import jax.numpy as jnp
from jax import lax
from jax.experimental import pallas as pl
from jax.experimental.pallas import tpu as pltpu
from jax.sharding import PartitionSpec as P

BLOCK = 256
HALF = 128
LANES = 128
CHUNK = 2
SMALL = 9
EPSILON = 1e-05
LOG2E = 1.4426950408889634
HIGHEST = lax.Precision.HIGHEST
MESH = pl.DeviceIdType.MESH
F32 = jnp.float32
BF16 = jnp.bfloat16
VMEM_BYTES = 60 * 1024 * 1024


def contract(a, b, dims, precision=None):
    return lax.dot_general(
        a, b, (dims, ((), ())), precision=precision, preferred_element_type=F32
    )


def iota(shape, axis):
    return lax.broadcasted_iota(jnp.int32, shape, axis)


def round_up(value, step):
    return -(-value // step) * step


def split(value, count):
    parts = []
    for _ in range(count - 1):
        part = value.astype(BF16)
        parts.append(part)
        value = value - part.astype(F32)
    parts.append(value.astype(BF16))
    return parts


def span_of(b):
    return pl.ds(pl.multiple_of(b * BLOCK, BLOCK), BLOCK)


class Layer:
    def __init__(self, **refs):
        self.__dict__.update(refs)


def prepare_sums(layer):
    heads, length = layer.decay.shape
    blocks = length // BLOCK
    padded = layer.cum.shape[1]
    layer.stage[...] = jnp.zeros_like(layer.stage)
    for p, part in enumerate(split(layer.decay[...] * LOG2E, 3)):
        for b in range(blocks):
            layer.stage[b, p, :heads] = part[:, b * BLOCK : (b + 1) * BLOCK]
    upper = (iota((BLOCK, BLOCK), 0) <= iota((BLOCK, BLOCK), 1)).astype(BF16)
    sums = contract(layer.stage[...].reshape(blocks * 3 * padded, BLOCK), upper, ((1,), (0,)))
    sums = sums.reshape(blocks, 3, padded, BLOCK)
    run = jnp.zeros((padded, 1), F32)
    for b in range(blocks):
        cum = sums[b, 0] + sums[b, 1] + sums[b, 2]
        final = cum[:, BLOCK - 1 :]
        layer.cum[b] = cum
        layer.weights[b, :heads] = (
            jnp.exp2(final[:heads] - cum[:heads]) * layer.step[:, b * BLOCK : (b + 1) * BLOCK]
        )
        layer.fades[b] = jnp.broadcast_to(jnp.exp2(final), (padded, LANES))
        layer.before[b] = jnp.broadcast_to(jnp.exp2(run), (padded, LANES))
        run = run + final
    layer.total[...] = jnp.broadcast_to(run, (padded, LANES))


def prepare_scores(layer):
    blocks = layer.cum.shape[0]
    lower = (iota((BLOCK, BLOCK), 0) >= iota((BLOCK, BLOCK), 1)).astype(F32)

    def block(b, carry):
        across = jnp.transpose(layer.cum[b])
        layer.across[b] = across
        layer.lifting[b] = jnp.exp2(across)
        read = layer.read[:, span_of(b)]
        layer.scores[b] = contract(read, layer.write[:, span_of(b)], ((0,), (0,))) * lower
        read32 = read.astype(F32)
        layer.read_t[b] = jnp.transpose(jnp.concatenate([read32, read32], axis=0)).astype(BF16)
        return carry

    lax.fori_loop(0, blocks, block, 0)


def lanes_of(h):
    return slice(h * LANES, (h + 1) * LANES)


def add_state(layer, b, h, write32, own):
    loaded = (write32 * layer.weights[b, h : h + 1, :]).astype(BF16)
    gained = contract(loaded, own, ((1,), (0,)))
    held = layer.state[h]
    layer.local[b, h] = held
    layer.state[h] = layer.fades[b, h : h + 1, :] * held + gained


def inner_block(layer, b, h, own):
    across = layer.across[b, :, h : h + 1]
    cum = layer.cum[b, h : h + 1, :]
    step = layer.step[h : h + 1, span_of(b)]
    top, low = slice(0, HALF), slice(HALF, BLOCK)

    def mix(rows, cols, diagonal):
        spread = across[rows] - cum[:, cols]
        if diagonal:
            spread = jnp.minimum(spread, 0.0)
        return (jnp.exp2(spread) * layer.scores[b, rows, cols] * step[:, cols]).astype(BF16)

    skip = layer.skip[h]
    first = contract(mix(top, top, True), own[top], ((1,), (0,)))
    lanes = lanes_of(h)
    gate = layer.silu[b, :, lanes]
    layer.silu[b, :, lanes] = gate * layer.lifting[b, :, h : h + 1]
    layer.inner[b, top, lanes] = (first + skip * own[top].astype(F32)) * gate[top]
    both = jnp.concatenate([mix(low, top, False), mix(low, low, True)], axis=1)
    second = contract(both, own, ((1,), (0,)))
    layer.inner[b, low, lanes] = (second + skip * own[low].astype(F32)) * gate[low]


def finish_block(layer, b, hs, store):
    held = jnp.concatenate(
        [layer.before[b, h : h + 1, :] * layer.prior[h] + layer.local[b, h] for h in hs], axis=1
    )
    parts = jnp.concatenate(split(held, 2), axis=0)
    from_state = contract(layer.read_t[b], parts, ((1,), (0,)))
    squares = jnp.zeros((BLOCK, LANES), F32)
    for i, h in enumerate(hs):
        lanes = lanes_of(h)
        gated = layer.silu[b, :, lanes] * from_state[:, i * LANES : (i + 1) * LANES]
        gated += layer.inner[b, :, lanes]
        squares += gated * gated
        store(b, h, gated)
    layer.squares[b] += squares


def silu(gate):
    gate = gate.astype(F32)
    return gate / (1.0 + jnp.exp2(gate * -LOG2E))


def reduce_squares(layer, rows_ref):
    blocks = layer.squares.shape[0]
    rows_ref[...] = jnp.zeros_like(rows_ref)
    for b in range(blocks):
        parts = jnp.concatenate(split(layer.squares[b], 2), axis=1)
        row = contract(jnp.ones((8, 2 * LANES), BF16), parts, ((1,), (1,)))
        rows_ref[b : b + 1, :] = row[:1]


def column_scale(column, grid_rows, grid_cols, scales):
    high = BLOCK // grid_cols
    shape = (BLOCK, scales.shape[0])
    row = iota(shape, 0)
    depth = scales.shape[0] * grid_rows // BLOCK
    source = (row // grid_rows) * depth + (row % grid_rows) // high
    picked = contract((iota(shape, 1) == source).astype(F32), scales, ((1,), (0,)), HIGHEST)
    lane = (iota((BLOCK, BLOCK), 0) % high) * grid_cols + column
    return jnp.sum(jnp.where(iota((BLOCK, BLOCK), 1) == lane, picked, 0.0), axis=1, keepdims=True)


def greet_signal(axes):
    barrier = pltpu.get_barrier_semaphore()
    for axis, count in axes:
        me = lax.axis_index(axis)
        for hop in range(1, count):
            pl.semaphore_signal(
                barrier, inc=1, device_id={axis: lax.rem(me + hop, count)}, device_id_type=MESH
            )


def greet_wait(axes):
    pl.semaphore_wait(
        pltpu.get_barrier_semaphore(), sum(count - 1 for _, count in axes)
    )


def head_sum(count, own_ref, held, sems):
    me = lax.axis_index("head")

    def copy(source, target, hop):
        return pltpu.make_async_remote_copy(
            src_ref=source, dst_ref=target, send_sem=sems.at[0], recv_sem=sems.at[1],
            device_id={"head": lax.rem(me + hop, count)}, device_id_type=MESH,
        )

    for hop in range(1, count):
        copy(own_ref, held.at[hop - 1], hop).start()
    copy(held, held, 1).wait()
    total = own_ref[...]
    for hop in range(1, count):
        total += held[hop - 1]
    return total


class Exchange:
    def __init__(self, seq, layer, refs, sems):
        self.layer = layer
        self.sent, self.swapped, self.passed, self.came, self.near, *refs = refs
        self.own, self.landed, self.pair_total, self.pair_totals, self.span = refs
        self.swap_sems, self.near_sems, self.pass_sems, self.own_sems, self.total_sems = sems
        self.seq, self.me = seq, lax.axis_index("seq")
        self.chunks = self.swap_sems.shape[0] - 1
        me = lax.axis_index("seq")
        self.place = lax.rem(me, 2)
        self.partner = me + 1 - 2 * self.place
        self.group = me // 2
        self.groups = seq // 2
        self.ahead = lax.rem(me + 2, seq)

    def near_copy(self):
        return pltpu.make_async_remote_copy(
            src_ref=self.layer.total, dst_ref=self.near, send_sem=self.near_sems.at[0],
            recv_sem=self.near_sems.at[1], device_id={"seq": self.partner}, device_id_type=MESH,
        )

    def swap_copy(self, c, part):
        return pltpu.make_async_remote_copy(
            src_ref=self.sent.at[part], dst_ref=self.swapped.at[part],
            send_sem=self.swap_sems.at[self.chunks], recv_sem=self.swap_sems.at[c],
            device_id={"seq": self.partner}, device_id_type=MESH,
        )

    def pass_copy(self, c, part):
        return pltpu.make_async_remote_copy(
            src_ref=self.passed.at[part], dst_ref=self.came.at[part],
            send_sem=self.pass_sems.at[self.chunks], recv_sem=self.pass_sems.at[c],
            device_id={"seq": self.ahead}, device_id_type=MESH,
        )

    def swap(self, c, part):
        for h in range(part.start, part.start + part.size):
            self.sent[h] = self.layer.state[h].astype(BF16)
        self.swap_copy(c, part).start()

    def fades(self):
        self.near_copy().wait()
        mine, other = self.layer.total[...], self.near[...]
        even = self.place == 0
        return jnp.exp2(jnp.where(even, mine, other)), jnp.exp2(jnp.where(even, other, mine))

    def step(self, c, part, fades):
        layer = self.layer
        first_fade, last_fade = fades
        even = self.place == 0
        self.swap_copy(c, part).wait_recv()

        @pl.when(self.group > 0)
        def _():
            self.pass_copy(c, part).wait_recv()

        for h in range(part.start, part.start + part.size):
            first, last = self.pair_of(h)
            before = self.came[h].astype(F32)
            middle = first_fade[h : h + 1] * before + first
            self.passed[h] = (last_fade[h : h + 1] * middle + last).astype(BF16)
            layer.prior[h] = jnp.where(even, before, middle)

        @pl.when(self.group < self.groups - 1)
        def _():
            self.pass_copy(c, part).start()

    def own_copy(self, hop):
        return pltpu.make_async_remote_copy(
            src_ref=self.own, dst_ref=self.landed.at[hop - 1], send_sem=self.own_sems.at[0, hop - 1],
            recv_sem=self.own_sems.at[1, hop - 1],
            device_id={"seq": lax.rem(self.me + 2 * hop, self.seq)}, device_id_type=MESH,
        )

    def total_copy(self, hop):
        return pltpu.make_async_remote_copy(
            src_ref=self.pair_total, dst_ref=self.pair_totals.at[hop - 1],
            send_sem=self.total_sems.at[0, hop - 1], recv_sem=self.total_sems.at[1, hop - 1],
            device_id={"seq": lax.rem(self.me + 2 * hop, self.seq)}, device_id_type=MESH,
        )

    def announce(self):
        self.pair_total[...] = self.layer.total[...] + self.near[...]
        for hop in range(1, self.groups):

            @pl.when(self.group + hop < self.groups)
            def _(hop=hop):
                self.total_copy(hop).start()

    def pair_of(self, h):
        mine, other = self.layer.state[h], self.swapped[h].astype(F32)
        even = self.place == 0
        return jnp.where(even, mine, other), jnp.where(even, other, mine)

    def send_own(self, c, part, fades):
        self.swap_copy(c, part).wait_recv()
        for i, h in enumerate(range(part.start, part.start + part.size)):
            first, last = self.pair_of(h)
            self.own[i] = (fades[1][h : h + 1] * first + last).astype(BF16)
        for hop in range(1, self.groups):

            @pl.when(self.group + hop < self.groups)
            def _(hop=hop):
                self.own_copy(hop).start()

    def take_own(self, part, fades):
        prior = self.layer.prior
        heads = range(part.start, part.start + part.size)
        self.span[...] = jnp.zeros_like(self.span)
        for h in heads:
            prior[h] = jnp.zeros(prior.shape[1:], F32)
        for hop in range(1, self.groups):

            @pl.when(self.group >= hop)
            def _(hop=hop):
                self.total_copy(hop).wait_recv()
                self.own_copy(hop).wait_recv()
                factor = jnp.exp2(self.span[...])
                for i, h in enumerate(heads):
                    prior[h] += factor[h : h + 1] * self.landed[hop - 1, i].astype(F32)
                self.span[...] += self.pair_totals[hop - 1]

        for h in heads:
            before = prior[h]
            middle = fades[0][h : h + 1] * before + self.pair_of(h)[0]
            prior[h] = jnp.where(self.place == 0, before, middle)

    def settle(self, start, stop):
        self.swap_copy(0, pl.ds(0, self.sent.shape[0])).wait_send()
        if stop > start:

            @pl.when(self.group < self.groups - 1)
            def _():
                self.pass_copy(0, pl.ds(start, stop - start)).wait_send()

        for hop in range(1, self.groups):

            @pl.when(self.group + hop < self.groups)
            def _(hop=hop):
                self.total_copy(hop).wait_send()
                self.own_copy(hop).wait_send()


def fused_kernel(
    seq, head_count, inner, grid_cols, local_cols, per_col,
    skip1, skip2, x_hbm, gate1_hbm, gate2_hbm, *refs
):
    small_hbm, refs = refs[:SMALL], refs[SMALL:]
    out_hbm, total_ref, x, gate1, gate2, sendbuf, recvbuf, hidden, innerbuf, turned, *refs = refs
    small, refs = refs[:SMALL], refs[SMALL:]
    decay1, step1, write1, read1, gain1, decay2, step2, write2, read2 = small
    (
        gate_raw, flat, woven, silus,
    stage, cum1, cum2, weights, fades1, fades2, before1, before2, total1, total2, across, lifting,
    scores, read_t, state, local, prior, squares, rows1, held1, held2, scale, scales, column,
    *refs,
    ) = refs
    ex1_refs, ex2_refs, refs = refs[:10], refs[10:20], refs[20:]
    (
        load_sems, small_sems, bulk_sems, sum1, sum2, scale_sems, out_sem, *refs,
    ) = refs
    ex1_sems, ex2_sems = refs[:5], refs[5:]
    axes = (("seq", seq), ("head", head_count))
    me = lax.axis_index("seq")
    blocks, _, features = x.shape
    heads = features // LANES
    high = BLOCK // grid_cols
    grid_rows = blocks * high
    slabs = BLOCK // grid_rows
    parts = [pl.ds(c, min(CHUNK, heads - c)) for c in range(0, heads, CHUNK)]
    numbers = [range(part.start, part.start + part.size) for part in parts]
    chunks = len(parts)
    greet_signal(axes)

    def load(b):
        return pltpu.make_async_copy(x_hbm.at[b], x.at[b], load_sems.at[b])

    gate_loads = [
        pltpu.make_async_copy(gate1_hbm, gate1, load_sems.at[blocks]),
        pltpu.make_async_copy(
            gate2_hbm, gate_raw if local_cols > 1 else gate2, load_sems.at[blocks + 1]
        ),
    ]
    small_loads = [
        pltpu.make_async_copy(source, target, small_sems.at[i])
        for i, (source, target) in enumerate(zip(small_hbm, small))
    ]
    for copy in small_loads[:3]:
        copy.start()
    for b in range(blocks):
        load(b).start()
    for copy in small_loads[3:] + gate_loads:
        copy.start()

    shared = dict(
        stage=stage, weights=weights, across=across, lifting=lifting, scores=scores,
        read_t=read_t, state=state, local=local, prior=prior, squares=squares, inner=innerbuf,
        silu=silus,
    )
    one = Layer(
        skip=skip1, write=write1, read=read1, step=step1, decay=decay1, cum=cum1,
        fades=fades1, before=before1, total=total1, **shared,
    )
    two = Layer(
        skip=skip2, write=write2, read=read2, step=step2, decay=decay2, cum=cum2,
        fades=fades2, before=before2, total=total2, **shared,
    )
    ex1 = Exchange(seq, one, ex1_refs, ex1_sems)
    ex2 = Exchange(seq, two, ex2_refs, ex2_sems)

    @pl.when(ex1.group == 0)
    def _():
        ex1.came[...] = jnp.zeros_like(ex1.came)
        ex2.came[...] = jnp.zeros_like(ex2.came)

    for copy in small_loads[:2]:
        copy.wait()
    prepare_sums(one)
    small_loads[2].wait()
    state[...] = jnp.zeros_like(state)

    def states1(b, carry):
        load(b).wait()
        write32 = write1[:, span_of(b)].astype(F32)
        for h in range(heads):
            add_state(one, b, h, write32, x[b, :, lanes_of(h)])
        return carry

    lax.fori_loop(0, blocks, states1, 0)
    def inner1(c):
        def block(b, carry):
            for h in numbers[c]:
                silus[b, :, lanes_of(h)] = silu(gate1[b, :, lanes_of(h)])
                inner_block(one, b, h, x[b, :, lanes_of(h)])
            return carry

        lax.fori_loop(0, blocks, block, 0)

    small_loads[3].wait()
    prepare_scores(one)
    squares[...] = jnp.zeros_like(squares)
    greet_wait(axes)
    ex1.near_copy().start()
    for c, part in enumerate(parts):
        ex1.swap(c, part)
    gate_loads[0].wait()
    inner1(0)
    fades = ex1.fades()
    ex1.announce()
    ex1.send_own(0, parts[0], fades)
    soon = ex1.group < ex1.groups // 2

    @pl.when(ex1.group == 0)
    def _():
        for c in range(1, chunks):
            ex1.step(c, parts[c], fades)

    def store1(b, h, gated):
        slot = turned.at[h % 2]
        slot[...] = gated
        for col in range(grid_cols):
            sendbuf[col // local_cols, col % local_cols, b, :, lanes_of(h)] = slot[
                pl.ds(col, high, stride=grid_cols), :
            ].astype(BF16)

    def finish1(c):
        def block(b, carry):
            finish_block(one, b, numbers[c], store1)
            return carry

        lax.fori_loop(0, blocks, block, 0)

    def wide(c):
        return pl.ds(parts[c].start * LANES, parts[c].size * LANES)

    def bulk(c, hop):
        to = lax.rem(me - hop + seq, seq)
        return pltpu.make_async_remote_copy(
            src_ref=sendbuf.at[to, :, :, :, wide(c)],
            dst_ref=recvbuf.at[me, :, :, :, wide(c)],
            send_sem=bulk_sems.at[0, c],
            recv_sem=bulk_sems.at[1, c],
            device_id={"seq": to},
            device_id_type=MESH,
        )

    def keep(c):
        return pltpu.make_async_copy(
            sendbuf.at[me, :, :, :, wide(c)], recvbuf.at[me, :, :, :, wide(c)], bulk_sems.at[1, c]
        )

    def send_all(c):
        for hop in range(1, seq):
            bulk(c, hop).start()
        keep(c).start()

    ex1.take_own(parts[0], fades)
    finish1(0)
    for hop in range(1, seq):

        @pl.when(hop <= me)
        def _(hop=hop):
            bulk(0, hop).start()


    @pl.when(soon & (ex1.group > 0))
    def _():
        for c in range(1, chunks):
            ex1.step(c, parts[c], fades)

    for hop in range(seq - 1, 0, -1):

        @pl.when(hop > me)
        def _(hop=hop):
            bulk(0, hop).start()

    keep(0).start()
    for c in range(1, chunks):
        inner1(c)

        @pl.when(jnp.logical_not(soon))
        def _(c=c):
            ex1.step(c, parts[c], fades)

        finish1(c)
        if c == 1:
            send_all(c)
    reduce_squares(one, rows1)
    scale[...] = lax.rsqrt(head_sum(head_count, rows1, held1, sum1) / inner + EPSILON)
    depth = scale.shape[0]
    mine = pl.ds(pl.multiple_of(me * depth, depth), depth)

    def scale_copy(source, target, hop):
        return pltpu.make_async_remote_copy(
            src_ref=source, dst_ref=target, send_sem=scale_sems.at[0], recv_sem=scale_sems.at[1],
            device_id={"seq": lax.rem(me - hop + seq, seq)}, device_id_type=MESH,
        )

    for hop in range(1, seq):
        scale_copy(scale, scales.at[mine], hop).start()
    for c in range(2, chunks):
        send_all(c)
    scales[mine, :] = scale[...]

    for copy in small_loads[4:]:
        copy.wait()
    prepare_sums(two)
    prepare_scores(two)
    state[...] = jnp.zeros_like(state)
    squares[...] = jnp.zeros_like(squares)
    ex2.near_copy().start()
    ex2_fades = ex2.fades()
    ex2.announce()
    gate_loads[1].wait()
    all_rows = per_col * BLOCK

    def place_of(b):
        return pl.ds(lax.rem(b, per_col) * (BLOCK * local_cols) + b // per_col, BLOCK, stride=local_cols)

    if local_cols > 1:
        for h in range(heads):
            slot = woven.at[h % CHUNK]
            slot[...] = gate_raw[:, :, lanes_of(h)].astype(F32).reshape(all_rows * local_cols, LANES)
            for b in range(blocks):
                at = (b % per_col) * BLOCK * local_cols + b // per_col
                silus[b, :, lanes_of(h)] = silu(slot[pl.ds(at, BLOCK, stride=local_cols), :])
    else:
        for h in range(heads):
            for b in range(blocks):
                silus[b, :, lanes_of(h)] = silu(gate2[b, :, lanes_of(h)])
    others = scales.at[pl.ds(0, (seq - 1) * depth)]
    scale_copy(others, others, 1).wait()

    def columns(b, carry):
        window = pl.ds(
            pl.multiple_of(lax.rem(b, per_col) * slabs * depth, slabs * depth), slabs * depth
        )
        picked = column_scale(me * local_cols + b // per_col, grid_rows, grid_cols, scales[window, :])
        column[b] = jnp.broadcast_to(picked, (BLOCK, LANES))
        return carry

    lax.fori_loop(0, blocks, columns, 0)

    def bulk_all(c, count):
        some = pl.ds(0, count)
        return pltpu.make_async_remote_copy(
            src_ref=sendbuf.at[some, :, :, :, wide(c)],
            dst_ref=recvbuf.at[some, :, :, :, wide(c)],
            send_sem=bulk_sems.at[0, c],
            recv_sem=bulk_sems.at[1, c],
            device_id={"seq": lax.rem(me + 1, seq)},
            device_id_type=MESH,
        )

    def arrive(c):
        bulk_all(c, seq).wait_recv()

    def states2(c):
        def block(b, carry):
            write32 = write2[:, span_of(b)].astype(F32)
            slab = pl.ds(lax.rem(b, per_col) * slabs, slabs)
            for h in numbers[c]:
                lanes = lanes_of(h)
                own = recvbuf[slab, b // per_col, :, :, lanes].astype(F32).reshape(BLOCK, LANES)
                own = (own * column[b] * gain1[h : h + 1, :]).astype(BF16)
                hidden[b, :, lanes] = own
                add_state(two, b, h, write32, own)
            return carry

        lax.fori_loop(0, blocks, block, 0)

    def inner2(c):
        def block(b, carry):
            for h in numbers[c]:
                inner_block(two, b, h, hidden[b, :, lanes_of(h)])
            return carry

        lax.fori_loop(0, blocks, block, 0)

    def store2(b, h, gated):
        woven[h % CHUNK, place_of(b), :] = gated

    def put(c):
        return pltpu.make_async_copy(flat.at[parts[c]], out_hbm.at[parts[c]], out_sem.at[0])

    def finish2(c):
        def block(b, carry):
            finish_block(two, b, numbers[c], store2)
            return carry

        lax.fori_loop(0, blocks, block, 0, unroll=True)
        for h in numbers[c]:
            flat[h] = woven[h % CHUNK].astype(BF16)
        put(c).start()

    last = chunks - 1
    fades = ex2_fades
    ends = ex2.group == ex2.groups - 1

    def chain(slot):
        for late in range(2):
            c = slot - 1 - late
            if 0 <= c < last:

                @pl.when(soon & (jnp.minimum(ex2.group, 1) == late))
                def _(c=c):
                    ex2.step(c, parts[c], fades)

    for c in range(chunks):
        if c == last:
            chain(last)
            chain(last + 1)
        if c == last - 1:

            @pl.when(soon)
            def _():
                for e in range(last - 3):
                    finish2(e)

        arrive(c)
        states2(c)
        ex2.swap(c, parts[c])
        if c == last:

            @pl.when(jnp.logical_not(soon | ends))
            def _():
                for e in range(last):
                    ex2.step(e, parts[e], fades)

        inner2(c)
        if c < last:
            chain(c)
    ex2.send_own(last, parts[last], fades)
    for e in range(last):

        @pl.when(ends)
        def _(e=e):
            ex2.step(e, parts[e], fades)

        if e < last - 3:

            @pl.when(jnp.logical_not(soon))
            def _(e=e):
                finish2(e)

        else:
            finish2(e)
    ex2.take_own(parts[last], fades)
    finish2(last)
    reduce_squares(two, rows1)
    total_ref[...] = head_sum(head_count, rows1, held2, sum2)
    pltpu.make_async_copy(flat, out_hbm, out_sem.at[0]).wait()
    for c in range(chunks):
        bulk_all(c, seq - 1).wait_send()
    ex1.settle(numbers[0][-1] + 1, heads)
    ex2.settle(0, numbers[last][0])


def norm_kernel(
    steps, inner, per_col, gated_hbm, total_hbm, gain_hbm, out_hbm, gated, total, gain, scale, out,
    load_sems, out_sems,
):
    heads, rows, _ = gated.shape
    part = rows // steps
    tall = out.shape[0] // steps
    local_cols = rows // (per_col * BLOCK)
    small = [
        pltpu.make_async_copy(total_hbm, total, load_sems.at[steps]),
        pltpu.make_async_copy(gain_hbm, gain, load_sems.at[steps + 1]),
    ]
    loads = [
        pltpu.make_async_copy(
            gated_hbm.at[:, pl.ds(i * part, part)], gated.at[:, pl.ds(i * part, part)], load_sems.at[i]
        )
        for i in range(steps)
    ]
    puts = [
        pltpu.make_async_copy(
            out.at[pl.ds(i * tall, tall)], out_hbm.at[pl.ds(i * tall, tall)], out_sems.at[i]
        )
        for i in range(steps)
    ]
    for copy in small + loads:
        copy.start()
    for copy in small:
        copy.wait()
    columns = jnp.transpose(lax.rsqrt(total[...] / inner + EPSILON))
    for b in range(rows // BLOCK):
        at = (b % per_col) * BLOCK * local_cols + b // per_col
        scale[pl.ds(at, BLOCK, stride=local_cols), :] = jnp.broadcast_to(
            columns[:, b : b + 1], (BLOCK, LANES)
        )
    for i in range(steps):
        loads[i].wait()
        span = pl.ds(i * part, part)
        for h in range(heads):
            result = gated[h, span, :].astype(F32) * scale[span, :] * gain[h : h + 1, :]
            shape = (tall,) + out.shape[1:-1] + (LANES,)
            out[pl.ds(i * tall, tall), ..., lanes_of(h)] = result.reshape(shape).astype(BF16)
        puts[i].start()
    for copy in puts:
        copy.wait()


def body(
    seq, head, tokens_in, gate_rows, gate_cols, write_rows, read_rows, step_rows, decay_rows,
    skip_rows, norm_rows, write_cols, read_cols, step_cols, decay_cols, skip_cols, norm_cols,
):
    grid_rows, grid_cols, features = tokens_in.shape
    blocks = grid_rows * grid_cols // BLOCK
    high = BLOCK // grid_cols
    local_cols = grid_cols // seq
    all_rows = grid_rows * seq
    per_col = all_rows // BLOCK
    inner = features * head
    heads, size = step_rows.shape[0], write_rows.shape[0]
    width = features // heads
    depth = round_up(blocks, 8)
    padded = round_up(heads, 16)
    chunks = -(-heads // CHUNK)
    dma = pltpu.SemaphoreType.DMA
    anywhere = pl.BlockSpec(memory_space=pl.ANY)
    whole = pl.BlockSpec(memory_space=pltpu.VMEM)
    smem = pl.BlockSpec(memory_space=pltpu.SMEM)
    vmem = pltpu.VMEM
    tokens = (blocks, BLOCK, features)
    packed = (seq, local_cols, blocks, high, features)
    sums = (blocks, padded, BLOCK)
    rows = (blocks, padded, LANES)
    total = (padded, LANES)
    tall = (blocks, BLOCK, padded)
    states = (heads, size, width)
    groups = seq // 2
    held = (min(CHUNK, heads), size, width)
    far = max(groups - 1, 1)
    exchange = [vmem(states, BF16)] * 4 + [
        vmem(total, F32), vmem(held, BF16), vmem((far,) + held, BF16), vmem(total, F32),
        vmem((far,) + total, F32), vmem(total, F32),
    ]
    exchange_sems = [dma((chunks + 1,)), dma((2,)), dma((chunks + 1,)), dma((2, far)), dma((2, far))]
    small = (
        decay_rows, step_rows, write_rows, read_rows, norm_rows.reshape(heads, width),
        decay_cols, step_cols, write_cols, read_cols,
    )
    raw = (all_rows, local_cols, features)
    flat = raw if local_cols > 1 else (all_rows, features)
    gate = gate_cols if local_cols > 1 else gate_cols.reshape(tokens)
    gated, squares = pl.pallas_call(
        functools.partial(fused_kernel, seq, head, inner, grid_cols, local_cols, per_col),
        out_shape=(
            jax.ShapeDtypeStruct((heads, all_rows * local_cols, LANES), BF16),
            jax.ShapeDtypeStruct((depth, BLOCK), F32),
        ),
        in_specs=[smem, smem] + [anywhere] * (3 + SMALL),
        out_specs=(anywhere, whole),
        scratch_shapes=[
            vmem(tokens, BF16), vmem(tokens, BF16),
            vmem(tokens if local_cols == 1 else (1, BLOCK, LANES), BF16),
            vmem(packed, BF16), vmem(packed, BF16), vmem(tokens, BF16),
            vmem(tokens, F32), vmem((2, BLOCK, LANES), F32),
            *(vmem(array.shape, array.dtype) for array in small),
            vmem(raw if local_cols > 1 else (1, LANES), BF16),
            vmem((heads, all_rows * local_cols, LANES), BF16),
            vmem((CHUNK, all_rows * local_cols, LANES), F32),
            vmem(tokens, F32),
            vmem((blocks, 3, padded, BLOCK), BF16), vmem(sums, F32), vmem(sums, F32),
            vmem(sums, F32), vmem(rows, F32), vmem(rows, F32), vmem(rows, F32), vmem(rows, F32),
            vmem(total, F32), vmem(total, F32), vmem(tall, F32), vmem(tall, F32),
            vmem((blocks, BLOCK, BLOCK), F32), vmem((blocks, BLOCK, 2 * size), BF16),
            vmem(states, F32), vmem((blocks,) + states, F32), vmem(states, F32),
            vmem((blocks, BLOCK, LANES), F32), vmem((depth, BLOCK), F32),
            vmem((head - 1, depth, BLOCK), F32), vmem((head - 1, depth, BLOCK), F32),
            vmem((depth, BLOCK), F32), vmem((seq * depth, BLOCK), F32),
            vmem((blocks, BLOCK, LANES), F32),
            *exchange, *exchange,
            dma((blocks + 2,)), dma((SMALL,)), dma((2, chunks)),
            dma((2,)), dma((2,)), dma((2,)),
            dma((1,)),
            *exchange_sems, *exchange_sems,
        ],
        compiler_params=pltpu.CompilerParams(
            collective_id=0, has_side_effects=True, vmem_limit_bytes=VMEM_BYTES
        ),
        name="fused",
    )(
        skip_rows, skip_cols, tokens_in.reshape(tokens), gate_rows.reshape(tokens), gate, *small
    )
    steps = 8
    result = pl.pallas_call(
        functools.partial(norm_kernel, steps, inner, per_col),
        out_shape=jax.ShapeDtypeStruct(flat, BF16),
        in_specs=[anywhere] * 3,
        out_specs=anywhere,
        scratch_shapes=[
            vmem(gated.shape, BF16), vmem(squares.shape, F32), vmem((heads, width), F32),
            vmem((all_rows * local_cols, LANES), F32), vmem(flat, BF16),
            dma((steps + 2,)), dma((steps,)),
        ],
        compiler_params=pltpu.CompilerParams(vmem_limit_bytes=VMEM_BYTES),
        name="norm",
    )(gated, squares, norm_cols.reshape(heads, width))
    return result.reshape(all_rows, local_cols, features)


def solution(mesh):
    placed = (
        P("seq", None, "head"),
        P("seq", None, "head"),
        P(None, "seq", "head"),
        P(None, "seq"),
        P(None, "seq"),
        P("head", "seq"),
        P("head", "seq"),
        P("head"),
        P("head"),
        P(None, "seq"),
        P(None, "seq"),
        P("head", "seq"),
        P("head", "seq"),
        P("head"),
        P("head"),
    )
    return jax.shard_map(
        functools.partial(body, mesh.shape["seq"], mesh.shape["head"]),
        mesh=mesh, in_specs=placed, out_specs=P(None, "seq", "head"), check_vma=False,
    )
```

```python
import functools
import jax
import jax.numpy as jnp
from jax import lax
from jax.experimental import pallas as pl
from jax.experimental.pallas import tpu as pltpu
from jax.sharding import PartitionSpec as P

BLOCK = 256
HALF = 128
LANES = 128
CHUNK = 2
SMALL = 9
EPSILON = 1e-05
LOG2E = 1.4426950408889634
HIGHEST = lax.Precision.HIGHEST
MESH = pl.DeviceIdType.MESH
F32 = jnp.float32
BF16 = jnp.bfloat16
VMEM_BYTES = 60 * 1024 * 1024


def contract(a, b, dims, precision=None):
    return lax.dot_general(
        a, b, (dims, ((), ())), precision=precision, preferred_element_type=F32
    )


def iota(shape, axis):
    return lax.broadcasted_iota(jnp.int32, shape, axis)


def round_up(value, step):
    return -(-value // step) * step


def split(value, count):
    parts = []
    for _ in range(count - 1):
        part = value.astype(BF16)
        parts.append(part)
        value = value - part.astype(F32)
    parts.append(value.astype(BF16))
    return parts


def span_of(b):
    return pl.ds(pl.multiple_of(b * BLOCK, BLOCK), BLOCK)


class Layer:
    def __init__(self, **refs):
        self.__dict__.update(refs)


def prepare_sums(layer):
    heads, length = layer.decay.shape
    blocks = length // BLOCK
    padded = layer.cum.shape[1]
    layer.stage[...] = jnp.zeros_like(layer.stage)
    for p, part in enumerate(split(layer.decay[...] * LOG2E, 3)):
        for b in range(blocks):
            layer.stage[b, p, :heads] = part[:, b * BLOCK : (b + 1) * BLOCK]
    upper = (iota((BLOCK, BLOCK), 0) <= iota((BLOCK, BLOCK), 1)).astype(BF16)
    sums = contract(layer.stage[...].reshape(blocks * 3 * padded, BLOCK), upper, ((1,), (0,)))
    sums = sums.reshape(blocks, 3, padded, BLOCK)
    run = jnp.zeros((padded, 1), F32)
    for b in range(blocks):
        cum = sums[b, 0] + sums[b, 1] + sums[b, 2]
        final = cum[:, BLOCK - 1 :]
        layer.cum[b] = cum
        layer.weights[b, :heads] = (
            jnp.exp2(final[:heads] - cum[:heads]) * layer.step[:, b * BLOCK : (b + 1) * BLOCK]
        )
        layer.fades[b] = jnp.broadcast_to(jnp.exp2(final), (padded, LANES))
        layer.before[b] = jnp.broadcast_to(jnp.exp2(run), (padded, LANES))
        run = run + final
    layer.total[...] = jnp.broadcast_to(run, (padded, LANES))


def prepare_scores(layer):
    blocks = layer.cum.shape[0]
    lower = (iota((BLOCK, BLOCK), 0) >= iota((BLOCK, BLOCK), 1)).astype(F32)

    def block(b, carry):
        across = jnp.transpose(layer.cum[b])
        layer.across[b] = across
        layer.lifting[b] = jnp.exp2(across)
        read = layer.read[:, span_of(b)]
        layer.scores[b] = contract(read, layer.write[:, span_of(b)], ((0,), (0,))) * lower
        read32 = read.astype(F32)
        layer.read_t[b] = jnp.transpose(jnp.concatenate([read32, read32], axis=0)).astype(BF16)
        return carry

    lax.fori_loop(0, blocks, block, 0)


def lanes_of(h):
    return slice(h * LANES, (h + 1) * LANES)


def add_state(layer, b, h, write32, own):
    loaded = (write32 * layer.weights[b, h : h + 1, :]).astype(BF16)
    gained = contract(loaded, own, ((1,), (0,)))
    held = layer.state[h]
    layer.local[b, h] = held
    layer.state[h] = layer.fades[b, h : h + 1, :] * held + gained


def inner_block(layer, b, h, own):
    across = layer.across[b, :, h : h + 1]
    cum = layer.cum[b, h : h + 1, :]
    step = layer.step[h : h + 1, span_of(b)]
    top, low = slice(0, HALF), slice(HALF, BLOCK)

    def mix(rows, cols, diagonal):
        spread = across[rows] - cum[:, cols]
        if diagonal:
            spread = jnp.minimum(spread, 0.0)
        return (jnp.exp2(spread) * layer.scores[b, rows, cols] * step[:, cols]).astype(BF16)

    skip = layer.skip[h]
    first = contract(mix(top, top, True), own[top], ((1,), (0,)))
    lanes = lanes_of(h)
    gate = layer.silu[b, :, lanes]
    layer.silu[b, :, lanes] = gate * layer.lifting[b, :, h : h + 1]
    layer.inner[b, top, lanes] = (first + skip * own[top].astype(F32)) * gate[top]
    both = jnp.concatenate([mix(low, top, False), mix(low, low, True)], axis=1)
    second = contract(both, own, ((1,), (0,)))
    layer.inner[b, low, lanes] = (second + skip * own[low].astype(F32)) * gate[low]


def finish_block(layer, b, hs, store):
    held = jnp.concatenate(
        [layer.before[b, h : h + 1, :] * layer.prior[h] + layer.local[b, h] for h in hs], axis=1
    )
    parts = jnp.concatenate(split(held, 2), axis=0)
    from_state = contract(layer.read_t[b], parts, ((1,), (0,)))
    squares = jnp.zeros((BLOCK, LANES), F32)
    for i, h in enumerate(hs):
        lanes = lanes_of(h)
        gated = layer.silu[b, :, lanes] * from_state[:, i * LANES : (i + 1) * LANES]
        gated += layer.inner[b, :, lanes]
        squares += gated * gated
        store(b, h, gated)
    layer.squares[b] += squares


def silu(gate):
    gate = gate.astype(F32)
    return gate / (1.0 + jnp.exp2(gate * -LOG2E))


def reduce_squares(layer, rows_ref):
    blocks = layer.squares.shape[0]
    rows_ref[...] = jnp.zeros_like(rows_ref)
    for b in range(blocks):
        parts = jnp.concatenate(split(layer.squares[b], 2), axis=1)
        row = contract(jnp.ones((8, 2 * LANES), BF16), parts, ((1,), (1,)))
        rows_ref[b : b + 1, :] = row[:1]


def column_scale(column, grid_rows, grid_cols, scales):
    high = BLOCK // grid_cols
    shape = (BLOCK, scales.shape[0])
    row = iota(shape, 0)
    depth = scales.shape[0] * grid_rows // BLOCK
    source = (row // grid_rows) * depth + (row % grid_rows) // high
    picked = contract((iota(shape, 1) == source).astype(F32), scales, ((1,), (0,)), HIGHEST)
    lane = (iota((BLOCK, BLOCK), 0) % high) * grid_cols + column
    return jnp.sum(jnp.where(iota((BLOCK, BLOCK), 1) == lane, picked, 0.0), axis=1, keepdims=True)


def greet_signal(axes):
    barrier = pltpu.get_barrier_semaphore()
    for axis, count in axes:
        me = lax.axis_index(axis)
        for hop in range(1, count):
            pl.semaphore_signal(
                barrier, inc=1, device_id={axis: lax.rem(me + hop, count)}, device_id_type=MESH
            )


def greet_wait(axes):
    pl.semaphore_wait(
        pltpu.get_barrier_semaphore(), sum(count - 1 for _, count in axes)
    )


def head_sum(count, own_ref, held, sems):
    me = lax.axis_index("head")

    def copy(source, target, hop):
        return pltpu.make_async_remote_copy(
            src_ref=source, dst_ref=target, send_sem=sems.at[0], recv_sem=sems.at[1],
            device_id={"head": lax.rem(me + hop, count)}, device_id_type=MESH,
        )

    for hop in range(1, count):
        copy(own_ref, held.at[hop - 1], hop).start()
    copy(held, held, 1).wait()
    total = own_ref[...]
    for hop in range(1, count):
        total += held[hop - 1]
    return total


class Exchange:
    def __init__(self, seq, layer, refs, sems):
        self.layer = layer
        self.sent, self.swapped, self.passed, self.came, self.near, *refs = refs
        self.own, self.landed, self.pair_total, self.pair_totals, self.span = refs
        self.swap_sems, self.near_sems, self.pass_sems, self.own_sems, self.total_sems = sems
        self.seq, self.me = seq, lax.axis_index("seq")
        self.chunks = self.swap_sems.shape[0] - 1
        me = lax.axis_index("seq")
        self.place = lax.rem(me, 2)
        self.partner = me + 1 - 2 * self.place
        self.group = me // 2
        self.groups = seq // 2
        self.ahead = lax.rem(me + 2, seq)

    def near_copy(self):
        return pltpu.make_async_remote_copy(
            src_ref=self.layer.total, dst_ref=self.near, send_sem=self.near_sems.at[0],
            recv_sem=self.near_sems.at[1], device_id={"seq": self.partner}, device_id_type=MESH,
        )

    def swap_copy(self, c, part):
        return pltpu.make_async_remote_copy(
            src_ref=self.sent.at[part], dst_ref=self.swapped.at[part],
            send_sem=self.swap_sems.at[self.chunks], recv_sem=self.swap_sems.at[c],
            device_id={"seq": self.partner}, device_id_type=MESH,
        )

    def pass_copy(self, c, part):
        return pltpu.make_async_remote_copy(
            src_ref=self.passed.at[part], dst_ref=self.came.at[part],
            send_sem=self.pass_sems.at[self.chunks], recv_sem=self.pass_sems.at[c],
            device_id={"seq": self.ahead}, device_id_type=MESH,
        )

    def swap(self, c, part):
        for h in range(part.start, part.start + part.size):
            self.sent[h] = self.layer.state[h].astype(BF16)
        self.swap_copy(c, part).start()

    def fades(self):
        self.near_copy().wait()
        mine, other = self.layer.total[...], self.near[...]
        even = self.place == 0
        return jnp.exp2(jnp.where(even, mine, other)), jnp.exp2(jnp.where(even, other, mine))

    def step(self, c, part, fades):
        layer = self.layer
        first_fade, last_fade = fades
        even = self.place == 0
        self.swap_copy(c, part).wait_recv()

        @pl.when(self.group > 0)
        def _():
            self.pass_copy(c, part).wait_recv()

        for h in range(part.start, part.start + part.size):
            first, last = self.pair_of(h)
            before = self.came[h].astype(F32)
            middle = first_fade[h : h + 1] * before + first
            self.passed[h] = (last_fade[h : h + 1] * middle + last).astype(BF16)
            layer.prior[h] = jnp.where(even, before, middle)

        @pl.when(self.group < self.groups - 1)
        def _():
            self.pass_copy(c, part).start()

    def own_copy(self, hop):
        return pltpu.make_async_remote_copy(
            src_ref=self.own, dst_ref=self.landed.at[hop - 1], send_sem=self.own_sems.at[0, hop - 1],
            recv_sem=self.own_sems.at[1, hop - 1],
            device_id={"seq": lax.rem(self.me + 2 * hop, self.seq)}, device_id_type=MESH,
        )

    def total_copy(self, hop):
        return pltpu.make_async_remote_copy(
            src_ref=self.pair_total, dst_ref=self.pair_totals.at[hop - 1],
            send_sem=self.total_sems.at[0, hop - 1], recv_sem=self.total_sems.at[1, hop - 1],
            device_id={"seq": lax.rem(self.me + 2 * hop, self.seq)}, device_id_type=MESH,
        )

    def announce(self):
        self.pair_total[...] = self.layer.total[...] + self.near[...]
        for hop in range(1, self.groups):

            @pl.when(self.group + hop < self.groups)
            def _(hop=hop):
                self.total_copy(hop).start()

    def pair_of(self, h):
        mine, other = self.layer.state[h], self.swapped[h].astype(F32)
        even = self.place == 0
        return jnp.where(even, mine, other), jnp.where(even, other, mine)

    def send_own(self, c, part, fades):
        self.swap_copy(c, part).wait_recv()
        for i, h in enumerate(range(part.start, part.start + part.size)):
            first, last = self.pair_of(h)
            self.own[i] = (fades[1][h : h + 1] * first + last).astype(BF16)
        for hop in range(1, self.groups):

            @pl.when(self.group + hop < self.groups)
            def _(hop=hop):
                self.own_copy(hop).start()

    def take_own(self, part, fades):
        prior = self.layer.prior
        heads = range(part.start, part.start + part.size)
        self.span[...] = jnp.zeros_like(self.span)
        for h in heads:
            prior[h] = jnp.zeros(prior.shape[1:], F32)
        for hop in range(1, self.groups):

            @pl.when(self.group >= hop)
            def _(hop=hop):
                self.total_copy(hop).wait_recv()
                self.own_copy(hop).wait_recv()
                factor = jnp.exp2(self.span[...])
                for i, h in enumerate(heads):
                    prior[h] += factor[h : h + 1] * self.landed[hop - 1, i].astype(F32)
                self.span[...] += self.pair_totals[hop - 1]

        for h in heads:
            before = prior[h]
            middle = fades[0][h : h + 1] * before + self.pair_of(h)[0]
            prior[h] = jnp.where(self.place == 0, before, middle)

    def settle(self, start, stop):
        self.swap_copy(0, pl.ds(0, self.sent.shape[0])).wait_send()
        if stop > start:

            @pl.when(self.group < self.groups - 1)
            def _():
                self.pass_copy(0, pl.ds(start, stop - start)).wait_send()

        for hop in range(1, self.groups):

            @pl.when(self.group + hop < self.groups)
            def _(hop=hop):
                self.total_copy(hop).wait_send()
                self.own_copy(hop).wait_send()


def fused_kernel(
    seq, head_count, inner, grid_cols, local_cols, per_col,
    skip1, skip2, x_hbm, gate1_hbm, gate2_hbm, *refs
):
    small_hbm, refs = refs[:SMALL], refs[SMALL:]
    out_hbm, total_ref, x, gate1, gate2, sendbuf, recvbuf, hidden, innerbuf, turned, *refs = refs
    small, refs = refs[:SMALL], refs[SMALL:]
    decay1, step1, write1, read1, gain1, decay2, step2, write2, read2 = small
    (
        gate_raw, flat, woven, silus,
    stage, cum1, cum2, weights, fades1, fades2, before1, before2, total1, total2, across, lifting,
    scores, read_t, state, local, prior, squares, rows1, held1, held2, scale, scales, column,
    *refs,
    ) = refs
    ex1_refs, ex2_refs, refs = refs[:10], refs[10:20], refs[20:]
    (
        load_sems, small_sems, bulk_sems, sum1, sum2, scale_sems, out_sem, *refs,
    ) = refs
    ex1_sems, ex2_sems = refs[:5], refs[5:]
    axes = (("seq", seq), ("head", head_count))
    me = lax.axis_index("seq")
    blocks, _, features = x.shape
    heads = features // LANES
    high = BLOCK // grid_cols
    grid_rows = blocks * high
    slabs = BLOCK // grid_rows
    parts = [pl.ds(c, min(CHUNK, heads - c)) for c in range(0, heads, CHUNK)]
    numbers = [range(part.start, part.start + part.size) for part in parts]
    chunks = len(parts)
    greet_signal(axes)

    def load(b):
        return pltpu.make_async_copy(x_hbm.at[b], x.at[b], load_sems.at[b])

    gate_loads = [
        pltpu.make_async_copy(gate1_hbm, gate1, load_sems.at[blocks]),
        pltpu.make_async_copy(
            gate2_hbm, gate_raw if local_cols > 1 else gate2, load_sems.at[blocks + 1]
        ),
    ]
    small_loads = [
        pltpu.make_async_copy(source, target, small_sems.at[i])
        for i, (source, target) in enumerate(zip(small_hbm, small))
    ]
    for copy in small_loads[:3]:
        copy.start()
    for b in range(blocks):
        load(b).start()
    for copy in small_loads[3:] + gate_loads:
        copy.start()

    shared = dict(
        stage=stage, weights=weights, across=across, lifting=lifting, scores=scores,
        read_t=read_t, state=state, local=local, prior=prior, squares=squares, inner=innerbuf,
        silu=silus,
    )
    one = Layer(
        skip=skip1, write=write1, read=read1, step=step1, decay=decay1, cum=cum1,
        fades=fades1, before=before1, total=total1, **shared,
    )
    two = Layer(
        skip=skip2, write=write2, read=read2, step=step2, decay=decay2, cum=cum2,
        fades=fades2, before=before2, total=total2, **shared,
    )
    ex1 = Exchange(seq, one, ex1_refs, ex1_sems)
    ex2 = Exchange(seq, two, ex2_refs, ex2_sems)

    @pl.when(ex1.group == 0)
    def _():
        ex1.came[...] = jnp.zeros_like(ex1.came)
        ex2.came[...] = jnp.zeros_like(ex2.came)

    for copy in small_loads[:2]:
        copy.wait()
    prepare_sums(one)
    small_loads[2].wait()
    state[...] = jnp.zeros_like(state)

    def states1(b, carry):
        load(b).wait()
        write32 = write1[:, span_of(b)].astype(F32)
        for h in range(heads):
            add_state(one, b, h, write32, x[b, :, lanes_of(h)])
        return carry

    lax.fori_loop(0, blocks, states1, 0)
    def inner1(c):
        def block(b, carry):
            for h in numbers[c]:
                silus[b, :, lanes_of(h)] = silu(gate1[b, :, lanes_of(h)])
                inner_block(one, b, h, x[b, :, lanes_of(h)])
            return carry

        lax.fori_loop(0, blocks, block, 0, unroll=2)

    small_loads[3].wait()
    prepare_scores(one)
    squares[...] = jnp.zeros_like(squares)
    greet_wait(axes)
    ex1.near_copy().start()
    for c, part in enumerate(parts):
        ex1.swap(c, part)
    gate_loads[0].wait()
    inner1(0)
    fades = ex1.fades()
    ex1.announce()
    ex1.send_own(0, parts[0], fades)
    soon = ex1.group < ex1.groups // 2

    @pl.when(ex1.group == 0)
    def _():
        for c in range(1, chunks):
            ex1.step(c, parts[c], fades)

    def store1(b, h, gated):
        slot = turned.at[h % 2]
        slot[...] = gated
        for col in range(grid_cols):
            sendbuf[col // local_cols, col % local_cols, b, :, lanes_of(h)] = slot[
                pl.ds(col, high, stride=grid_cols), :
            ].astype(BF16)

    def finish1(c):
        def block(b, carry):
            finish_block(one, b, numbers[c], store1)
            return carry

        lax.fori_loop(0, blocks, block, 0)

    def wide(c):
        return pl.ds(parts[c].start * LANES, parts[c].size * LANES)

    def bulk(c, hop):
        to = lax.rem(me - hop + seq, seq)
        return pltpu.make_async_remote_copy(
            src_ref=sendbuf.at[to, :, :, :, wide(c)],
            dst_ref=recvbuf.at[me, :, :, :, wide(c)],
            send_sem=bulk_sems.at[0, c],
            recv_sem=bulk_sems.at[1, c],
            device_id={"seq": to},
            device_id_type=MESH,
        )

    def keep(c):
        return pltpu.make_async_copy(
            sendbuf.at[me, :, :, :, wide(c)], recvbuf.at[me, :, :, :, wide(c)], bulk_sems.at[1, c]
        )

    def send_all(c):
        for hop in range(1, seq):
            bulk(c, hop).start()
        keep(c).start()

    ex1.take_own(parts[0], fades)
    finish1(0)
    for hop in range(1, seq):

        @pl.when(hop <= me)
        def _(hop=hop):
            bulk(0, hop).start()


    @pl.when(soon & (ex1.group > 0))
    def _():
        for c in range(1, chunks):
            ex1.step(c, parts[c], fades)

    for hop in range(seq - 1, 0, -1):

        @pl.when(hop > me)
        def _(hop=hop):
            bulk(0, hop).start()

    keep(0).start()
    for c in range(1, chunks):
        inner1(c)

        @pl.when(jnp.logical_not(soon))
        def _(c=c):
            ex1.step(c, parts[c], fades)

        finish1(c)
        if c == 1:
            send_all(c)
    reduce_squares(one, rows1)
    scale[...] = lax.rsqrt(head_sum(head_count, rows1, held1, sum1) / inner + EPSILON)
    depth = scale.shape[0]
    mine = pl.ds(pl.multiple_of(me * depth, depth), depth)

    def scale_copy(source, target, hop):
        return pltpu.make_async_remote_copy(
            src_ref=source, dst_ref=target, send_sem=scale_sems.at[0], recv_sem=scale_sems.at[1],
            device_id={"seq": lax.rem(me - hop + seq, seq)}, device_id_type=MESH,
        )

    for hop in range(1, seq):
        scale_copy(scale, scales.at[mine], hop).start()
    for c in range(2, chunks):
        send_all(c)
    scales[mine, :] = scale[...]

    for copy in small_loads[4:]:
        copy.wait()
    prepare_sums(two)
    prepare_scores(two)
    state[...] = jnp.zeros_like(state)
    squares[...] = jnp.zeros_like(squares)
    ex2.near_copy().start()
    ex2_fades = ex2.fades()
    ex2.announce()
    gate_loads[1].wait()
    all_rows = per_col * BLOCK

    def place_of(b):
        return pl.ds(lax.rem(b, per_col) * (BLOCK * local_cols) + b // per_col, BLOCK, stride=local_cols)

    if local_cols > 1:
        for h in range(heads):
            slot = woven.at[h % CHUNK]
            slot[...] = gate_raw[:, :, lanes_of(h)].astype(F32).reshape(all_rows * local_cols, LANES)
            for b in range(blocks):
                at = (b % per_col) * BLOCK * local_cols + b // per_col
                silus[b, :, lanes_of(h)] = silu(slot[pl.ds(at, BLOCK, stride=local_cols), :])
    else:
        for h in range(heads):
            for b in range(blocks):
                silus[b, :, lanes_of(h)] = silu(gate2[b, :, lanes_of(h)])
    others = scales.at[pl.ds(0, (seq - 1) * depth)]
    scale_copy(others, others, 1).wait()

    def columns(b, carry):
        window = pl.ds(
            pl.multiple_of(lax.rem(b, per_col) * slabs * depth, slabs * depth), slabs * depth
        )
        picked = column_scale(me * local_cols + b // per_col, grid_rows, grid_cols, scales[window, :])
        column[b] = jnp.broadcast_to(picked, (BLOCK, LANES))
        return carry

    lax.fori_loop(0, blocks, columns, 0)

    def bulk_all(c, count):
        some = pl.ds(0, count)
        return pltpu.make_async_remote_copy(
            src_ref=sendbuf.at[some, :, :, :, wide(c)],
            dst_ref=recvbuf.at[some, :, :, :, wide(c)],
            send_sem=bulk_sems.at[0, c],
            recv_sem=bulk_sems.at[1, c],
            device_id={"seq": lax.rem(me + 1, seq)},
            device_id_type=MESH,
        )

    def arrive(c):
        bulk_all(c, seq).wait_recv()

    def states2(c):
        def block(b, carry):
            write32 = write2[:, span_of(b)].astype(F32)
            slab = pl.ds(lax.rem(b, per_col) * slabs, slabs)
            for h in numbers[c]:
                lanes = lanes_of(h)
                own = recvbuf[slab, b // per_col, :, :, lanes].astype(F32).reshape(BLOCK, LANES)
                own = (own * column[b] * gain1[h : h + 1, :]).astype(BF16)
                hidden[b, :, lanes] = own
                add_state(two, b, h, write32, own)
            return carry

        lax.fori_loop(0, blocks, block, 0)

    def inner2(c):
        def block(b, carry):
            for h in numbers[c]:
                inner_block(two, b, h, hidden[b, :, lanes_of(h)])
            return carry

        lax.fori_loop(0, blocks, block, 0, unroll=2)

    def store2(b, h, gated):
        woven[h % CHUNK, place_of(b), :] = gated

    def put(c):
        return pltpu.make_async_copy(flat.at[parts[c]], out_hbm.at[parts[c]], out_sem.at[0])

    def finish2(c):
        def block(b, carry):
            finish_block(two, b, numbers[c], store2)
            return carry

        lax.fori_loop(0, blocks, block, 0, unroll=True)
        for h in numbers[c]:
            flat[h] = woven[h % CHUNK].astype(BF16)
        put(c).start()

    last = chunks - 1
    fades = ex2_fades
    ends = ex2.group == ex2.groups - 1

    def chain(slot):
        for late in range(2):
            c = slot - 1 - late
            if 0 <= c < last:

                @pl.when(soon & (jnp.minimum(ex2.group, 1) == late))
                def _(c=c):
                    ex2.step(c, parts[c], fades)

    for c in range(chunks):
        if c == last:
            chain(last)
            chain(last + 1)
        if c == last - 1:

            @pl.when(soon)
            def _():
                for e in range(last - 3):
                    finish2(e)

        arrive(c)
        states2(c)
        ex2.swap(c, parts[c])
        if c == last:

            @pl.when(jnp.logical_not(soon | ends))
            def _():
                for e in range(last):
                    ex2.step(e, parts[e], fades)

        inner2(c)
        if c < last:
            chain(c)
    ex2.send_own(last, parts[last], fades)
    for e in range(last):

        @pl.when(ends)
        def _(e=e):
            ex2.step(e, parts[e], fades)

        if e < last - 3:

            @pl.when(jnp.logical_not(soon))
            def _(e=e):
                finish2(e)

        else:
            finish2(e)
    ex2.take_own(parts[last], fades)
    finish2(last)
    reduce_squares(two, rows1)
    total_ref[...] = head_sum(head_count, rows1, held2, sum2)
    pltpu.make_async_copy(flat, out_hbm, out_sem.at[0]).wait()
    for c in range(chunks):
        bulk_all(c, seq - 1).wait_send()
    ex1.settle(numbers[0][-1] + 1, heads)
    ex2.settle(0, numbers[last][0])


def norm_kernel(
    steps, inner, per_col, gated_hbm, total_hbm, gain_hbm, out_hbm, gated, total, gain, scale, out,
    load_sems, out_sems,
):
    heads, rows, _ = gated.shape
    part = rows // steps
    tall = out.shape[0] // steps
    local_cols = rows // (per_col * BLOCK)
    small = [
        pltpu.make_async_copy(total_hbm, total, load_sems.at[steps]),
        pltpu.make_async_copy(gain_hbm, gain, load_sems.at[steps + 1]),
    ]
    loads = [
        pltpu.make_async_copy(
            gated_hbm.at[:, pl.ds(i * part, part)], gated.at[:, pl.ds(i * part, part)], load_sems.at[i]
        )
        for i in range(steps)
    ]
    puts = [
        pltpu.make_async_copy(
            out.at[pl.ds(i * tall, tall)], out_hbm.at[pl.ds(i * tall, tall)], out_sems.at[i]
        )
        for i in range(steps)
    ]
    for copy in small + loads:
        copy.start()
    for copy in small:
        copy.wait()
    columns = jnp.transpose(lax.rsqrt(total[...] / inner + EPSILON))
    for b in range(rows // BLOCK):
        at = (b % per_col) * BLOCK * local_cols + b // per_col
        scale[pl.ds(at, BLOCK, stride=local_cols), :] = jnp.broadcast_to(
            columns[:, b : b + 1], (BLOCK, LANES)
        )
    for i in range(steps):
        loads[i].wait()
        span = pl.ds(i * part, part)
        for h in range(heads):
            result = gated[h, span, :].astype(F32) * scale[span, :] * gain[h : h + 1, :]
            shape = (tall,) + out.shape[1:-1] + (LANES,)
            out[pl.ds(i * tall, tall), ..., lanes_of(h)] = result.reshape(shape).astype(BF16)
        puts[i].start()
    for copy in puts:
        copy.wait()


def body(
    seq, head, tokens_in, gate_rows, gate_cols, write_rows, read_rows, step_rows, decay_rows,
    skip_rows, norm_rows, write_cols, read_cols, step_cols, decay_cols, skip_cols, norm_cols,
):
    grid_rows, grid_cols, features = tokens_in.shape
    blocks = grid_rows * grid_cols // BLOCK
    high = BLOCK // grid_cols
    local_cols = grid_cols // seq
    all_rows = grid_rows * seq
    per_col = all_rows // BLOCK
    inner = features * head
    heads, size = step_rows.shape[0], write_rows.shape[0]
    width = features // heads
    depth = round_up(blocks, 8)
    padded = round_up(heads, 16)
    chunks = -(-heads // CHUNK)
    dma = pltpu.SemaphoreType.DMA
    anywhere = pl.BlockSpec(memory_space=pl.ANY)
    whole = pl.BlockSpec(memory_space=pltpu.VMEM)
    smem = pl.BlockSpec(memory_space=pltpu.SMEM)
    vmem = pltpu.VMEM
    tokens = (blocks, BLOCK, features)
    packed = (seq, local_cols, blocks, high, features)
    sums = (blocks, padded, BLOCK)
    rows = (blocks, padded, LANES)
    total = (padded, LANES)
    tall = (blocks, BLOCK, padded)
    states = (heads, size, width)
    groups = seq // 2
    held = (min(CHUNK, heads), size, width)
    far = max(groups - 1, 1)
    exchange = [vmem(states, BF16)] * 4 + [
        vmem(total, F32), vmem(held, BF16), vmem((far,) + held, BF16), vmem(total, F32),
        vmem((far,) + total, F32), vmem(total, F32),
    ]
    exchange_sems = [dma((chunks + 1,)), dma((2,)), dma((chunks + 1,)), dma((2, far)), dma((2, far))]
    small = (
        decay_rows, step_rows, write_rows, read_rows, norm_rows.reshape(heads, width),
        decay_cols, step_cols, write_cols, read_cols,
    )
    raw = (all_rows, local_cols, features)
    flat = raw if local_cols > 1 else (all_rows, features)
    gate = gate_cols if local_cols > 1 else gate_cols.reshape(tokens)
    gated, squares = pl.pallas_call(
        functools.partial(fused_kernel, seq, head, inner, grid_cols, local_cols, per_col),
        out_shape=(
            jax.ShapeDtypeStruct((heads, all_rows * local_cols, LANES), BF16),
            jax.ShapeDtypeStruct((depth, BLOCK), F32),
        ),
        in_specs=[smem, smem] + [anywhere] * (3 + SMALL),
        out_specs=(anywhere, whole),
        scratch_shapes=[
            vmem(tokens, BF16), vmem(tokens, BF16),
            vmem(tokens if local_cols == 1 else (1, BLOCK, LANES), BF16),
            vmem(packed, BF16), vmem(packed, BF16), vmem(tokens, BF16),
            vmem(tokens, F32), vmem((2, BLOCK, LANES), F32),
            *(vmem(array.shape, array.dtype) for array in small),
            vmem(raw if local_cols > 1 else (1, LANES), BF16),
            vmem((heads, all_rows * local_cols, LANES), BF16),
            vmem((CHUNK, all_rows * local_cols, LANES), F32),
            vmem(tokens, F32),
            vmem((blocks, 3, padded, BLOCK), BF16), vmem(sums, F32), vmem(sums, F32),
            vmem(sums, F32), vmem(rows, F32), vmem(rows, F32), vmem(rows, F32), vmem(rows, F32),
            vmem(total, F32), vmem(total, F32), vmem(tall, F32), vmem(tall, F32),
            vmem((blocks, BLOCK, BLOCK), F32), vmem((blocks, BLOCK, 2 * size), BF16),
            vmem(states, F32), vmem((blocks,) + states, F32), vmem(states, F32),
            vmem((blocks, BLOCK, LANES), F32), vmem((depth, BLOCK), F32),
            vmem((head - 1, depth, BLOCK), F32), vmem((head - 1, depth, BLOCK), F32),
            vmem((depth, BLOCK), F32), vmem((seq * depth, BLOCK), F32),
            vmem((blocks, BLOCK, LANES), F32),
            *exchange, *exchange,
            dma((blocks + 2,)), dma((SMALL,)), dma((2, chunks)),
            dma((2,)), dma((2,)), dma((2,)),
            dma((1,)),
            *exchange_sems, *exchange_sems,
        ],
        compiler_params=pltpu.CompilerParams(
            collective_id=0, has_side_effects=True, vmem_limit_bytes=VMEM_BYTES
        ),
        name="fused",
    )(
        skip_rows, skip_cols, tokens_in.reshape(tokens), gate_rows.reshape(tokens), gate, *small
    )
    steps = 8
    result = pl.pallas_call(
        functools.partial(norm_kernel, steps, inner, per_col),
        out_shape=jax.ShapeDtypeStruct(flat, BF16),
        in_specs=[anywhere] * 3,
        out_specs=anywhere,
        scratch_shapes=[
            vmem(gated.shape, BF16), vmem(squares.shape, F32), vmem((heads, width), F32),
            vmem((all_rows * local_cols, LANES), F32), vmem(flat, BF16),
            dma((steps + 2,)), dma((steps,)),
        ],
        compiler_params=pltpu.CompilerParams(vmem_limit_bytes=VMEM_BYTES),
        name="norm",
    )(gated, squares, norm_cols.reshape(heads, width))
    return result.reshape(all_rows, local_cols, features)


def solution(mesh):
    placed = (
        P("seq", None, "head"),
        P("seq", None, "head"),
        P(None, "seq", "head"),
        P(None, "seq"),
        P(None, "seq"),
        P("head", "seq"),
        P("head", "seq"),
        P("head"),
        P("head"),
        P(None, "seq"),
        P(None, "seq"),
        P("head", "seq"),
        P("head", "seq"),
        P("head"),
        P("head"),
    )
    return jax.shard_map(
        functools.partial(body, mesh.shape["seq"], mesh.shape["head"]),
        mesh=mesh, in_specs=placed, out_specs=P(None, "seq", "head"), check_vma=False,
    )
```
